512 devices in a mesh: wide: 64 (over y_lo, z, core), narrow: 8 (over y_hi, x).
Axes of the slice: x: 4, y: 4 (y_hi: 2, y_lo: 2; y = y_hi * 2 + y_lo), z: 16, core: 2. Of those that a mesh axis runs over, the one named last changes fastest.
Arguments:
- tokens: bfloat16 [8192, 2048], P('wide', 'narrow'), may hold values from -6 to 6
- expert_ids: int32 [8192, 6], P('wide'), may hold values from 0 to 63, all different within a row; in each aligned block of 128 rows (0 to 127, 128 to 255, ...) at most 14 rows name the same one
- route_weights: bfloat16 [8192, 6], P('wide'), may hold values from 0.049804688 to 0.5
- w_gate: bfloat16 [64, 1408, 2048], P('wide', 'narrow'), may hold values from -0.125 to 0.125
- w_up: bfloat16 [64, 1408, 2048], P('wide', 'narrow'), may hold values from -0.125 to 0.125
- w_down: bfloat16 [64, 1408, 2048], P('wide', 'narrow'), may hold values from -0.15625 to 0.15625
Outputs:
- mixed: bfloat16 [8192, 2048], P('wide', 'narrow')
The draws below stay inside these ranges and needn't reach their ends.
Inputs may be any that keep to these rules, and one draw needn't show every extreme that they name: `expert_ids`: within a row the 6 experts differ. Among the 128 tokens of one aligned block, no expert is named more than 14 times, a bound that some block reaches.
All inputs are finite; a program needn't handle non-finite values.
Results may differ from the reference program's by a relative error of at most 0.017.
Values may be sent and summed in bfloat16 or wider, within the bound.
A program may use at most 64 MiB of HBM per device.

```python
import math
import jax
import jax.numpy as jnp
import numpy as np
from jax import lax

D = 2048
FF = 1408
TOP = 6
TOK_DEV = 128
TOKENS = 8192
EXPERTS = 64
CAP = 14
N_NARROW = 8


def block_scale(stream_key, shape, pieces, smallest, top_value):
    level, own = 1.0, jax.random.fold_in(stream_key, 6)
    for dim, parts in pieces:
        heights = jnp.exp(jax.random.uniform(jax.random.fold_in(own, dim), (parts,), jnp.float32, smallest / len(pieces), top_value / len(pieces)))
        level = level * jnp.repeat(heights, shape[dim] // parts).reshape([-1 if axis == dim else 1 for axis in range(len(shape))])
    return level


def assign_block(own_key, own, number, rows, count, top, most, skew):
    ranking = jax.random.permutation(own_key, count)
    crowded, common = load_shares(count, rows * top, most, skew, True), load_shares(count, rows * top, most, skew, False)
    places = jnp.arange(count)

    def named(tallies, offset_by):
        used = int((tallies > 0).sum())
        fixed = max(1, used // 4)
        moved = fixed + (places - fixed + offset_by * (used - fixed)) % max(1, count - fixed)
        return jnp.zeros((count,), jnp.int32).at[ranking[jnp.where(places < fixed, places, moved)]].set(jnp.asarray(tallies, jnp.int32))

    tallies = jnp.where(number % 4 == 0, named(crowded, number // 4), named(common, number - number // 4 - 1))
    mixed = jax.random.permutation(jax.random.fold_in(own, 3), count)
    source_of, sink = mixed[0:count // 2 * 2:2], mixed[1:count // 2 * 2:2]
    margin = jnp.minimum(tallies[source_of] - 1, most - tallies[sink]) // 2
    margin = jnp.where((source_of == ranking[0]) | (sink == ranking[0]) | (tallies[sink] == 0), 0, jnp.maximum(margin, 0))
    moved = jax.random.randint(jax.random.fold_in(own, 4), (count // 2,), 0, 1 << 20) % (margin + 1)
    tallies = tallies.at[source_of].add(-moved).at[sink].add(moved)
    labels = jnp.searchsorted(jnp.cumsum(tallies), jnp.arange(rows * top), side="right").astype(jnp.int32)
    grid = labels.reshape(top, rows).T
    grid = grid[jax.random.permutation(jax.random.fold_in(own, 1), rows)]
    offset_by = jax.random.randint(jax.random.fold_in(own, 2), (rows, 1), 0, top)
    return jnp.take_along_axis(grid, (jnp.arange(top)[None, :] + offset_by) % top, axis=1)


def load_shares(count, total, most, lean, full):
    portions = [(1 << 20) // math.isqrt(rank ** lean) + 1 for rank in range(1, count + 1)]
    largest = most if full else min(most, max(-(-total // count), total * portions[0] // sum(portions)))
    least = 1 if total - largest >= count - 1 else 0
    counts, surplus = [largest] + [least] * (count - 1), total - largest - least * (count - 1)
    while surplus > 0:
        movable = [i for i in range(1, count) if counts[i] < largest] or [i for i in range(1, count) if counts[i] < most]
        mass, left = sum([portions[i] for i in movable]), surplus
        for i in movable:
            extra = min(most - counts[i], max(1, left * portions[i] // mass), surplus)
            counts[i] = counts[i] + extra
            surplus = surplus - extra
    return np.array(counts)


def noise(key, shape, deviation, limit, pieces=(), kind=jnp.bfloat16):
    array = deviation * jax.random.normal(key, shape, jnp.float32)
    if pieces:
        array = array * block_scale(key, shape, pieces, -0.22, 0.18)
    return jnp.clip(array, -limit, limit).astype(kind)


def setup_inputs(seed: int = 0) -> dict:
    seeds = jax.random.split(jax.random.key(seed), 7)
    tokens = noise(seeds[0], (TOKENS, D), 1.0, 6.0, ((0, 64), (1, 8)))
    expert_ids_keys = jax.random.split(jax.random.fold_in(seeds[1], 1), TOKENS // TOK_DEV)
    expert_ids_turns = jax.random.permutation(jax.random.fold_in(seeds[1], 3), TOKENS // TOK_DEV)
    expert_ids = jax.vmap(lambda own, number: assign_block(jax.random.fold_in(seeds[1], 2), own, number, TOK_DEV, EXPERTS, TOP, CAP, 2))(expert_ids_keys, expert_ids_turns).reshape((TOKENS, TOP))
    route_weights = jnp.clip(0.049804688 + 0.4501953 * jax.random.uniform(seeds[2], (TOKENS, TOP), jnp.float32) ** block_scale(seeds[2], (TOKENS, TOP), ((0, 64),), -0.2, 0.2), 0.049804688, 0.5).astype(jnp.bfloat16)
    w_gate = noise(seeds[3], (EXPERTS, FF, D), D ** -0.5, 0.125, ((0, 64), (1, 8)))
    w_up = noise(seeds[4], (EXPERTS, FF, D), D ** -0.5, 0.125, ((0, 64), (1, 8)))
    w_down = noise(seeds[5], (EXPERTS, FF, D), FF ** -0.5, 0.15625, ((0, 64), (1, 8)))
    return dict(tokens=tokens, expert_ids=expert_ids, route_weights=route_weights, w_gate=w_gate, w_up=w_up, w_down=w_down)


def reference(tokens, expert_ids, route_weights, w_gate, w_up, w_down):
    blocks = TOKENS // TOK_DEV
    pairs = TOK_DEV * TOP
    block_ids = expert_ids.reshape(blocks, pairs)
    onehot = (block_ids[:, :, None] == jnp.arange(EXPERTS, dtype=jnp.int32)[None, None, :]).astype(jnp.int32)
    running = jnp.cumsum(onehot, axis=1)
    slot_index = jnp.sum(running * onehot, axis=2) - 1
    block_num = jnp.arange(blocks, dtype=jnp.int32)[:, None]
    row_index = (block_num * CAP + slot_index).reshape(-1).astype(jnp.int32)
    token_index = (block_num * TOK_DEV + jnp.arange(pairs, dtype=jnp.int32)[None, :] // TOP).reshape(-1).astype(jnp.int32)
    flat_ids = block_ids.reshape(-1).astype(jnp.int32)
    row_token = jnp.full((EXPERTS, blocks * CAP), TOKENS, dtype=jnp.int32)
    row_token = row_token.at[flat_ids, row_index].set(token_index)
    row_weight = jnp.zeros((EXPERTS, blocks * CAP), dtype=jnp.float32)
    row_weight = row_weight.at[flat_ids, row_index].set(route_weights.reshape(-1).astype(jnp.float32))
    padded = jnp.concatenate([tokens, jnp.zeros((1, D), dtype=tokens.dtype)], axis=0)
    group_ff = FF // N_NARROW

    def one_expert(total, inputs):
        gate_e, up_e, down_e, tok_e, weight_e = inputs
        slot_rows = padded[tok_e]
        gate_proj = jnp.dot(slot_rows, gate_e.T, preferred_element_type=jnp.float32)
        up_proj = jnp.dot(slot_rows, up_e.T, preferred_element_type=jnp.float32)
        hidden = (jax.nn.silu(gate_proj) * up_proj).astype(jnp.bfloat16)
        hidden = lax.optimization_barrier(hidden)
        partial_value = jnp.einsum("rgf,gfd->rgd", hidden.reshape(-1, N_NARROW, group_ff).astype(jnp.float32),
                             down_e.reshape(N_NARROW, group_ff, D).astype(jnp.float32)).astype(jnp.bfloat16)
        partial_value = lax.optimization_barrier(partial_value)
        expert_out = jnp.sum(partial_value.astype(jnp.float32), axis=1)
        total = total.at[tok_e].add(weight_e[:, None] * expert_out)
        return total, None

    start = jnp.zeros((TOKENS + 1, D), dtype=jnp.float32)
    total, unused = lax.scan(one_expert, start, (w_gate, w_up, w_down, row_token, row_weight))
    return total[:TOKENS].astype(jnp.bfloat16)
```

```python
import jax
import jax.numpy as jnp
from jax import lax
from jax.sharding import PartitionSpec as P


def local(tokens, expert_ids, route_weights, w_gate, w_up, w_down):
    tok_rows = expert_ids.shape[0]
    top_count = expert_ids.shape[1]
    local_experts = w_gate.shape[0]
    groups_wide = lax.axis_size("wide")
    experts_all = local_experts * groups_wide
    capacity = 7 * tok_rows * top_count // (6 * experts_all)
    slots_all = experts_all * capacity
    flat_ids = expert_ids.reshape(-1)
    onehot = (flat_ids[:, None] == jnp.arange(experts_all, dtype=jnp.int32)[None, :]).astype(
        jnp.int32
    )
    running = jnp.cumsum(onehot, axis=0)
    slot_index = jnp.sum(running * onehot, axis=1) - 1
    destination = (flat_ids * capacity + slot_index).reshape(tok_rows, top_count)
    hit = destination[:, :, None] == jnp.arange(slots_all, dtype=jnp.int32)[None, None, :]
    dispatch = jnp.any(hit, axis=1).astype(jnp.bfloat16)
    combine = jnp.sum(
        jnp.where(hit, route_weights.astype(jnp.float32)[:, :, None], 0.0), axis=1
    ).astype(jnp.bfloat16)
    outgoing = jnp.einsum("ts,td->sd", dispatch, tokens, preferred_element_type=jnp.float32).astype(
        jnp.bfloat16
    )
    received = lax.all_to_all(outgoing, "wide", split_axis=0, concat_axis=0, tiled=True)
    slot_rows = lax.all_gather(received, "narrow", axis=1, tiled=True)
    gate_proj = jnp.einsum("sd,fd->sf", slot_rows, w_gate[0], preferred_element_type=jnp.float32)
    up_proj = jnp.einsum("sd,fd->sf", slot_rows, w_up[0], preferred_element_type=jnp.float32)
    hidden = (jax.nn.silu(gate_proj) * up_proj).astype(jnp.bfloat16)
    partial_value = jnp.einsum(
        "sf,fd->sd", hidden, w_down[0], preferred_element_type=jnp.float32
    ).astype(jnp.bfloat16)
    summed = lax.psum_scatter(partial_value, "narrow", scatter_dimension=1, tiled=True)
    returned = lax.all_to_all(summed, "wide", split_axis=0, concat_axis=0, tiled=True)
    mixed = jnp.einsum("ts,sd->td", combine, returned, preferred_element_type=jnp.float32)
    return mixed.astype(jnp.bfloat16)


def solution(mesh):
    in_specs = (
        P("wide", "narrow"),
        P("wide", None),
        P("wide", None),
        P("wide", "narrow", None),
        P("wide", "narrow", None),
        P("wide", "narrow", None),
    )
    out_specs = P("wide", "narrow")
    return jax.shard_map(local, mesh=mesh, in_specs=in_specs, out_specs=out_specs, check_vma=False)
```

```python
import jax
import jax.numpy as jnp
from jax import lax
from jax.experimental import pallas as pl
from jax.experimental.pallas import tpu as pltpu
from jax.sharding import PartitionSpec as P

MESH = pl.DeviceIdType.MESH


def _exchange_kernel(n_peers, pick_src, x_ref, y_ref, send_sem, recv_sem, own_sem):
    me = lax.axis_index("narrow")
    w = lax.axis_index("wide")
    barrier = pltpu.get_barrier_semaphore()
    for k in range(1, n_peers):
        peer = lax.rem(me + k, n_peers)
        pl.semaphore_signal(barrier, inc=1, device_id=(w, peer), device_id_type=MESH)
    pl.semaphore_wait(barrier, n_peers - 1)
    own = pltpu.make_async_copy(pick_src(x_ref, me), y_ref.at[me], own_sem)
    own.start()
    copies = []
    for k in range(1, n_peers):
        peer = lax.rem(me + k, n_peers)
        c = pltpu.make_async_remote_copy(
            src_ref=pick_src(x_ref, peer),
            dst_ref=y_ref.at[me],
            send_sem=send_sem.at[k - 1],
            recv_sem=recv_sem.at[k - 1],
            device_id=(w, peer),
            device_id_type=MESH,
        )
        c.start()
        copies.append(c)
    for k in range(1, n_peers):
        src = lax.rem(me + n_peers - k, n_peers)
        pltpu.make_async_remote_copy(
            src_ref=pick_src(x_ref, src),
            dst_ref=y_ref.at[src],
            send_sem=send_sem.at[k - 1],
            recv_sem=recv_sem.at[k - 1],
            device_id=(w, src),
            device_id_type=MESH,
        ).wait_recv()
    for c in copies:
        c.wait_send()
    own.wait()


def _exchange(x, n_peers, gather, collective_id):
    if gather:
        out_shape = (n_peers,) + x.shape
        pick_src = lambda ref, i: ref
    else:
        out_shape = x.shape
        pick_src = lambda ref, i: ref.at[i]
    nbytes = x.size * x.dtype.itemsize
    return pl.pallas_call(
        lambda *refs: _exchange_kernel(n_peers, pick_src, *refs),
        out_shape=jax.ShapeDtypeStruct(out_shape, x.dtype),
        in_specs=[pl.BlockSpec(memory_space=pl.ANY)],
        out_specs=pl.BlockSpec(memory_space=pl.ANY),
        scratch_shapes=[
            pltpu.SemaphoreType.DMA((n_peers - 1,)),
            pltpu.SemaphoreType.DMA((n_peers - 1,)),
            pltpu.SemaphoreType.DMA(()),
        ],
        compiler_params=pltpu.CompilerParams(collective_id=collective_id, has_side_effects=True),
        cost_estimate=pl.CostEstimate(flops=0, bytes_accessed=2 * nbytes, transcendentals=0),
    )(x)


def local(tokens, expert_ids, route_weights, w_gate, w_up, w_down):
    tok_rows = expert_ids.shape[0]
    top_count = expert_ids.shape[1]
    local_experts = w_gate.shape[0]
    groups_wide = lax.axis_size("wide")
    experts_all = local_experts * groups_wide
    capacity = 7 * tok_rows * top_count // (6 * experts_all)
    slots_all = experts_all * capacity
    flat_ids = expert_ids.reshape(-1)
    onehot = (flat_ids[:, None] == jnp.arange(experts_all, dtype=jnp.int32)[None, :]).astype(
        jnp.int32
    )
    running = jnp.cumsum(onehot, axis=0)
    slot_index = jnp.sum(running * onehot, axis=1) - 1
    destination = (flat_ids * capacity + slot_index).reshape(tok_rows, top_count)
    hit = destination[:, :, None] == jnp.arange(slots_all, dtype=jnp.int32)[None, None, :]
    dispatch = jnp.any(hit, axis=1).astype(jnp.bfloat16)
    combine = jnp.sum(
        jnp.where(hit, route_weights.astype(jnp.float32)[:, :, None], 0.0), axis=1
    ).astype(jnp.bfloat16)
    outgoing = jnp.einsum("ts,td->sd", dispatch, tokens, preferred_element_type=jnp.float32).astype(
        jnp.bfloat16
    )
    received = lax.all_to_all(outgoing, "wide", split_axis=0, concat_axis=0, tiled=True)
    n_narrow = lax.axis_size("narrow")
    width = tokens.shape[1]
    slot_rows = _exchange(received, n_narrow, True, 0)
    wg = w_gate[0].reshape(-1, n_narrow, width)
    wu = w_up[0].reshape(-1, n_narrow, width)
    wd = w_down[0].reshape(-1, n_narrow, width)
    gate_proj = jnp.einsum("nsd,fnd->sf", slot_rows, wg, preferred_element_type=jnp.float32)
    up_proj = jnp.einsum("nsd,fnd->sf", slot_rows, wu, preferred_element_type=jnp.float32)
    hidden = (jax.nn.silu(gate_proj) * up_proj).astype(jnp.bfloat16)
    partial_value = jnp.einsum(
        "sf,fnd->nsd", hidden, wd, preferred_element_type=jnp.float32
    ).astype(jnp.bfloat16)
    parts = _exchange(partial_value, n_narrow, False, 1)
    summed = jnp.sum(parts.astype(jnp.float32), axis=0).astype(jnp.bfloat16)
    returned = lax.all_to_all(summed, "wide", split_axis=0, concat_axis=0, tiled=True)
    mixed = jnp.einsum("ts,sd->td", combine, returned, preferred_element_type=jnp.float32)
    return mixed.astype(jnp.bfloat16)


def solution(mesh):
    in_specs = (
        P("wide", "narrow"),
        P("wide", None),
        P("wide", None),
        P("wide", "narrow", None),
        P("wide", "narrow", None),
        P("wide", "narrow", None),
    )
    out_specs = P("wide", "narrow")
    return jax.shard_map(local, mesh=mesh, in_specs=in_specs, out_specs=out_specs, check_vma=False)
```

```python
import jax
import jax.numpy as jnp
from jax import lax
from jax.experimental import pallas as pl
from jax.experimental.pallas import tpu as pltpu
from jax.sharding import PartitionSpec as P

MESH = pl.DeviceIdType.MESH


def _exchange_kernel(n_peers, pick_src, axis, x_ref, y_ref, send_sem, recv_sem, own_sem):
    me = lax.axis_index(axis)
    other = lax.axis_index("wide" if axis == "narrow" else "narrow")
    if axis == "narrow":
        dev = lambda p: (other, p)
    else:
        dev = lambda p: (p, other)
    barrier = pltpu.get_barrier_semaphore()
    for k in range(1, n_peers):
        peer = lax.rem(me + k, n_peers)
        pl.semaphore_signal(barrier, inc=1, device_id=dev(peer), device_id_type=MESH)
    pl.semaphore_wait(barrier, n_peers - 1)
    own = pltpu.make_async_copy(pick_src(x_ref, me), y_ref.at[me], own_sem)
    own.start()
    copies = []
    for k in range(1, n_peers):
        peer = lax.rem(me + k, n_peers)
        c = pltpu.make_async_remote_copy(
            src_ref=pick_src(x_ref, peer),
            dst_ref=y_ref.at[me],
            send_sem=send_sem.at[k - 1],
            recv_sem=recv_sem.at[k - 1],
            device_id=dev(peer),
            device_id_type=MESH,
        )
        c.start()
        copies.append(c)
    for k in range(1, n_peers):
        src = lax.rem(me + n_peers - k, n_peers)
        pltpu.make_async_remote_copy(
            src_ref=pick_src(x_ref, src),
            dst_ref=y_ref.at[src],
            send_sem=send_sem.at[k - 1],
            recv_sem=recv_sem.at[k - 1],
            device_id=dev(src),
            device_id_type=MESH,
        ).wait_recv()
    for c in copies:
        c.wait_send()
    own.wait()


def _exchange(x, n_peers, gather, collective_id, axis="narrow"):
    if gather:
        out_shape = (n_peers,) + x.shape
        pick_src = lambda ref, i: ref
    else:
        out_shape = x.shape
        pick_src = lambda ref, i: ref.at[i]
    nbytes = x.size * x.dtype.itemsize
    return pl.pallas_call(
        lambda *refs: _exchange_kernel(n_peers, pick_src, axis, *refs),
        out_shape=jax.ShapeDtypeStruct(out_shape, x.dtype),
        in_specs=[pl.BlockSpec(memory_space=pl.ANY)],
        out_specs=pl.BlockSpec(memory_space=pl.ANY),
        scratch_shapes=[
            pltpu.SemaphoreType.DMA((n_peers - 1,)),
            pltpu.SemaphoreType.DMA((n_peers - 1,)),
            pltpu.SemaphoreType.DMA(()),
        ],
        compiler_params=pltpu.CompilerParams(collective_id=collective_id, has_side_effects=True),
        cost_estimate=pl.CostEstimate(flops=0, bytes_accessed=2 * nbytes, transcendentals=0),
    )(x)


def local(tokens, expert_ids, route_weights, w_gate, w_up, w_down):
    tok_rows = expert_ids.shape[0]
    top_count = expert_ids.shape[1]
    local_experts = w_gate.shape[0]
    groups_wide = lax.axis_size("wide")
    experts_all = local_experts * groups_wide
    capacity = 7 * tok_rows * top_count // (6 * experts_all)
    slots_all = experts_all * capacity
    flat_ids = expert_ids.reshape(-1)
    onehot = (flat_ids[:, None] == jnp.arange(experts_all, dtype=jnp.int32)[None, :]).astype(
        jnp.int32
    )
    running = jnp.cumsum(onehot, axis=0)
    slot_index = jnp.sum(running * onehot, axis=1) - 1
    destination = (flat_ids * capacity + slot_index).reshape(tok_rows, top_count)
    hit = destination[:, :, None] == jnp.arange(slots_all, dtype=jnp.int32)[None, None, :]
    dispatch = jnp.any(hit, axis=1).astype(jnp.bfloat16)
    combine = jnp.sum(
        jnp.where(hit, route_weights.astype(jnp.float32)[:, :, None], 0.0), axis=1
    ).astype(jnp.bfloat16)
    outgoing = jnp.einsum("ts,td->sd", dispatch, tokens, preferred_element_type=jnp.float32).astype(
        jnp.bfloat16
    )
    received = _exchange(outgoing.reshape(groups_wide, capacity, -1), groups_wide, False, 2, "wide")
    received = received.reshape(slots_all, -1)
    n_narrow = lax.axis_size("narrow")
    width = tokens.shape[1]
    slot_rows = _exchange(received, n_narrow, True, 0)
    wg = w_gate[0].reshape(-1, n_narrow, width)
    wu = w_up[0].reshape(-1, n_narrow, width)
    wd = w_down[0].reshape(-1, n_narrow, width)
    gate_proj = jnp.einsum("nsd,fnd->sf", slot_rows, wg, preferred_element_type=jnp.float32)
    up_proj = jnp.einsum("nsd,fnd->sf", slot_rows, wu, preferred_element_type=jnp.float32)
    hidden = (jax.nn.silu(gate_proj) * up_proj).astype(jnp.bfloat16)
    partial_value = jnp.einsum(
        "sf,fnd->nsd", hidden, wd, preferred_element_type=jnp.float32
    ).astype(jnp.bfloat16)
    parts = _exchange(partial_value, n_narrow, False, 1)
    summed = jnp.sum(parts.astype(jnp.float32), axis=0).astype(jnp.bfloat16)
    returned = _exchange(summed.reshape(groups_wide, capacity, -1), groups_wide, False, 3, "wide")
    returned = returned.reshape(slots_all, -1)
    mixed = jnp.einsum("ts,sd->td", combine, returned, preferred_element_type=jnp.float32)
    return mixed.astype(jnp.bfloat16)


def solution(mesh):
    in_specs = (
        P("wide", "narrow"),
        P("wide", None),
        P("wide", None),
        P("wide", "narrow", None),
        P("wide", "narrow", None),
        P("wide", "narrow", None),
    )
    out_specs = P("wide", "narrow")
    return jax.shard_map(local, mesh=mesh, in_specs=in_specs, out_specs=out_specs, check_vma=False)
```

```python
import jax
import jax.numpy as jnp
from jax import lax
from jax.experimental import pallas as pl
from jax.experimental.pallas import tpu as pltpu
from jax.sharding import PartitionSpec as P

MESH = pl.DeviceIdType.MESH


def _exchange_kernel(n_peers, pick_src, axis, x_ref, y_ref, send_sem, recv_sem, own_sem):
    me = lax.axis_index(axis)
    other = lax.axis_index("wide" if axis == "narrow" else "narrow")
    if axis == "narrow":
        dev = lambda p: (other, p)
    else:
        dev = lambda p: (p, other)
    barrier = pltpu.get_barrier_semaphore()
    for k in range(1, n_peers):
        peer = lax.rem(me + k, n_peers)
        pl.semaphore_signal(barrier, inc=1, device_id=dev(peer), device_id_type=MESH)
    pl.semaphore_wait(barrier, n_peers - 1)
    own = pltpu.make_async_copy(pick_src(x_ref, me), y_ref.at[me], own_sem)
    own.start()
    copies = []
    for k in range(1, n_peers):
        peer = lax.rem(me + k, n_peers)
        c = pltpu.make_async_remote_copy(
            src_ref=pick_src(x_ref, peer),
            dst_ref=y_ref.at[me],
            send_sem=send_sem.at[k - 1],
            recv_sem=recv_sem.at[k - 1],
            device_id=dev(peer),
            device_id_type=MESH,
        )
        c.start()
        copies.append(c)
    for k in range(1, n_peers):
        src = lax.rem(me + n_peers - k, n_peers)
        pltpu.make_async_remote_copy(
            src_ref=pick_src(x_ref, src),
            dst_ref=y_ref.at[src],
            send_sem=send_sem.at[k - 1],
            recv_sem=recv_sem.at[k - 1],
            device_id=dev(src),
            device_id_type=MESH,
        ).wait_recv()
    for c in copies:
        c.wait_send()
    own.wait()


def _gather_kernel(x_ref, y_ref, sem_y, sem_x1, sem_x2, own_sem):
    me = lax.axis_index("narrow")
    w = lax.axis_index("wide")
    yh = me // 4
    xi = me % 4
    partner = (1 - yh) * 4 + xi
    right = yh * 4 + (xi + 1) % 4
    left = yh * 4 + (xi + 3) % 4
    barrier = pltpu.get_barrier_semaphore()
    for peer in (partner, right, left):
        pl.semaphore_signal(barrier, inc=1, device_id=(w, peer), device_id_type=MESH)
    pl.semaphore_wait(barrier, 3)

    def remote(src, slot, sem, peer):
        return pltpu.make_async_remote_copy(
            src_ref=src,
            dst_ref=y_ref.at[slot],
            send_sem=sem[0],
            recv_sem=sem[1],
            device_id=(w, peer),
            device_id_type=MESH,
        )

    own = pltpu.make_async_copy(x_ref, y_ref.at[me], own_sem)
    own.start()
    cy = remote(x_ref, me, (sem_y.at[0], sem_y.at[1]), partner)
    cy.start()
    c1 = [
        remote(x_ref, me, (sem_x1.at[0, 0], sem_x1.at[0, 1]), right),
        remote(x_ref, me, (sem_x1.at[1, 0], sem_x1.at[1, 1]), left),
    ]
    for c in c1:
        c.start()
    remote(x_ref, partner, (sem_y.at[0], sem_y.at[1]), partner).wait_recv()
    c2 = [
        remote(y_ref.at[partner], partner, (sem_x1.at[2, 0], sem_x1.at[2, 1]), right),
        remote(y_ref.at[partner], partner, (sem_x1.at[3, 0], sem_x1.at[3, 1]), left),
    ]
    for c in c2:
        c.start()
    lp = (1 - yh) * 4 + (xi + 3) % 4
    rp = (1 - yh) * 4 + (xi + 1) % 4
    remote(x_ref, left, (sem_x1.at[0, 0], sem_x1.at[0, 1]), left).wait_recv()
    remote(x_ref, right, (sem_x1.at[1, 0], sem_x1.at[1, 1]), right).wait_recv()
    c3 = [
        remote(y_ref.at[left], left, (sem_x2.at[0, 0], sem_x2.at[0, 1]), right),
    ]
    c3[0].start()
    remote(x_ref, rp, (sem_x1.at[3, 0], sem_x1.at[3, 1]), right).wait_recv()
    c4 = remote(y_ref.at[rp], rp, (sem_x2.at[1, 0], sem_x2.at[1, 1]), left)
    c4.start()
    remote(x_ref, lp, (sem_x1.at[2, 0], sem_x1.at[2, 1]), left).wait_recv()
    far = yh * 4 + (xi + 2) % 4
    far_p = (1 - yh) * 4 + (xi + 2) % 4
    remote(x_ref, far, (sem_x2.at[0, 0], sem_x2.at[0, 1]), left).wait_recv()
    remote(x_ref, far_p, (sem_x2.at[1, 0], sem_x2.at[1, 1]), right).wait_recv()
    for c in [cy] + c1 + c2 + c3 + [c4]:
        c.wait_send()
    own.wait()


def _gather(x, n_peers, collective_id):
    nbytes = x.size * x.dtype.itemsize
    return pl.pallas_call(
        _gather_kernel,
        out_shape=jax.ShapeDtypeStruct((n_peers,) + x.shape, x.dtype),
        in_specs=[pl.BlockSpec(memory_space=pl.ANY)],
        out_specs=pl.BlockSpec(memory_space=pl.ANY),
        scratch_shapes=[
            pltpu.SemaphoreType.DMA((2,)),
            pltpu.SemaphoreType.DMA((4, 2)),
            pltpu.SemaphoreType.DMA((2, 2)),
            pltpu.SemaphoreType.DMA(()),
        ],
        compiler_params=pltpu.CompilerParams(collective_id=collective_id, has_side_effects=True),
        cost_estimate=pl.CostEstimate(flops=0, bytes_accessed=2 * n_peers * nbytes, transcendentals=0),
    )(x)


def _exchange(x, n_peers, gather, collective_id, axis="narrow"):
    if gather:
        out_shape = (n_peers,) + x.shape
        pick_src = lambda ref, i: ref
    else:
        out_shape = x.shape
        pick_src = lambda ref, i: ref.at[i]
    nbytes = x.size * x.dtype.itemsize
    return pl.pallas_call(
        lambda *refs: _exchange_kernel(n_peers, pick_src, axis, *refs),
        out_shape=jax.ShapeDtypeStruct(out_shape, x.dtype),
        in_specs=[pl.BlockSpec(memory_space=pl.ANY)],
        out_specs=pl.BlockSpec(memory_space=pl.ANY),
        scratch_shapes=[
            pltpu.SemaphoreType.DMA((n_peers - 1,)),
            pltpu.SemaphoreType.DMA((n_peers - 1,)),
            pltpu.SemaphoreType.DMA(()),
        ],
        compiler_params=pltpu.CompilerParams(collective_id=collective_id, has_side_effects=True),
        cost_estimate=pl.CostEstimate(flops=0, bytes_accessed=2 * nbytes, transcendentals=0),
    )(x)


def local(tokens, expert_ids, route_weights, w_gate, w_up, w_down):
    tok_rows = expert_ids.shape[0]
    top_count = expert_ids.shape[1]
    local_experts = w_gate.shape[0]
    groups_wide = lax.axis_size("wide")
    experts_all = local_experts * groups_wide
    capacity = 7 * tok_rows * top_count // (6 * experts_all)
    slots_all = experts_all * capacity
    flat_ids = expert_ids.reshape(-1)
    onehot = (flat_ids[:, None] == jnp.arange(experts_all, dtype=jnp.int32)[None, :]).astype(
        jnp.int32
    )
    running = jnp.cumsum(onehot, axis=0)
    slot_index = jnp.sum(running * onehot, axis=1) - 1
    destination = (flat_ids * capacity + slot_index).reshape(tok_rows, top_count)
    hit = destination[:, :, None] == jnp.arange(slots_all, dtype=jnp.int32)[None, None, :]
    dispatch = jnp.any(hit, axis=1).astype(jnp.bfloat16)
    combine = jnp.sum(
        jnp.where(hit, route_weights.astype(jnp.float32)[:, :, None], 0.0), axis=1
    ).astype(jnp.bfloat16)
    outgoing = jnp.einsum("ts,td->sd", dispatch, tokens, preferred_element_type=jnp.float32).astype(
        jnp.bfloat16
    )
    received = _exchange(outgoing.reshape(groups_wide, capacity, -1), groups_wide, False, 2, "wide")
    received = received.reshape(slots_all, -1)
    n_narrow = lax.axis_size("narrow")
    width = tokens.shape[1]
    slot_rows = _gather(received, n_narrow, 0)
    wg = w_gate[0].reshape(-1, n_narrow, width)
    wu = w_up[0].reshape(-1, n_narrow, width)
    wd = w_down[0].reshape(-1, n_narrow, width)
    gate_proj = jnp.einsum("nsd,fnd->sf", slot_rows, wg, preferred_element_type=jnp.float32)
    up_proj = jnp.einsum("nsd,fnd->sf", slot_rows, wu, preferred_element_type=jnp.float32)
    hidden = (jax.nn.silu(gate_proj) * up_proj).astype(jnp.bfloat16)
    partial_value = jnp.einsum(
        "sf,fnd->nsd", hidden, wd, preferred_element_type=jnp.float32
    ).astype(jnp.bfloat16)
    parts = _exchange(partial_value, n_narrow, False, 1)
    summed = jnp.sum(parts.astype(jnp.float32), axis=0).astype(jnp.bfloat16)
    returned = _exchange(summed.reshape(groups_wide, capacity, -1), groups_wide, False, 3, "wide")
    returned = returned.reshape(slots_all, -1)
    mixed = jnp.einsum("ts,sd->td", combine, returned, preferred_element_type=jnp.float32)
    return mixed.astype(jnp.bfloat16)


def solution(mesh):
    in_specs = (
        P("wide", "narrow"),
        P("wide", None),
        P("wide", None),
        P("wide", "narrow", None),
        P("wide", "narrow", None),
        P("wide", "narrow", None),
    )
    out_specs = P("wide", "narrow")
    return jax.shard_map(local, mesh=mesh, in_specs=in_specs, out_specs=out_specs, check_vma=False)
```

```python
import jax
import jax.numpy as jnp
from jax import lax
from jax.experimental import pallas as pl
from jax.experimental.pallas import tpu as pltpu
from jax.sharding import PartitionSpec as P

MESH = pl.DeviceIdType.MESH


def _exchange_kernel(n_peers, pick_src, axis, x_ref, y_ref, send_sem, recv_sem, own_sem):
    me = lax.axis_index(axis)
    other = lax.axis_index("wide" if axis == "narrow" else "narrow")
    if axis == "narrow":
        dev = lambda p: (other, p)
    else:
        dev = lambda p: (p, other)
    barrier = pltpu.get_barrier_semaphore()
    for k in range(1, n_peers):
        peer = lax.rem(me + k, n_peers)
        pl.semaphore_signal(barrier, inc=1, device_id=dev(peer), device_id_type=MESH)
    pl.semaphore_wait(barrier, n_peers - 1)
    own = pltpu.make_async_copy(pick_src(x_ref, me), y_ref.at[me], own_sem)
    own.start()
    copies = []
    for k in range(1, n_peers):
        peer = lax.rem(me + k, n_peers)
        c = pltpu.make_async_remote_copy(
            src_ref=pick_src(x_ref, peer),
            dst_ref=y_ref.at[me],
            send_sem=send_sem.at[k - 1],
            recv_sem=recv_sem.at[k - 1],
            device_id=dev(peer),
            device_id_type=MESH,
        )
        c.start()
        copies.append(c)
    for k in range(1, n_peers):
        src = lax.rem(me + n_peers - k, n_peers)
        pltpu.make_async_remote_copy(
            src_ref=pick_src(x_ref, src),
            dst_ref=y_ref.at[src],
            send_sem=send_sem.at[k - 1],
            recv_sem=recv_sem.at[k - 1],
            device_id=dev(src),
            device_id_type=MESH,
        ).wait_recv()
    for c in copies:
        c.wait_send()
    own.wait()


def _gather_kernel(x_ref, y_ref, sem_y, sem_x1, sem_x2, own_sem):
    me = lax.axis_index("narrow")
    w = lax.axis_index("wide")
    yh = me // 4
    xi = me % 4
    partner = (1 - yh) * 4 + xi
    right = yh * 4 + (xi + 1) % 4
    left = yh * 4 + (xi + 3) % 4
    barrier = pltpu.get_barrier_semaphore()
    for peer in (partner, right, left):
        pl.semaphore_signal(barrier, inc=1, device_id=(w, peer), device_id_type=MESH)
    pl.semaphore_wait(barrier, 3)

    def remote(src, slot, sem, peer):
        return pltpu.make_async_remote_copy(
            src_ref=src,
            dst_ref=y_ref.at[slot],
            send_sem=sem[0],
            recv_sem=sem[1],
            device_id=(w, peer),
            device_id_type=MESH,
        )

    own = pltpu.make_async_copy(x_ref, y_ref.at[me], own_sem)
    own.start()
    cy = remote(x_ref, me, (sem_y.at[0], sem_y.at[1]), partner)
    cy.start()
    c1 = [
        remote(x_ref, me, (sem_x1.at[0, 0], sem_x1.at[0, 1]), right),
        remote(x_ref, me, (sem_x1.at[1, 0], sem_x1.at[1, 1]), left),
    ]
    for c in c1:
        c.start()
    remote(x_ref, partner, (sem_y.at[0], sem_y.at[1]), partner).wait_recv()
    c2 = [
        remote(y_ref.at[partner], partner, (sem_x1.at[2, 0], sem_x1.at[2, 1]), right),
        remote(y_ref.at[partner], partner, (sem_x1.at[3, 0], sem_x1.at[3, 1]), left),
    ]
    for c in c2:
        c.start()
    lp = (1 - yh) * 4 + (xi + 3) % 4
    rp = (1 - yh) * 4 + (xi + 1) % 4
    remote(x_ref, left, (sem_x1.at[0, 0], sem_x1.at[0, 1]), left).wait_recv()
    remote(x_ref, right, (sem_x1.at[1, 0], sem_x1.at[1, 1]), right).wait_recv()
    c3 = [
        remote(y_ref.at[left], left, (sem_x2.at[0, 0], sem_x2.at[0, 1]), right),
    ]
    c3[0].start()
    remote(x_ref, rp, (sem_x1.at[3, 0], sem_x1.at[3, 1]), right).wait_recv()
    c4 = remote(y_ref.at[rp], rp, (sem_x2.at[1, 0], sem_x2.at[1, 1]), left)
    c4.start()
    remote(x_ref, lp, (sem_x1.at[2, 0], sem_x1.at[2, 1]), left).wait_recv()
    far = yh * 4 + (xi + 2) % 4
    far_p = (1 - yh) * 4 + (xi + 2) % 4
    remote(x_ref, far, (sem_x2.at[0, 0], sem_x2.at[0, 1]), left).wait_recv()
    remote(x_ref, far_p, (sem_x2.at[1, 0], sem_x2.at[1, 1]), right).wait_recv()
    for c in [cy] + c1 + c2 + c3 + [c4]:
        c.wait_send()
    own.wait()


def _gather(x, n_peers, collective_id):
    nbytes = x.size * x.dtype.itemsize
    return pl.pallas_call(
        _gather_kernel,
        out_shape=jax.ShapeDtypeStruct((n_peers,) + x.shape, x.dtype),
        in_specs=[pl.BlockSpec(memory_space=pl.ANY)],
        out_specs=pl.BlockSpec(memory_space=pl.ANY),
        scratch_shapes=[
            pltpu.SemaphoreType.DMA((2,)),
            pltpu.SemaphoreType.DMA((4, 2)),
            pltpu.SemaphoreType.DMA((2, 2)),
            pltpu.SemaphoreType.DMA(()),
        ],
        compiler_params=pltpu.CompilerParams(collective_id=collective_id, has_side_effects=True),
        cost_estimate=pl.CostEstimate(flops=0, bytes_accessed=2 * n_peers * nbytes, transcendentals=0),
    )(x)


def _add_into(dst, *srcs):
    rows_all = dst.shape[0]
    step = 128 if rows_all % 128 == 0 else rows_all

    def body(i, carry):
        rows = pl.ds(pl.multiple_of(i * step, step), step)
        total = srcs[0][rows, :].astype(jnp.float32)
        for src in srcs[1:]:
            total = total + src[rows, :].astype(jnp.float32)
        dst[rows, :] = total.astype(dst.dtype)
        return carry

    lax.fori_loop(0, rows_all // step, body, 0)


def _reduce_kernel(p_ref, o_ref, rp, rm, sp, sm, qy, ry, sem_p, sem_m, sem_y):
    me = lax.axis_index("narrow")
    w = lax.axis_index("wide")
    yh = me // 4
    xi = me % 4
    other = 1 - yh
    partner = other * 4 + xi
    right = yh * 4 + (xi + 1) % 4
    left = yh * 4 + (xi + 3) % 4
    barrier = pltpu.get_barrier_semaphore()
    for peer in (partner, right, left):
        pl.semaphore_signal(barrier, inc=1, device_id=(w, peer), device_id_type=MESH)
    pl.semaphore_wait(barrier, 3)

    def remote(src, dst, sem, peer):
        return pltpu.make_async_remote_copy(
            src_ref=src,
            dst_ref=dst,
            send_sem=sem.at[0],
            recv_sem=sem.at[1],
            device_id=(w, peer),
            device_id_type=MESH,
        )

    mine = lambda h, k: p_ref.at[h * 4 + (xi + k) % 4]
    sends = []
    c = remote(mine(other, 3), rp.at[0], sem_p.at[0], right)
    c.start()
    sends.append(c)
    c = remote(mine(yh, 1), rm.at[0], sem_m.at[0], left)
    c.start()
    sends.append(c)
    for step, (kp, km) in enumerate(((2, 2), (1, 3))):
        remote(sp.at[step], rp.at[step], sem_p.at[step], left).wait_recv()
        _add_into(sp.at[step], rp.at[step], mine(other, kp))
        c = remote(sp.at[step], rp.at[step + 1], sem_p.at[step + 1], right)
        c.start()
        sends.append(c)
        remote(sm.at[step], rm.at[step], sem_m.at[step], right).wait_recv()
        _add_into(sm.at[step], rm.at[step], mine(yh, km))
        c = remote(sm.at[step], rm.at[step + 1], sem_m.at[step + 1], left)
        c.start()
        sends.append(c)
    remote(qy, rp.at[2], sem_p.at[2], left).wait_recv()
    _add_into(qy, rp.at[2], mine(other, 0))
    c = remote(qy, ry, sem_y, partner)
    c.start()
    sends.append(c)
    remote(sm.at[1], rm.at[2], sem_m.at[2], right).wait_recv()
    remote(qy, ry, sem_y, partner).wait_recv()
    _add_into(o_ref, rm.at[2], mine(yh, 0), ry)
    for c in sends:
        c.wait_send()


def _reduce(p, collective_id):
    n_peers, rows, cols = p.shape
    block = pltpu.VMEM((rows, cols), p.dtype)
    return pl.pallas_call(
        _reduce_kernel,
        out_shape=jax.ShapeDtypeStruct((rows, cols), p.dtype),
        in_specs=[pl.BlockSpec(memory_space=pltpu.VMEM)],
        out_specs=pl.BlockSpec(memory_space=pltpu.VMEM),
        scratch_shapes=[
            pltpu.VMEM((3, rows, cols), p.dtype),
            pltpu.VMEM((3, rows, cols), p.dtype),
            pltpu.VMEM((2, rows, cols), p.dtype),
            pltpu.VMEM((2, rows, cols), p.dtype),
            block,
            block,
            pltpu.SemaphoreType.DMA((3, 2)),
            pltpu.SemaphoreType.DMA((3, 2)),
            pltpu.SemaphoreType.DMA((2,)),
        ],
        compiler_params=pltpu.CompilerParams(collective_id=collective_id, has_side_effects=True),
        cost_estimate=pl.CostEstimate(
            flops=2 * p.size, bytes_accessed=2 * p.size * p.dtype.itemsize, transcendentals=0
        ),
    )(p)


def _exchange(x, n_peers, gather, collective_id, axis="narrow"):
    if gather:
        out_shape = (n_peers,) + x.shape
        pick_src = lambda ref, i: ref
    else:
        out_shape = x.shape
        pick_src = lambda ref, i: ref.at[i]
    nbytes = x.size * x.dtype.itemsize
    return pl.pallas_call(
        lambda *refs: _exchange_kernel(n_peers, pick_src, axis, *refs),
        out_shape=jax.ShapeDtypeStruct(out_shape, x.dtype),
        in_specs=[pl.BlockSpec(memory_space=pl.ANY)],
        out_specs=pl.BlockSpec(memory_space=pl.ANY),
        scratch_shapes=[
            pltpu.SemaphoreType.DMA((n_peers - 1,)),
            pltpu.SemaphoreType.DMA((n_peers - 1,)),
            pltpu.SemaphoreType.DMA(()),
        ],
        compiler_params=pltpu.CompilerParams(collective_id=collective_id, has_side_effects=True),
        cost_estimate=pl.CostEstimate(flops=0, bytes_accessed=2 * nbytes, transcendentals=0),
    )(x)


def local(tokens, expert_ids, route_weights, w_gate, w_up, w_down):
    tok_rows = expert_ids.shape[0]
    top_count = expert_ids.shape[1]
    local_experts = w_gate.shape[0]
    groups_wide = lax.axis_size("wide")
    experts_all = local_experts * groups_wide
    capacity = 7 * tok_rows * top_count // (6 * experts_all)
    slots_all = experts_all * capacity
    flat_ids = expert_ids.reshape(-1)
    onehot = (flat_ids[:, None] == jnp.arange(experts_all, dtype=jnp.int32)[None, :]).astype(
        jnp.int32
    )
    running = jnp.cumsum(onehot, axis=0)
    slot_index = jnp.sum(running * onehot, axis=1) - 1
    destination = (flat_ids * capacity + slot_index).reshape(tok_rows, top_count)
    hit = destination[:, :, None] == jnp.arange(slots_all, dtype=jnp.int32)[None, None, :]
    dispatch = jnp.any(hit, axis=1).astype(jnp.bfloat16)
    combine = jnp.sum(
        jnp.where(hit, route_weights.astype(jnp.float32)[:, :, None], 0.0), axis=1
    ).astype(jnp.bfloat16)
    outgoing = jnp.einsum("ts,td->sd", dispatch, tokens, preferred_element_type=jnp.float32).astype(
        jnp.bfloat16
    )
    received = _exchange(outgoing.reshape(groups_wide, capacity, -1), groups_wide, False, 2, "wide")
    received = received.reshape(slots_all, -1)
    n_narrow = lax.axis_size("narrow")
    width = tokens.shape[1]
    slot_rows = _gather(received, n_narrow, 0)
    wg = w_gate[0].reshape(-1, n_narrow, width)
    wu = w_up[0].reshape(-1, n_narrow, width)
    wd = w_down[0].reshape(-1, n_narrow, width)
    gate_proj = jnp.einsum("nsd,fnd->sf", slot_rows, wg, preferred_element_type=jnp.float32)
    up_proj = jnp.einsum("nsd,fnd->sf", slot_rows, wu, preferred_element_type=jnp.float32)
    hidden = (jax.nn.silu(gate_proj) * up_proj).astype(jnp.bfloat16)
    partial_value = jnp.einsum(
        "sf,fnd->nsd", hidden, wd, preferred_element_type=jnp.float32
    ).astype(jnp.bfloat16)
    summed = _reduce(partial_value, 1)
    returned = _exchange(summed.reshape(groups_wide, capacity, -1), groups_wide, False, 3, "wide")
    returned = returned.reshape(slots_all, -1)
    mixed = jnp.einsum("ts,sd->td", combine, returned, preferred_element_type=jnp.float32)
    return mixed.astype(jnp.bfloat16)


def solution(mesh):
    in_specs = (
        P("wide", "narrow"),
        P("wide", None),
        P("wide", None),
        P("wide", "narrow", None),
        P("wide", "narrow", None),
        P("wide", "narrow", None),
    )
    out_specs = P("wide", "narrow")
    return jax.shard_map(local, mesh=mesh, in_specs=in_specs, out_specs=out_specs, check_vma=False)
```

```python
import jax
import jax.numpy as jnp
from jax import lax
from jax.experimental import pallas as pl
from jax.experimental.pallas import tpu as pltpu
from jax.sharding import PartitionSpec as P

MESH = pl.DeviceIdType.MESH


def _exchange_kernel(n_peers, pick_src, axis, x_ref, y_ref, send_sem, recv_sem, own_sem):
    me = lax.axis_index(axis)
    other = lax.axis_index("wide" if axis == "narrow" else "narrow")
    if axis == "narrow":
        dev = lambda p: (other, p)
    else:
        dev = lambda p: (p, other)
    barrier = pltpu.get_barrier_semaphore()
    for k in range(1, n_peers):
        peer = lax.rem(me + k, n_peers)
        pl.semaphore_signal(barrier, inc=1, device_id=dev(peer), device_id_type=MESH)
    pl.semaphore_wait(barrier, n_peers - 1)
    own = pltpu.make_async_copy(pick_src(x_ref, me), y_ref.at[me], own_sem)
    own.start()
    copies = []
    for k in range(1, n_peers):
        peer = lax.rem(me + k, n_peers)
        c = pltpu.make_async_remote_copy(
            src_ref=pick_src(x_ref, peer),
            dst_ref=y_ref.at[me],
            send_sem=send_sem.at[k - 1],
            recv_sem=recv_sem.at[k - 1],
            device_id=dev(peer),
            device_id_type=MESH,
        )
        c.start()
        copies.append(c)
    for k in range(1, n_peers):
        src = lax.rem(me + n_peers - k, n_peers)
        pltpu.make_async_remote_copy(
            src_ref=pick_src(x_ref, src),
            dst_ref=y_ref.at[src],
            send_sem=send_sem.at[k - 1],
            recv_sem=recv_sem.at[k - 1],
            device_id=dev(src),
            device_id_type=MESH,
        ).wait_recv()
    for c in copies:
        c.wait_send()
    own.wait()


def _gather_kernel(x_ref, y_ref, sem_y, sem_x1, sem_x2, own_sem):
    me = lax.axis_index("narrow")
    w = lax.axis_index("wide")
    yh = me // 4
    xi = me % 4
    partner = (1 - yh) * 4 + xi
    right = yh * 4 + (xi + 1) % 4
    left = yh * 4 + (xi + 3) % 4
    barrier = pltpu.get_barrier_semaphore()
    for peer in (partner, right, left):
        pl.semaphore_signal(barrier, inc=1, device_id=(w, peer), device_id_type=MESH)
    pl.semaphore_wait(barrier, 3)

    def remote(src, slot, sem, peer):
        return pltpu.make_async_remote_copy(
            src_ref=src,
            dst_ref=y_ref.at[slot],
            send_sem=sem[0],
            recv_sem=sem[1],
            device_id=(w, peer),
            device_id_type=MESH,
        )

    own = pltpu.make_async_copy(x_ref, y_ref.at[me], own_sem)
    own.start()
    cy = remote(x_ref, me, (sem_y.at[0], sem_y.at[1]), partner)
    cy.start()
    c1 = [
        remote(x_ref, me, (sem_x1.at[0, 0], sem_x1.at[0, 1]), right),
        remote(x_ref, me, (sem_x1.at[1, 0], sem_x1.at[1, 1]), left),
    ]
    for c in c1:
        c.start()
    remote(x_ref, partner, (sem_y.at[0], sem_y.at[1]), partner).wait_recv()
    c2 = [
        remote(y_ref.at[partner], partner, (sem_x1.at[2, 0], sem_x1.at[2, 1]), right),
        remote(y_ref.at[partner], partner, (sem_x1.at[3, 0], sem_x1.at[3, 1]), left),
    ]
    for c in c2:
        c.start()
    lp = (1 - yh) * 4 + (xi + 3) % 4
    rp = (1 - yh) * 4 + (xi + 1) % 4
    remote(x_ref, left, (sem_x1.at[0, 0], sem_x1.at[0, 1]), left).wait_recv()
    remote(x_ref, right, (sem_x1.at[1, 0], sem_x1.at[1, 1]), right).wait_recv()
    c3 = [
        remote(y_ref.at[left], left, (sem_x2.at[0, 0], sem_x2.at[0, 1]), right),
    ]
    c3[0].start()
    remote(x_ref, rp, (sem_x1.at[3, 0], sem_x1.at[3, 1]), right).wait_recv()
    c4 = remote(y_ref.at[rp], rp, (sem_x2.at[1, 0], sem_x2.at[1, 1]), left)
    c4.start()
    remote(x_ref, lp, (sem_x1.at[2, 0], sem_x1.at[2, 1]), left).wait_recv()
    far = yh * 4 + (xi + 2) % 4
    far_p = (1 - yh) * 4 + (xi + 2) % 4
    remote(x_ref, far, (sem_x2.at[0, 0], sem_x2.at[0, 1]), left).wait_recv()
    remote(x_ref, far_p, (sem_x2.at[1, 0], sem_x2.at[1, 1]), right).wait_recv()
    for c in [cy] + c1 + c2 + c3 + [c4]:
        c.wait_send()
    own.wait()


def _gather(x, n_peers, collective_id):
    nbytes = x.size * x.dtype.itemsize
    return pl.pallas_call(
        _gather_kernel,
        out_shape=jax.ShapeDtypeStruct((n_peers,) + x.shape, x.dtype),
        in_specs=[pl.BlockSpec(memory_space=pl.ANY)],
        out_specs=pl.BlockSpec(memory_space=pl.ANY),
        scratch_shapes=[
            pltpu.SemaphoreType.DMA((2,)),
            pltpu.SemaphoreType.DMA((4, 2)),
            pltpu.SemaphoreType.DMA((2, 2)),
            pltpu.SemaphoreType.DMA(()),
        ],
        compiler_params=pltpu.CompilerParams(collective_id=collective_id, has_side_effects=True),
        cost_estimate=pl.CostEstimate(flops=0, bytes_accessed=2 * n_peers * nbytes, transcendentals=0),
    )(x)


def _add_into(dst, *srcs):
    rows_all = dst.shape[0]
    step = 128 if rows_all % 128 == 0 else rows_all

    def body(i, carry):
        rows = pl.ds(pl.multiple_of(i * step, step), step)
        total = srcs[0][rows, :].astype(jnp.float32)
        for src in srcs[1:]:
            total = total + src[rows, :].astype(jnp.float32)
        dst[rows, :] = total.astype(dst.dtype)
        return carry

    lax.fori_loop(0, rows_all // step, body, 0)


def _reduce_kernel(p_ref, o_ref, rp, rm, sp, sm, qy, ry, sem_p, sem_m, sem_y):
    me = lax.axis_index("narrow")
    w = lax.axis_index("wide")
    yh = me // 4
    xi = me % 4
    other = 1 - yh
    partner = other * 4 + xi
    right = yh * 4 + (xi + 1) % 4
    left = yh * 4 + (xi + 3) % 4
    barrier = pltpu.get_barrier_semaphore()
    for peer in (partner, right, left):
        pl.semaphore_signal(barrier, inc=1, device_id=(w, peer), device_id_type=MESH)
    pl.semaphore_wait(barrier, 3)

    def remote(src, dst, sem, peer):
        return pltpu.make_async_remote_copy(
            src_ref=src,
            dst_ref=dst,
            send_sem=sem.at[0],
            recv_sem=sem.at[1],
            device_id=(w, peer),
            device_id_type=MESH,
        )

    mine = lambda h, k: p_ref.at[h * 4 + (xi + k) % 4]
    sends = []
    c = remote(mine(other, 3), rp.at[0], sem_p.at[0], right)
    c.start()
    sends.append(c)
    c = remote(mine(yh, 1), rm.at[0], sem_m.at[0], left)
    c.start()
    sends.append(c)
    for step, (kp, km) in enumerate(((2, 2), (1, 3))):
        remote(sp.at[step], rp.at[step], sem_p.at[step], left).wait_recv()
        _add_into(sp.at[step], rp.at[step], mine(other, kp))
        c = remote(sp.at[step], rp.at[step + 1], sem_p.at[step + 1], right)
        c.start()
        sends.append(c)
        remote(sm.at[step], rm.at[step], sem_m.at[step], right).wait_recv()
        _add_into(sm.at[step], rm.at[step], mine(yh, km))
        c = remote(sm.at[step], rm.at[step + 1], sem_m.at[step + 1], left)
        c.start()
        sends.append(c)
    remote(qy, rp.at[2], sem_p.at[2], left).wait_recv()
    _add_into(qy, rp.at[2], mine(other, 0))
    c = remote(qy, ry, sem_y, partner)
    c.start()
    sends.append(c)
    remote(sm.at[1], rm.at[2], sem_m.at[2], right).wait_recv()
    remote(qy, ry, sem_y, partner).wait_recv()
    _add_into(o_ref, rm.at[2], mine(yh, 0), ry)
    for c in sends:
        c.wait_send()


def _reduce(p, collective_id):
    n_peers, rows, cols = p.shape
    block = pltpu.VMEM((rows, cols), p.dtype)
    return pl.pallas_call(
        _reduce_kernel,
        out_shape=jax.ShapeDtypeStruct((rows, cols), p.dtype),
        in_specs=[pl.BlockSpec(memory_space=pltpu.VMEM)],
        out_specs=pl.BlockSpec(memory_space=pltpu.VMEM),
        scratch_shapes=[
            pltpu.VMEM((3, rows, cols), p.dtype),
            pltpu.VMEM((3, rows, cols), p.dtype),
            pltpu.VMEM((2, rows, cols), p.dtype),
            pltpu.VMEM((2, rows, cols), p.dtype),
            block,
            block,
            pltpu.SemaphoreType.DMA((3, 2)),
            pltpu.SemaphoreType.DMA((3, 2)),
            pltpu.SemaphoreType.DMA((2,)),
        ],
        compiler_params=pltpu.CompilerParams(collective_id=collective_id, has_side_effects=True),
        cost_estimate=pl.CostEstimate(
            flops=2 * p.size, bytes_accessed=2 * p.size * p.dtype.itemsize, transcendentals=0
        ),
    )(p)


def _wide_kernel(x_ref, y_ref, t_ref, sem_z, sem_g, own_z, own_g):
    nz = x_ref.shape[1]
    me = lax.axis_index("wide")
    n = lax.axis_index("narrow")
    yl = me // (2 * nz)
    zi = (me // 2) % nz
    co = me % 2
    dev = lambda a, z, c: ((a * nz + z) * 2 + c, n)
    groups = [((yl + j // 2) % 2, (co + j % 2) % 2) for j in range(1, 4)]
    barrier = pltpu.get_barrier_semaphore()
    for k in range(1, nz):
        pl.semaphore_signal(barrier, inc=1, device_id=dev(yl, (zi + k) % nz, co), device_id_type=MESH)
    for a, c in groups:
        pl.semaphore_signal(barrier, inc=1, device_id=dev(a, zi, c), device_id_type=MESH)
    pl.semaphore_wait(barrier, nz - 1 + 3)

    def remote(src, dst, sem, peer):
        return pltpu.make_async_remote_copy(
            src_ref=src,
            dst_ref=dst,
            send_sem=sem.at[0],
            recv_sem=sem.at[1],
            device_id=peer,
            device_id_type=MESH,
        )

    own = pltpu.make_async_copy(x_ref.at[:, zi], t_ref.at[zi], own_z)
    own.start()
    sends = []
    for k in range(1, nz):
        zp = (zi + k) % nz
        c = remote(x_ref.at[:, zp], t_ref.at[zi], sem_z.at[k - 1], dev(yl, zp, co))
        c.start()
        sends.append(c)
    for k in range(1, nz):
        zs = (zi + nz - k) % nz
        remote(x_ref.at[:, zs], t_ref.at[zs], sem_z.at[k - 1], dev(yl, zs, co)).wait_recv()
    own.wait()
    own = pltpu.make_async_copy(t_ref.at[:, yl, co], y_ref.at[yl, :, co], own_g)
    own.start()
    for j, (a, c) in enumerate(groups):
        cp = remote(t_ref.at[:, a, c], y_ref.at[yl, :, co], sem_g.at[j], dev(a, zi, c))
        cp.start()
        sends.append(cp)
    for j, (a, c) in enumerate(groups):
        remote(t_ref.at[:, yl, co], y_ref.at[a, :, c], sem_g.at[j], dev(a, zi, c)).wait_recv()
    for c in sends:
        c.wait_send()
    own.wait()


def _wide(x, collective_id):
    n_dev, rows, cols = x.shape
    nz = n_dev // 4
    x = x.reshape(2, nz, 2, rows, cols)
    y = pl.pallas_call(
        _wide_kernel,
        out_shape=jax.ShapeDtypeStruct(x.shape, x.dtype),
        in_specs=[pl.BlockSpec(memory_space=pl.ANY)],
        out_specs=pl.BlockSpec(memory_space=pl.ANY),
        scratch_shapes=[
            pltpu.VMEM((nz, 2, 2, rows, cols), x.dtype),
            pltpu.SemaphoreType.DMA((nz - 1, 2)),
            pltpu.SemaphoreType.DMA((3, 2)),
            pltpu.SemaphoreType.DMA(()),
            pltpu.SemaphoreType.DMA(()),
        ],
        compiler_params=pltpu.CompilerParams(collective_id=collective_id, has_side_effects=True),
        cost_estimate=pl.CostEstimate(flops=0, bytes_accessed=4 * x.size * x.dtype.itemsize, transcendentals=0),
    )(x)
    return y.reshape(n_dev, rows, cols)


def _exchange(x, n_peers, gather, collective_id, axis="narrow"):
    if gather:
        out_shape = (n_peers,) + x.shape
        pick_src = lambda ref, i: ref
    else:
        out_shape = x.shape
        pick_src = lambda ref, i: ref.at[i]
    nbytes = x.size * x.dtype.itemsize
    return pl.pallas_call(
        lambda *refs: _exchange_kernel(n_peers, pick_src, axis, *refs),
        out_shape=jax.ShapeDtypeStruct(out_shape, x.dtype),
        in_specs=[pl.BlockSpec(memory_space=pl.ANY)],
        out_specs=pl.BlockSpec(memory_space=pl.ANY),
        scratch_shapes=[
            pltpu.SemaphoreType.DMA((n_peers - 1,)),
            pltpu.SemaphoreType.DMA((n_peers - 1,)),
            pltpu.SemaphoreType.DMA(()),
        ],
        compiler_params=pltpu.CompilerParams(collective_id=collective_id, has_side_effects=True),
        cost_estimate=pl.CostEstimate(flops=0, bytes_accessed=2 * nbytes, transcendentals=0),
    )(x)


def local(tokens, expert_ids, route_weights, w_gate, w_up, w_down):
    tok_rows = expert_ids.shape[0]
    top_count = expert_ids.shape[1]
    local_experts = w_gate.shape[0]
    groups_wide = lax.axis_size("wide")
    experts_all = local_experts * groups_wide
    capacity = 7 * tok_rows * top_count // (6 * experts_all)
    slots_all = experts_all * capacity
    flat_ids = expert_ids.reshape(-1)
    onehot = (flat_ids[:, None] == jnp.arange(experts_all, dtype=jnp.int32)[None, :]).astype(
        jnp.int32
    )
    running = jnp.cumsum(onehot, axis=0)
    slot_index = jnp.sum(running * onehot, axis=1) - 1
    destination = (flat_ids * capacity + slot_index).reshape(tok_rows, top_count)
    hit = destination[:, :, None] == jnp.arange(slots_all, dtype=jnp.int32)[None, None, :]
    dispatch = jnp.any(hit, axis=1).astype(jnp.bfloat16)
    combine = jnp.sum(
        jnp.where(hit, route_weights.astype(jnp.float32)[:, :, None], 0.0), axis=1
    ).astype(jnp.bfloat16)
    outgoing = jnp.einsum("ts,td->sd", dispatch, tokens, preferred_element_type=jnp.float32).astype(
        jnp.bfloat16
    )
    received = _wide(outgoing.reshape(groups_wide, capacity, -1), 2)
    received = received.reshape(slots_all, -1)
    n_narrow = lax.axis_size("narrow")
    width = tokens.shape[1]
    slot_rows = _gather(received, n_narrow, 0)
    wg = w_gate[0].reshape(-1, n_narrow, width)
    wu = w_up[0].reshape(-1, n_narrow, width)
    wd = w_down[0].reshape(-1, n_narrow, width)
    gate_proj = jnp.einsum("nsd,fnd->sf", slot_rows, wg, preferred_element_type=jnp.float32)
    up_proj = jnp.einsum("nsd,fnd->sf", slot_rows, wu, preferred_element_type=jnp.float32)
    hidden = (jax.nn.silu(gate_proj) * up_proj).astype(jnp.bfloat16)
    partial_value = jnp.einsum(
        "sf,fnd->nsd", hidden, wd, preferred_element_type=jnp.float32
    ).astype(jnp.bfloat16)
    summed = _reduce(partial_value, 1)
    returned = _wide(summed.reshape(groups_wide, capacity, -1), 3)
    returned = returned.reshape(slots_all, -1)
    mixed = jnp.einsum("ts,sd->td", combine, returned, preferred_element_type=jnp.float32)
    return mixed.astype(jnp.bfloat16)


def solution(mesh):
    in_specs = (
        P("wide", "narrow"),
        P("wide", None),
        P("wide", None),
        P("wide", "narrow", None),
        P("wide", "narrow", None),
        P("wide", "narrow", None),
    )
    out_specs = P("wide", "narrow")
    return jax.shard_map(local, mesh=mesh, in_specs=in_specs, out_specs=out_specs, check_vma=False)
```

```python
import types

import jax
import jax.numpy as jnp
from jax import lax
from jax.experimental import pallas as pl
from jax.experimental.pallas import tpu as pltpu
from jax.sharding import PartitionSpec as P

MESH = pl.DeviceIdType.MESH


def _exchange_kernel(n_peers, pick_src, axis, x_ref, y_ref, send_sem, recv_sem, own_sem):
    me = lax.axis_index(axis)
    other = lax.axis_index("wide" if axis == "narrow" else "narrow")
    if axis == "narrow":
        dev = lambda p: (other, p)
    else:
        dev = lambda p: (p, other)
    barrier = pltpu.get_barrier_semaphore()
    for k in range(1, n_peers):
        peer = lax.rem(me + k, n_peers)
        pl.semaphore_signal(barrier, inc=1, device_id=dev(peer), device_id_type=MESH)
    pl.semaphore_wait(barrier, n_peers - 1)
    own = pltpu.make_async_copy(pick_src(x_ref, me), y_ref.at[me], own_sem)
    own.start()
    copies = []
    for k in range(1, n_peers):
        peer = lax.rem(me + k, n_peers)
        c = pltpu.make_async_remote_copy(
            src_ref=pick_src(x_ref, peer),
            dst_ref=y_ref.at[me],
            send_sem=send_sem.at[k - 1],
            recv_sem=recv_sem.at[k - 1],
            device_id=dev(peer),
            device_id_type=MESH,
        )
        c.start()
        copies.append(c)
    for k in range(1, n_peers):
        src = lax.rem(me + n_peers - k, n_peers)
        pltpu.make_async_remote_copy(
            src_ref=pick_src(x_ref, src),
            dst_ref=y_ref.at[src],
            send_sem=send_sem.at[k - 1],
            recv_sem=recv_sem.at[k - 1],
            device_id=dev(src),
            device_id_type=MESH,
        ).wait_recv()
    for c in copies:
        c.wait_send()
    own.wait()


def _gather_chain(x_ref, slot_of, sem_y, sem_x1, sem_x2, own_sem):
    me = lax.axis_index("narrow")
    w = lax.axis_index("wide")
    yh = me // 4
    xi = me % 4
    partner = (1 - yh) * 4 + xi
    right = yh * 4 + (xi + 1) % 4
    left = yh * 4 + (xi + 3) % 4

    y_ref = types.SimpleNamespace(at=_Slots(slot_of))

    def remote(src, slot, sem, peer):
        return pltpu.make_async_remote_copy(
            src_ref=src,
            dst_ref=y_ref.at[slot],
            send_sem=sem[0],
            recv_sem=sem[1],
            device_id=(w, peer),
            device_id_type=MESH,
        )

    own = pltpu.make_async_copy(x_ref, y_ref.at[me], own_sem)
    own.start()
    cy = remote(x_ref, me, (sem_y.at[0], sem_y.at[1]), partner)
    cy.start()
    c1 = [
        remote(x_ref, me, (sem_x1.at[0, 0], sem_x1.at[0, 1]), right),
        remote(x_ref, me, (sem_x1.at[1, 0], sem_x1.at[1, 1]), left),
    ]
    for c in c1:
        c.start()
    remote(x_ref, partner, (sem_y.at[0], sem_y.at[1]), partner).wait_recv()
    c2 = [
        remote(y_ref.at[partner], partner, (sem_x1.at[2, 0], sem_x1.at[2, 1]), right),
        remote(y_ref.at[partner], partner, (sem_x1.at[3, 0], sem_x1.at[3, 1]), left),
    ]
    for c in c2:
        c.start()
    lp = (1 - yh) * 4 + (xi + 3) % 4
    rp = (1 - yh) * 4 + (xi + 1) % 4
    remote(x_ref, left, (sem_x1.at[0, 0], sem_x1.at[0, 1]), left).wait_recv()
    remote(x_ref, right, (sem_x1.at[1, 0], sem_x1.at[1, 1]), right).wait_recv()
    c3 = [
        remote(y_ref.at[left], left, (sem_x2.at[0, 0], sem_x2.at[0, 1]), right),
    ]
    c3[0].start()
    remote(x_ref, rp, (sem_x1.at[3, 0], sem_x1.at[3, 1]), right).wait_recv()
    c4 = remote(y_ref.at[rp], rp, (sem_x2.at[1, 0], sem_x2.at[1, 1]), left)
    c4.start()
    remote(x_ref, lp, (sem_x1.at[2, 0], sem_x1.at[2, 1]), left).wait_recv()
    far = yh * 4 + (xi + 2) % 4
    far_p = (1 - yh) * 4 + (xi + 2) % 4
    remote(x_ref, far, (sem_x2.at[0, 0], sem_x2.at[0, 1]), left).wait_recv()
    remote(x_ref, far_p, (sem_x2.at[1, 0], sem_x2.at[1, 1]), right).wait_recv()
    return [cy] + c1 + c2 + c3 + [c4], own


class _Slots:
    def __init__(self, fn):
        self.fn = fn

    def __getitem__(self, k):
        return self.fn(k)


def _narrow_peers():
    me = lax.axis_index("narrow")
    yh = me // 4
    xi = me % 4
    return ((1 - yh) * 4 + xi, yh * 4 + (xi + 1) % 4, yh * 4 + (xi + 3) % 4)


def _dispatch_kernel(x_ref, y_ref, r_ref, sem_w, own_w, sem_y, sem_x1, sem_x2, own_g):
    nw, _, cols = x_ref.shape
    halves = 2
    cw = cols // halves
    me_w = lax.axis_index("wide")
    me = lax.axis_index("narrow")
    barrier = pltpu.get_barrier_semaphore()

    def greet(k, carry):
        pl.semaphore_signal(barrier, inc=1, device_id=((me_w + k) % nw, me), device_id_type=MESH)
        return carry

    lax.fori_loop(1, nw, greet, 0)
    for peer in _narrow_peers():
        pl.semaphore_signal(barrier, inc=1, device_id=(me_w, peer), device_id_type=MESH)
    pl.semaphore_wait(barrier, nw - 1 + 3)

    def wide_copy(h, k, peer_of_copy, target):
        cs = pl.ds(h * cw, cw)
        return pltpu.make_async_remote_copy(
            src_ref=x_ref.at[peer_of_copy, :, cs],
            dst_ref=r_ref.at[target, :, cs],
            send_sem=sem_w.at[h, k, 0],
            recv_sem=sem_w.at[h, k, 1],
            device_id=(peer_of_copy, me),
            device_id_type=MESH,
        )

    def wide_start(h):
        cs = pl.ds(h * cw, cw)
        own = pltpu.make_async_copy(x_ref.at[me_w, :, cs], r_ref.at[me_w, :, cs], own_w.at[h])
        own.start()

        def body(k, carry):
            wide_copy(h, k, (me_w + k) % nw, me_w).start()
            return carry

        lax.fori_loop(1, nw, body, 0)
        return own

    def wide_wait(h, own):
        def body(k, carry):
            src = (me_w + nw - k) % nw
            pltpu.make_async_remote_copy(
                src_ref=x_ref.at[src, :, pl.ds(h * cw, cw)],
                dst_ref=r_ref.at[src, :, pl.ds(h * cw, cw)],
                send_sem=sem_w.at[h, k, 0],
                recv_sem=sem_w.at[h, k, 1],
                device_id=(src, me),
                device_id_type=MESH,
            ).wait_recv()
            return carry

        lax.fori_loop(1, nw, body, 0)
        own.wait()

    def wide_sent(h):
        def body(k, carry):
            wide_copy(h, k, (me_w + k) % nw, me_w).wait_send()
            return carry

        lax.fori_loop(1, nw, body, 0)

    pending = []
    own0 = wide_start(0)
    wide_wait(0, own0)
    own1 = wide_start(1)
    for h in range(halves):
        if h == 1:
            wide_wait(1, own1)
        cs = pl.ds(h * cw, cw)
        sends, own = _gather_chain(
            r_ref.at[:, :, cs],
            lambda k, cs=cs: y_ref.at[k, :, :, cs],
            sem_y.at[h],
            sem_x1.at[h],
            sem_x2.at[h],
            own_g.at[h],
        )
        pending.append((sends, own))
    for h in range(halves):
        wide_sent(h)
        sends, own = pending[h]
        for c in sends:
            c.wait_send()
        own.wait()


def _dispatch(x, n_narrow, collective_id):
    nw, rows, cols = x.shape
    return pl.pallas_call(
        _dispatch_kernel,
        out_shape=jax.ShapeDtypeStruct((n_narrow, nw, rows, cols), x.dtype),
        in_specs=[pl.BlockSpec(memory_space=pl.ANY)],
        out_specs=pl.BlockSpec(memory_space=pl.ANY),
        scratch_shapes=[
            pltpu.VMEM((nw, rows, cols), x.dtype),
            pltpu.SemaphoreType.DMA((2, nw, 2)),
            pltpu.SemaphoreType.DMA((2,)),
            pltpu.SemaphoreType.DMA((2, 2)),
            pltpu.SemaphoreType.DMA((2, 4, 2)),
            pltpu.SemaphoreType.DMA((2, 2, 2)),
            pltpu.SemaphoreType.DMA((2,)),
        ],
        compiler_params=pltpu.CompilerParams(collective_id=collective_id, has_side_effects=True),
        cost_estimate=pl.CostEstimate(
            flops=0, bytes_accessed=2 * (n_narrow + 1) * x.size * x.dtype.itemsize, transcendentals=0
        ),
    )(x)


def _add_into(dst, *srcs):
    rows_all = dst.shape[0]
    step = 128 if rows_all % 128 == 0 else rows_all

    def body(i, carry):
        rows = pl.ds(pl.multiple_of(i * step, step), step)
        total = srcs[0][rows, :].astype(jnp.float32)
        for src in srcs[1:]:
            total = total + src[rows, :].astype(jnp.float32)
        dst[rows, :] = total.astype(dst.dtype)
        return carry

    lax.fori_loop(0, rows_all // step, body, 0)


def _reduce_kernel(p_ref, o_ref, rp, rm, sp, sm, qy, ry, sem_p, sem_m, sem_y):
    me = lax.axis_index("narrow")
    w = lax.axis_index("wide")
    yh = me // 4
    xi = me % 4
    other = 1 - yh
    partner = other * 4 + xi
    right = yh * 4 + (xi + 1) % 4
    left = yh * 4 + (xi + 3) % 4
    barrier = pltpu.get_barrier_semaphore()
    for peer in (partner, right, left):
        pl.semaphore_signal(barrier, inc=1, device_id=(w, peer), device_id_type=MESH)
    pl.semaphore_wait(barrier, 3)

    def remote(src, dst, sem, peer):
        return pltpu.make_async_remote_copy(
            src_ref=src,
            dst_ref=dst,
            send_sem=sem.at[0],
            recv_sem=sem.at[1],
            device_id=(w, peer),
            device_id_type=MESH,
        )

    mine = lambda h, k: p_ref.at[h * 4 + (xi + k) % 4]
    sends = []
    c = remote(mine(other, 3), rp.at[0], sem_p.at[0], right)
    c.start()
    sends.append(c)
    c = remote(mine(yh, 1), rm.at[0], sem_m.at[0], left)
    c.start()
    sends.append(c)
    for step, (kp, km) in enumerate(((2, 2), (1, 3))):
        remote(sp.at[step], rp.at[step], sem_p.at[step], left).wait_recv()
        _add_into(sp.at[step], rp.at[step], mine(other, kp))
        c = remote(sp.at[step], rp.at[step + 1], sem_p.at[step + 1], right)
        c.start()
        sends.append(c)
        remote(sm.at[step], rm.at[step], sem_m.at[step], right).wait_recv()
        _add_into(sm.at[step], rm.at[step], mine(yh, km))
        c = remote(sm.at[step], rm.at[step + 1], sem_m.at[step + 1], left)
        c.start()
        sends.append(c)
    remote(qy, rp.at[2], sem_p.at[2], left).wait_recv()
    _add_into(qy, rp.at[2], mine(other, 0))
    c = remote(qy, ry, sem_y, partner)
    c.start()
    sends.append(c)
    remote(sm.at[1], rm.at[2], sem_m.at[2], right).wait_recv()
    remote(qy, ry, sem_y, partner).wait_recv()
    _add_into(o_ref, rm.at[2], mine(yh, 0), ry)
    for c in sends:
        c.wait_send()


def _reduce(p, collective_id):
    n_peers, rows, cols = p.shape
    block = pltpu.VMEM((rows, cols), p.dtype)
    return pl.pallas_call(
        _reduce_kernel,
        out_shape=jax.ShapeDtypeStruct((rows, cols), p.dtype),
        in_specs=[pl.BlockSpec(memory_space=pltpu.VMEM)],
        out_specs=pl.BlockSpec(memory_space=pltpu.VMEM),
        scratch_shapes=[
            pltpu.VMEM((3, rows, cols), p.dtype),
            pltpu.VMEM((3, rows, cols), p.dtype),
            pltpu.VMEM((2, rows, cols), p.dtype),
            pltpu.VMEM((2, rows, cols), p.dtype),
            block,
            block,
            pltpu.SemaphoreType.DMA((3, 2)),
            pltpu.SemaphoreType.DMA((3, 2)),
            pltpu.SemaphoreType.DMA((2,)),
        ],
        compiler_params=pltpu.CompilerParams(collective_id=collective_id, has_side_effects=True),
        cost_estimate=pl.CostEstimate(
            flops=2 * p.size, bytes_accessed=2 * p.size * p.dtype.itemsize, transcendentals=0
        ),
    )(p)


def _exchange(x, n_peers, gather, collective_id, axis="narrow"):
    if gather:
        out_shape = (n_peers,) + x.shape
        pick_src = lambda ref, i: ref
    else:
        out_shape = x.shape
        pick_src = lambda ref, i: ref.at[i]
    nbytes = x.size * x.dtype.itemsize
    return pl.pallas_call(
        lambda *refs: _exchange_kernel(n_peers, pick_src, axis, *refs),
        out_shape=jax.ShapeDtypeStruct(out_shape, x.dtype),
        in_specs=[pl.BlockSpec(memory_space=pl.ANY)],
        out_specs=pl.BlockSpec(memory_space=pl.ANY),
        scratch_shapes=[
            pltpu.SemaphoreType.DMA((n_peers - 1,)),
            pltpu.SemaphoreType.DMA((n_peers - 1,)),
            pltpu.SemaphoreType.DMA(()),
        ],
        compiler_params=pltpu.CompilerParams(collective_id=collective_id, has_side_effects=True),
        cost_estimate=pl.CostEstimate(flops=0, bytes_accessed=2 * nbytes, transcendentals=0),
    )(x)


def local(tokens, expert_ids, route_weights, w_gate, w_up, w_down):
    tok_rows = expert_ids.shape[0]
    top_count = expert_ids.shape[1]
    local_experts = w_gate.shape[0]
    groups_wide = lax.axis_size("wide")
    experts_all = local_experts * groups_wide
    capacity = 7 * tok_rows * top_count // (6 * experts_all)
    slots_all = experts_all * capacity
    flat_ids = expert_ids.reshape(-1)
    onehot = (flat_ids[:, None] == jnp.arange(experts_all, dtype=jnp.int32)[None, :]).astype(
        jnp.int32
    )
    running = jnp.cumsum(onehot, axis=0)
    slot_index = jnp.sum(running * onehot, axis=1) - 1
    destination = (flat_ids * capacity + slot_index).reshape(tok_rows, top_count)
    hit = destination[:, :, None] == jnp.arange(slots_all, dtype=jnp.int32)[None, None, :]
    dispatch = jnp.any(hit, axis=1).astype(jnp.bfloat16)
    combine = jnp.sum(
        jnp.where(hit, route_weights.astype(jnp.float32)[:, :, None], 0.0), axis=1
    ).astype(jnp.bfloat16)
    outgoing = jnp.einsum("ts,td->sd", dispatch, tokens, preferred_element_type=jnp.float32).astype(
        jnp.bfloat16
    )
    gathered = _dispatch(outgoing.reshape(groups_wide, capacity, -1), lax.axis_size("narrow"), 0)
    n_narrow = lax.axis_size("narrow")
    width = tokens.shape[1]
    slot_rows = gathered.reshape(n_narrow, slots_all, width)
    wg = w_gate[0].reshape(-1, n_narrow, width)
    wu = w_up[0].reshape(-1, n_narrow, width)
    wd = w_down[0].reshape(-1, n_narrow, width)
    gate_proj = jnp.einsum("nsd,fnd->sf", slot_rows, wg, preferred_element_type=jnp.float32)
    up_proj = jnp.einsum("nsd,fnd->sf", slot_rows, wu, preferred_element_type=jnp.float32)
    hidden = (jax.nn.silu(gate_proj) * up_proj).astype(jnp.bfloat16)
    partial_value = jnp.einsum(
        "sf,fnd->nsd", hidden, wd, preferred_element_type=jnp.float32
    ).astype(jnp.bfloat16)
    summed = _reduce(partial_value, 1)
    returned = _exchange(summed.reshape(groups_wide, capacity, -1), groups_wide, False, 3, "wide")
    returned = returned.reshape(slots_all, -1)
    mixed = jnp.einsum("ts,sd->td", combine, returned, preferred_element_type=jnp.float32)
    return mixed.astype(jnp.bfloat16)


def solution(mesh):
    in_specs = (
        P("wide", "narrow"),
        P("wide", None),
        P("wide", None),
        P("wide", "narrow", None),
        P("wide", "narrow", None),
        P("wide", "narrow", None),
    )
    out_specs = P("wide", "narrow")
    return jax.shard_map(local, mesh=mesh, in_specs=in_specs, out_specs=out_specs, check_vma=False)
```

```python
import types

import jax
import jax.numpy as jnp
from jax import lax
from jax.experimental import pallas as pl
from jax.experimental.pallas import tpu as pltpu
from jax.sharding import PartitionSpec as P

MESH = pl.DeviceIdType.MESH


def _exchange_kernel(n_peers, pick_src, axis, x_ref, y_ref, send_sem, recv_sem, own_sem):
    me = lax.axis_index(axis)
    other = lax.axis_index("wide" if axis == "narrow" else "narrow")
    if axis == "narrow":
        dev = lambda p: (other, p)
    else:
        dev = lambda p: (p, other)
    barrier = pltpu.get_barrier_semaphore()
    for k in range(1, n_peers):
        peer = lax.rem(me + k, n_peers)
        pl.semaphore_signal(barrier, inc=1, device_id=dev(peer), device_id_type=MESH)
    pl.semaphore_wait(barrier, n_peers - 1)
    own = pltpu.make_async_copy(pick_src(x_ref, me), y_ref.at[me], own_sem)
    own.start()
    copies = []
    for k in range(1, n_peers):
        peer = lax.rem(me + k, n_peers)
        c = pltpu.make_async_remote_copy(
            src_ref=pick_src(x_ref, peer),
            dst_ref=y_ref.at[me],
            send_sem=send_sem.at[k - 1],
            recv_sem=recv_sem.at[k - 1],
            device_id=dev(peer),
            device_id_type=MESH,
        )
        c.start()
        copies.append(c)
    for k in range(1, n_peers):
        src = lax.rem(me + n_peers - k, n_peers)
        pltpu.make_async_remote_copy(
            src_ref=pick_src(x_ref, src),
            dst_ref=y_ref.at[src],
            send_sem=send_sem.at[k - 1],
            recv_sem=recv_sem.at[k - 1],
            device_id=dev(src),
            device_id_type=MESH,
        ).wait_recv()
    for c in copies:
        c.wait_send()
    own.wait()


def _gather_chain(x_ref, slot_of, sem_y, sem_x1, sem_x2, own_sem):
    me = lax.axis_index("narrow")
    w = lax.axis_index("wide")
    yh = me // 4
    xi = me % 4
    partner = (1 - yh) * 4 + xi
    right = yh * 4 + (xi + 1) % 4
    left = yh * 4 + (xi + 3) % 4

    y_ref = types.SimpleNamespace(at=_Slots(slot_of))

    def remote(src, slot, sem, peer):
        return pltpu.make_async_remote_copy(
            src_ref=src,
            dst_ref=y_ref.at[slot],
            send_sem=sem[0],
            recv_sem=sem[1],
            device_id=(w, peer),
            device_id_type=MESH,
        )

    own = pltpu.make_async_copy(x_ref, y_ref.at[me], own_sem)
    own.start()
    cy = remote(x_ref, me, (sem_y.at[0], sem_y.at[1]), partner)
    cy.start()
    c1 = [
        remote(x_ref, me, (sem_x1.at[0, 0], sem_x1.at[0, 1]), right),
        remote(x_ref, me, (sem_x1.at[1, 0], sem_x1.at[1, 1]), left),
    ]
    for c in c1:
        c.start()
    remote(x_ref, partner, (sem_y.at[0], sem_y.at[1]), partner).wait_recv()
    c2 = [
        remote(y_ref.at[partner], partner, (sem_x1.at[2, 0], sem_x1.at[2, 1]), right),
        remote(y_ref.at[partner], partner, (sem_x1.at[3, 0], sem_x1.at[3, 1]), left),
    ]
    for c in c2:
        c.start()
    lp = (1 - yh) * 4 + (xi + 3) % 4
    rp = (1 - yh) * 4 + (xi + 1) % 4
    remote(x_ref, left, (sem_x1.at[0, 0], sem_x1.at[0, 1]), left).wait_recv()
    remote(x_ref, right, (sem_x1.at[1, 0], sem_x1.at[1, 1]), right).wait_recv()
    c3 = [
        remote(y_ref.at[left], left, (sem_x2.at[0, 0], sem_x2.at[0, 1]), right),
    ]
    c3[0].start()
    remote(x_ref, rp, (sem_x1.at[3, 0], sem_x1.at[3, 1]), right).wait_recv()
    c4 = remote(y_ref.at[rp], rp, (sem_x2.at[1, 0], sem_x2.at[1, 1]), left)
    c4.start()
    remote(x_ref, lp, (sem_x1.at[2, 0], sem_x1.at[2, 1]), left).wait_recv()
    far = yh * 4 + (xi + 2) % 4
    far_p = (1 - yh) * 4 + (xi + 2) % 4
    remote(x_ref, far, (sem_x2.at[0, 0], sem_x2.at[0, 1]), left).wait_recv()
    remote(x_ref, far_p, (sem_x2.at[1, 0], sem_x2.at[1, 1]), right).wait_recv()
    return [cy] + c1 + c2 + c3 + [c4], own


class _Slots:
    def __init__(self, fn):
        self.fn = fn

    def __getitem__(self, k):
        return self.fn(k)


def _narrow_peers():
    me = lax.axis_index("narrow")
    yh = me // 4
    xi = me % 4
    return ((1 - yh) * 4 + xi, yh * 4 + (xi + 1) % 4, yh * 4 + (xi + 3) % 4)


def _dispatch_kernel(x_ref, y_ref, r_ref, sem_w, own_w, sem_y, sem_x1, sem_x2, own_g):
    nw, _, cols = x_ref.shape
    halves = 2
    cw = cols // halves
    me_w = lax.axis_index("wide")
    me = lax.axis_index("narrow")
    barrier = pltpu.get_barrier_semaphore()

    def greet(k, carry):
        pl.semaphore_signal(barrier, inc=1, device_id=((me_w + k) % nw, me), device_id_type=MESH)
        return carry

    lax.fori_loop(1, nw, greet, 0)
    for peer in _narrow_peers():
        pl.semaphore_signal(barrier, inc=1, device_id=(me_w, peer), device_id_type=MESH)
    pl.semaphore_wait(barrier, nw - 1 + 3)

    def wide_copy(h, k, peer_of_copy, target):
        cs = pl.ds(h * cw, cw)
        return pltpu.make_async_remote_copy(
            src_ref=x_ref.at[peer_of_copy, :, cs],
            dst_ref=r_ref.at[target, :, cs],
            send_sem=sem_w.at[h, k, 0],
            recv_sem=sem_w.at[h, k, 1],
            device_id=(peer_of_copy, me),
            device_id_type=MESH,
        )

    def wide_start(h):
        cs = pl.ds(h * cw, cw)
        own = pltpu.make_async_copy(x_ref.at[me_w, :, cs], r_ref.at[me_w, :, cs], own_w.at[h])
        own.start()

        def body(k, carry):
            wide_copy(h, k, (me_w + k) % nw, me_w).start()
            return carry

        lax.fori_loop(1, nw, body, 0)
        return own

    def wide_wait(h, own):
        def body(k, carry):
            src = (me_w + nw - k) % nw
            pltpu.make_async_remote_copy(
                src_ref=x_ref.at[src, :, pl.ds(h * cw, cw)],
                dst_ref=r_ref.at[src, :, pl.ds(h * cw, cw)],
                send_sem=sem_w.at[h, k, 0],
                recv_sem=sem_w.at[h, k, 1],
                device_id=(src, me),
                device_id_type=MESH,
            ).wait_recv()
            return carry

        lax.fori_loop(1, nw, body, 0)
        own.wait()

    def wide_sent(h):
        def body(k, carry):
            wide_copy(h, k, (me_w + k) % nw, me_w).wait_send()
            return carry

        lax.fori_loop(1, nw, body, 0)

    pending = []
    own0 = wide_start(0)
    wide_wait(0, own0)
    own1 = wide_start(1)
    for h in range(halves):
        if h == 1:
            wide_wait(1, own1)
        cs = pl.ds(h * cw, cw)
        sends, own = _gather_chain(
            r_ref.at[:, :, cs],
            lambda k, cs=cs: y_ref.at[k, :, :, cs],
            sem_y.at[h],
            sem_x1.at[h],
            sem_x2.at[h],
            own_g.at[h],
        )
        pending.append((sends, own))
    for h in range(halves):
        wide_sent(h)
        sends, own = pending[h]
        for c in sends:
            c.wait_send()
        own.wait()


def _dispatch(x, n_narrow, collective_id):
    nw, rows, cols = x.shape
    return pl.pallas_call(
        _dispatch_kernel,
        out_shape=jax.ShapeDtypeStruct((n_narrow, nw, rows, cols), x.dtype),
        in_specs=[pl.BlockSpec(memory_space=pl.ANY)],
        out_specs=pl.BlockSpec(memory_space=pl.ANY),
        scratch_shapes=[
            pltpu.VMEM((nw, rows, cols), x.dtype),
            pltpu.SemaphoreType.DMA((2, nw, 2)),
            pltpu.SemaphoreType.DMA((2,)),
            pltpu.SemaphoreType.DMA((2, 2)),
            pltpu.SemaphoreType.DMA((2, 4, 2)),
            pltpu.SemaphoreType.DMA((2, 2, 2)),
            pltpu.SemaphoreType.DMA((2,)),
        ],
        compiler_params=pltpu.CompilerParams(collective_id=collective_id, has_side_effects=True),
        cost_estimate=pl.CostEstimate(
            flops=0, bytes_accessed=2 * (n_narrow + 1) * x.size * x.dtype.itemsize, transcendentals=0
        ),
    )(x)


def _add_into(dst, *srcs):
    rows_all = dst.shape[0]
    step = 128 if rows_all % 128 == 0 else rows_all

    def body(i, carry):
        rows = pl.ds(pl.multiple_of(i * step, step), step)
        total = srcs[0][rows].astype(jnp.float32)
        for src in srcs[1:]:
            total = total + src[rows].astype(jnp.float32)
        dst[rows] = total.astype(dst.dtype)
        return carry

    lax.fori_loop(0, rows_all // step, body, 0)


def _reduce_kernel(p_ref, o_ref, rp, rm, sp, sm, qy, ry, sem_p, sem_m, sem_y):
    me = lax.axis_index("narrow")
    w = lax.axis_index("wide")
    yh = me // 4
    xi = me % 4
    other = 1 - yh
    partner = other * 4 + xi
    right = yh * 4 + (xi + 1) % 4
    left = yh * 4 + (xi + 3) % 4
    barrier = pltpu.get_barrier_semaphore()
    for peer in (partner, right, left):
        pl.semaphore_signal(barrier, inc=1, device_id=(w, peer), device_id_type=MESH)
    pl.semaphore_wait(barrier, 3)

    def remote(src, dst, sem, peer):
        return pltpu.make_async_remote_copy(
            src_ref=src,
            dst_ref=dst,
            send_sem=sem.at[0],
            recv_sem=sem.at[1],
            device_id=(w, peer),
            device_id_type=MESH,
        )

    mine = lambda h, k: p_ref.at[h * 4 + (xi + k) % 4]
    sends = []
    c = remote(mine(other, 3), rp.at[0], sem_p.at[0], right)
    c.start()
    sends.append(c)
    c = remote(mine(yh, 1), rm.at[0], sem_m.at[0], left)
    c.start()
    sends.append(c)
    for step, (kp, km) in enumerate(((2, 2), (1, 3))):
        remote(sp.at[step], rp.at[step], sem_p.at[step], left).wait_recv()
        _add_into(sp.at[step], rp.at[step], mine(other, kp))
        c = remote(sp.at[step], rp.at[step + 1], sem_p.at[step + 1], right)
        c.start()
        sends.append(c)
        remote(sm.at[step], rm.at[step], sem_m.at[step], right).wait_recv()
        _add_into(sm.at[step], rm.at[step], mine(yh, km))
        c = remote(sm.at[step], rm.at[step + 1], sem_m.at[step + 1], left)
        c.start()
        sends.append(c)
    remote(qy, rp.at[2], sem_p.at[2], left).wait_recv()
    _add_into(qy, rp.at[2], mine(other, 0))
    c = remote(qy, ry, sem_y, partner)
    c.start()
    sends.append(c)
    remote(sm.at[1], rm.at[2], sem_m.at[2], right).wait_recv()
    remote(qy, ry, sem_y, partner).wait_recv()
    _add_into(o_ref, rm.at[2], mine(yh, 0), ry)
    for c in sends:
        c.wait_send()


def _reduce(p, collective_id):
    one = p.shape[1:]
    block = pltpu.VMEM(one, p.dtype)
    return pl.pallas_call(
        _reduce_kernel,
        out_shape=jax.ShapeDtypeStruct(one, p.dtype),
        in_specs=[pl.BlockSpec(memory_space=pltpu.VMEM)],
        out_specs=pl.BlockSpec(memory_space=pltpu.VMEM),
        scratch_shapes=[
            pltpu.VMEM((3,) + one, p.dtype),
            pltpu.VMEM((3,) + one, p.dtype),
            pltpu.VMEM((2,) + one, p.dtype),
            pltpu.VMEM((2,) + one, p.dtype),
            block,
            block,
            pltpu.SemaphoreType.DMA((3, 2)),
            pltpu.SemaphoreType.DMA((3, 2)),
            pltpu.SemaphoreType.DMA((2,)),
        ],
        compiler_params=pltpu.CompilerParams(collective_id=collective_id, has_side_effects=True),
        cost_estimate=pl.CostEstimate(
            flops=2 * p.size, bytes_accessed=2 * p.size * p.dtype.itemsize, transcendentals=0
        ),
    )(p)


def _exchange(x, n_peers, gather, collective_id, axis="narrow"):
    if gather:
        out_shape = (n_peers,) + x.shape
        pick_src = lambda ref, i: ref
    else:
        out_shape = x.shape
        pick_src = lambda ref, i: ref.at[i]
    nbytes = x.size * x.dtype.itemsize
    return pl.pallas_call(
        lambda *refs: _exchange_kernel(n_peers, pick_src, axis, *refs),
        out_shape=jax.ShapeDtypeStruct(out_shape, x.dtype),
        in_specs=[pl.BlockSpec(memory_space=pl.ANY)],
        out_specs=pl.BlockSpec(memory_space=pl.ANY),
        scratch_shapes=[
            pltpu.SemaphoreType.DMA((n_peers - 1,)),
            pltpu.SemaphoreType.DMA((n_peers - 1,)),
            pltpu.SemaphoreType.DMA(()),
        ],
        compiler_params=pltpu.CompilerParams(collective_id=collective_id, has_side_effects=True),
        cost_estimate=pl.CostEstimate(flops=0, bytes_accessed=2 * nbytes, transcendentals=0),
    )(x)


def local(tokens, expert_ids, route_weights, w_gate, w_up, w_down):
    tok_rows = expert_ids.shape[0]
    top_count = expert_ids.shape[1]
    local_experts = w_gate.shape[0]
    groups_wide = lax.axis_size("wide")
    experts_all = local_experts * groups_wide
    capacity = 7 * tok_rows * top_count // (6 * experts_all)
    slots_all = experts_all * capacity
    flat_ids = expert_ids.reshape(-1)
    onehot = (flat_ids[:, None] == jnp.arange(experts_all, dtype=jnp.int32)[None, :]).astype(
        jnp.int32
    )
    running = jnp.cumsum(onehot, axis=0)
    slot_index = jnp.sum(running * onehot, axis=1) - 1
    destination = (flat_ids * capacity + slot_index).reshape(tok_rows, top_count)
    hit = destination[:, :, None] == jnp.arange(slots_all, dtype=jnp.int32)[None, None, :]
    dispatch = jnp.any(hit, axis=1).astype(jnp.bfloat16)
    combine = jnp.sum(
        jnp.where(hit, route_weights.astype(jnp.float32)[:, :, None], 0.0), axis=1
    ).astype(jnp.bfloat16)
    dispatch = dispatch.reshape(tok_rows, groups_wide, capacity)
    combine = combine.reshape(tok_rows, groups_wide, capacity)
    outgoing = jnp.einsum(
        "tbc,td->bcd", dispatch, tokens, preferred_element_type=jnp.float32
    ).astype(jnp.bfloat16)
    n_narrow = lax.axis_size("narrow")
    width = tokens.shape[1]
    slot_rows = _dispatch(outgoing, n_narrow, 0)
    wg = w_gate[0].reshape(-1, n_narrow, width)
    wu = w_up[0].reshape(-1, n_narrow, width)
    wd = w_down[0].reshape(-1, n_narrow, width)
    gate_proj = jnp.einsum("nbcd,fnd->bcf", slot_rows, wg, preferred_element_type=jnp.float32)
    up_proj = jnp.einsum("nbcd,fnd->bcf", slot_rows, wu, preferred_element_type=jnp.float32)
    hidden = (jax.nn.silu(gate_proj) * up_proj).astype(jnp.bfloat16)
    partial_value = jnp.einsum(
        "sf,fnd->nsd", hidden.reshape(slots_all, -1), wd, preferred_element_type=jnp.float32
    ).astype(jnp.bfloat16)
    summed = _reduce(partial_value, 1)
    returned = _exchange(summed.reshape(groups_wide, capacity, -1), groups_wide, False, 3, "wide")
    mixed = jnp.einsum("tbc,bcd->td", combine, returned, preferred_element_type=jnp.float32)
    return mixed.astype(jnp.bfloat16)


def solution(mesh):
    in_specs = (
        P("wide", "narrow"),
        P("wide", None),
        P("wide", None),
        P("wide", "narrow", None),
        P("wide", "narrow", None),
        P("wide", "narrow", None),
    )
    out_specs = P("wide", "narrow")
    return jax.shard_map(local, mesh=mesh, in_specs=in_specs, out_specs=out_specs, check_vma=False)
```

```python
import types

import jax
import jax.numpy as jnp
from jax import lax
from jax.experimental import pallas as pl
from jax.experimental.pallas import tpu as pltpu
from jax.sharding import PartitionSpec as P

MESH = pl.DeviceIdType.MESH


def _exchange_kernel(n_peers, pick_src, axis, x_ref, y_ref, send_sem, recv_sem, own_sem):
    me = lax.axis_index(axis)
    other = lax.axis_index("wide" if axis == "narrow" else "narrow")
    if axis == "narrow":
        dev = lambda p: (other, p)
    else:
        dev = lambda p: (p, other)
    barrier = pltpu.get_barrier_semaphore()
    for k in range(1, n_peers):
        peer = lax.rem(me + k, n_peers)
        pl.semaphore_signal(barrier, inc=1, device_id=dev(peer), device_id_type=MESH)
    pl.semaphore_wait(barrier, n_peers - 1)
    own = pltpu.make_async_copy(pick_src(x_ref, me), y_ref.at[me], own_sem)
    own.start()
    copies = []
    for k in range(1, n_peers):
        peer = lax.rem(me + k, n_peers)
        c = pltpu.make_async_remote_copy(
            src_ref=pick_src(x_ref, peer),
            dst_ref=y_ref.at[me],
            send_sem=send_sem.at[k - 1],
            recv_sem=recv_sem.at[k - 1],
            device_id=dev(peer),
            device_id_type=MESH,
        )
        c.start()
        copies.append(c)
    for k in range(1, n_peers):
        src = lax.rem(me + n_peers - k, n_peers)
        pltpu.make_async_remote_copy(
            src_ref=pick_src(x_ref, src),
            dst_ref=y_ref.at[src],
            send_sem=send_sem.at[k - 1],
            recv_sem=recv_sem.at[k - 1],
            device_id=dev(src),
            device_id_type=MESH,
        ).wait_recv()
    for c in copies:
        c.wait_send()
    own.wait()


def _gather_chain(x_ref, slot_of, sem_y, sem_x1, sem_x2, own_sem):
    me = lax.axis_index("narrow")
    w = lax.axis_index("wide")
    yh = me // 4
    xi = me % 4
    partner = (1 - yh) * 4 + xi
    right = yh * 4 + (xi + 1) % 4
    left = yh * 4 + (xi + 3) % 4

    y_ref = types.SimpleNamespace(at=_Slots(slot_of))

    def remote(src, slot, sem, peer):
        return pltpu.make_async_remote_copy(
            src_ref=src,
            dst_ref=y_ref.at[slot],
            send_sem=sem[0],
            recv_sem=sem[1],
            device_id=(w, peer),
            device_id_type=MESH,
        )

    own = pltpu.make_async_copy(x_ref, y_ref.at[me], own_sem)
    own.start()
    cy = remote(x_ref, me, (sem_y.at[0], sem_y.at[1]), partner)
    cy.start()
    c1 = [
        remote(x_ref, me, (sem_x1.at[0, 0], sem_x1.at[0, 1]), right),
        remote(x_ref, me, (sem_x1.at[1, 0], sem_x1.at[1, 1]), left),
    ]
    for c in c1:
        c.start()
    remote(x_ref, partner, (sem_y.at[0], sem_y.at[1]), partner).wait_recv()
    c2 = [
        remote(y_ref.at[partner], partner, (sem_x1.at[2, 0], sem_x1.at[2, 1]), right),
        remote(y_ref.at[partner], partner, (sem_x1.at[3, 0], sem_x1.at[3, 1]), left),
    ]
    for c in c2:
        c.start()
    lp = (1 - yh) * 4 + (xi + 3) % 4
    rp = (1 - yh) * 4 + (xi + 1) % 4
    remote(x_ref, left, (sem_x1.at[0, 0], sem_x1.at[0, 1]), left).wait_recv()
    remote(x_ref, right, (sem_x1.at[1, 0], sem_x1.at[1, 1]), right).wait_recv()
    c3 = [
        remote(y_ref.at[left], left, (sem_x2.at[0, 0], sem_x2.at[0, 1]), right),
    ]
    c3[0].start()
    remote(x_ref, rp, (sem_x1.at[3, 0], sem_x1.at[3, 1]), right).wait_recv()
    c4 = remote(y_ref.at[rp], rp, (sem_x2.at[1, 0], sem_x2.at[1, 1]), left)
    c4.start()
    remote(x_ref, lp, (sem_x1.at[2, 0], sem_x1.at[2, 1]), left).wait_recv()
    far = yh * 4 + (xi + 2) % 4
    far_p = (1 - yh) * 4 + (xi + 2) % 4
    remote(x_ref, far, (sem_x2.at[0, 0], sem_x2.at[0, 1]), left).wait_recv()
    remote(x_ref, far_p, (sem_x2.at[1, 0], sem_x2.at[1, 1]), right).wait_recv()
    return [cy] + c1 + c2 + c3 + [c4], own


class _Slots:
    def __init__(self, fn):
        self.fn = fn

    def __getitem__(self, k):
        return self.fn(k)


def _narrow_peers():
    me = lax.axis_index("narrow")
    yh = me // 4
    xi = me % 4
    return ((1 - yh) * 4 + xi, yh * 4 + (xi + 1) % 4, yh * 4 + (xi + 3) % 4)


def _dispatch_kernel(x_ref, y_ref, r_ref, sem_w, own_w, sem_y, sem_x1, sem_x2, own_g):
    nw, _, cols = x_ref.shape
    halves = 2
    cw = cols // halves
    me_w = lax.axis_index("wide")
    me = lax.axis_index("narrow")
    barrier = pltpu.get_barrier_semaphore()

    def greet(k, carry):
        pl.semaphore_signal(barrier, inc=1, device_id=((me_w + k) % nw, me), device_id_type=MESH)
        return carry

    lax.fori_loop(1, nw, greet, 0)
    for peer in _narrow_peers():
        pl.semaphore_signal(barrier, inc=1, device_id=(me_w, peer), device_id_type=MESH)
    pl.semaphore_wait(barrier, nw - 1 + 3)

    def wide_copy(h, k, peer_of_copy, target):
        cs = pl.ds(h * cw, cw)
        return pltpu.make_async_remote_copy(
            src_ref=x_ref.at[peer_of_copy, :, cs],
            dst_ref=r_ref.at[target, :, cs],
            send_sem=sem_w.at[h, k, 0],
            recv_sem=sem_w.at[h, k, 1],
            device_id=(peer_of_copy, me),
            device_id_type=MESH,
        )

    def wide_start(h):
        cs = pl.ds(h * cw, cw)
        own = pltpu.make_async_copy(x_ref.at[me_w, :, cs], r_ref.at[me_w, :, cs], own_w.at[h])
        own.start()

        def body(k, carry):
            wide_copy(h, k, (me_w + k) % nw, me_w).start()
            return carry

        lax.fori_loop(1, nw, body, 0)
        return own

    def wide_wait(h, own):
        def body(k, carry):
            src = (me_w + nw - k) % nw
            pltpu.make_async_remote_copy(
                src_ref=x_ref.at[src, :, pl.ds(h * cw, cw)],
                dst_ref=r_ref.at[src, :, pl.ds(h * cw, cw)],
                send_sem=sem_w.at[h, k, 0],
                recv_sem=sem_w.at[h, k, 1],
                device_id=(src, me),
                device_id_type=MESH,
            ).wait_recv()
            return carry

        lax.fori_loop(1, nw, body, 0)
        own.wait()

    def wide_sent(h):
        def body(k, carry):
            wide_copy(h, k, (me_w + k) % nw, me_w).wait_send()
            return carry

        lax.fori_loop(1, nw, body, 0)

    pending = []
    own0 = wide_start(0)
    wide_wait(0, own0)
    own1 = wide_start(1)
    for h in range(halves):
        if h == 1:
            wide_wait(1, own1)
        cs = pl.ds(h * cw, cw)
        sends, own = _gather_chain(
            r_ref.at[:, :, cs],
            lambda k, cs=cs: y_ref.at[k, :, :, cs],
            sem_y.at[h],
            sem_x1.at[h],
            sem_x2.at[h],
            own_g.at[h],
        )
        pending.append((sends, own))
    for h in range(halves):
        wide_sent(h)
        sends, own = pending[h]
        for c in sends:
            c.wait_send()
        own.wait()


def _dispatch(x, n_narrow, collective_id):
    nw, rows, cols = x.shape
    return pl.pallas_call(
        _dispatch_kernel,
        out_shape=jax.ShapeDtypeStruct((n_narrow, nw, rows, cols), x.dtype),
        in_specs=[pl.BlockSpec(memory_space=pl.ANY)],
        out_specs=pl.BlockSpec(memory_space=pl.ANY),
        scratch_shapes=[
            pltpu.VMEM((nw, rows, cols), x.dtype),
            pltpu.SemaphoreType.DMA((2, nw, 2)),
            pltpu.SemaphoreType.DMA((2,)),
            pltpu.SemaphoreType.DMA((2, 2)),
            pltpu.SemaphoreType.DMA((2, 4, 2)),
            pltpu.SemaphoreType.DMA((2, 2, 2)),
            pltpu.SemaphoreType.DMA((2,)),
        ],
        compiler_params=pltpu.CompilerParams(collective_id=collective_id, has_side_effects=True),
        cost_estimate=pl.CostEstimate(
            flops=0, bytes_accessed=2 * (n_narrow + 1) * x.size * x.dtype.itemsize, transcendentals=0
        ),
    )(x)


def _add_into(dst, *srcs):
    rows_all = dst.shape[0]
    step = 128 if rows_all % 128 == 0 else rows_all

    def body(i, carry):
        rows = pl.ds(pl.multiple_of(i * step, step), step)
        total = srcs[0][rows].astype(jnp.float32)
        for src in srcs[1:]:
            total = total + src[rows].astype(jnp.float32)
        dst[rows] = total.astype(dst.dtype)
        return carry

    lax.fori_loop(0, rows_all // step, body, 0)


def _reduce_kernel(p_ref, r_ref, rp, rm, sp, sm, qy, ry, o_ref, sem_p, sem_m, sem_y, sem_w, own_w):
    me = lax.axis_index("narrow")
    w = lax.axis_index("wide")
    yh = me // 4
    xi = me % 4
    other = 1 - yh
    partner = other * 4 + xi
    right = yh * 4 + (xi + 1) % 4
    left = yh * 4 + (xi + 3) % 4
    nw = r_ref.shape[0]
    barrier = pltpu.get_barrier_semaphore()
    for peer in (partner, right, left):
        pl.semaphore_signal(barrier, inc=1, device_id=(w, peer), device_id_type=MESH)

    def greet(k, carry):
        pl.semaphore_signal(barrier, inc=1, device_id=((w + k) % nw, me), device_id_type=MESH)
        return carry

    lax.fori_loop(1, nw, greet, 0)
    pl.semaphore_wait(barrier, 3 + nw - 1)

    def remote(src, dst, sem, peer):
        return pltpu.make_async_remote_copy(
            src_ref=src,
            dst_ref=dst,
            send_sem=sem.at[0],
            recv_sem=sem.at[1],
            device_id=(w, peer),
            device_id_type=MESH,
        )

    mine = lambda h, k: p_ref.at[h * 4 + (xi + k) % 4]
    sends = []
    c = remote(mine(other, 3), rp.at[0], sem_p.at[0], right)
    c.start()
    sends.append(c)
    c = remote(mine(yh, 1), rm.at[0], sem_m.at[0], left)
    c.start()
    sends.append(c)
    for step, (kp, km) in enumerate(((2, 2), (1, 3))):
        remote(sp.at[step], rp.at[step], sem_p.at[step], left).wait_recv()
        _add_into(sp.at[step], rp.at[step], mine(other, kp))
        c = remote(sp.at[step], rp.at[step + 1], sem_p.at[step + 1], right)
        c.start()
        sends.append(c)
        remote(sm.at[step], rm.at[step], sem_m.at[step], right).wait_recv()
        _add_into(sm.at[step], rm.at[step], mine(yh, km))
        c = remote(sm.at[step], rm.at[step + 1], sem_m.at[step + 1], left)
        c.start()
        sends.append(c)
    remote(qy, rp.at[2], sem_p.at[2], left).wait_recv()
    _add_into(qy, rp.at[2], mine(other, 0))
    c = remote(qy, ry, sem_y, partner)
    c.start()
    sends.append(c)
    remote(sm.at[1], rm.at[2], sem_m.at[2], right).wait_recv()
    remote(qy, ry, sem_y, partner).wait_recv()
    own_p = mine(yh, 0)
    cap = o_ref.shape[1]
    for b in range(nw):
        rows = pl.ds(b * cap, cap)
        total = rm[2, rows].astype(jnp.float32) + own_p[rows].astype(jnp.float32)
        o_ref[b] = (total + ry[rows].astype(jnp.float32)).astype(o_ref.dtype)
    own = pltpu.make_async_copy(o_ref.at[w], r_ref.at[w], own_w)
    own.start()

    def wide_copy(k, peer, origin):
        return pltpu.make_async_remote_copy(
            src_ref=o_ref.at[peer],
            dst_ref=r_ref.at[origin],
            send_sem=sem_w.at[k, 0],
            recv_sem=sem_w.at[k, 1],
            device_id=(peer, me),
            device_id_type=MESH,
        )

    def send_body(k, carry):
        wide_copy(k, (w + k) % nw, w).start()
        return carry

    lax.fori_loop(1, nw, send_body, 0)

    def recv_body(k, carry):
        src = (w + nw - k) % nw
        wide_copy(k, src, src).wait_recv()
        return carry

    lax.fori_loop(1, nw, recv_body, 0)

    def sent_body(k, carry):
        wide_copy(k, (w + k) % nw, w).wait_send()
        return carry

    lax.fori_loop(1, nw, sent_body, 0)
    own.wait()
    for c in sends:
        c.wait_send()


def _reduce(p, nw, collective_id):
    one = p.shape[1:]
    blocks = (nw, one[0] // nw, one[1])
    block = pltpu.VMEM(one, p.dtype)
    return pl.pallas_call(
        _reduce_kernel,
        out_shape=jax.ShapeDtypeStruct(blocks, p.dtype),
        in_specs=[pl.BlockSpec(memory_space=pltpu.VMEM)],
        out_specs=pl.BlockSpec(memory_space=pl.ANY),
        scratch_shapes=[
            pltpu.VMEM((3,) + one, p.dtype),
            pltpu.VMEM((3,) + one, p.dtype),
            pltpu.VMEM((2,) + one, p.dtype),
            pltpu.VMEM((2,) + one, p.dtype),
            block,
            block,
            pltpu.VMEM(blocks, p.dtype),
            pltpu.SemaphoreType.DMA((3, 2)),
            pltpu.SemaphoreType.DMA((3, 2)),
            pltpu.SemaphoreType.DMA((2,)),
            pltpu.SemaphoreType.DMA((nw, 2)),
            pltpu.SemaphoreType.DMA(()),
        ],
        compiler_params=pltpu.CompilerParams(collective_id=collective_id, has_side_effects=True),
        cost_estimate=pl.CostEstimate(
            flops=2 * p.size, bytes_accessed=2 * p.size * p.dtype.itemsize, transcendentals=0
        ),
    )(p)


def _exchange(x, n_peers, gather, collective_id, axis="narrow"):
    if gather:
        out_shape = (n_peers,) + x.shape
        pick_src = lambda ref, i: ref
    else:
        out_shape = x.shape
        pick_src = lambda ref, i: ref.at[i]
    nbytes = x.size * x.dtype.itemsize
    return pl.pallas_call(
        lambda *refs: _exchange_kernel(n_peers, pick_src, axis, *refs),
        out_shape=jax.ShapeDtypeStruct(out_shape, x.dtype),
        in_specs=[pl.BlockSpec(memory_space=pl.ANY)],
        out_specs=pl.BlockSpec(memory_space=pl.ANY),
        scratch_shapes=[
            pltpu.SemaphoreType.DMA((n_peers - 1,)),
            pltpu.SemaphoreType.DMA((n_peers - 1,)),
            pltpu.SemaphoreType.DMA(()),
        ],
        compiler_params=pltpu.CompilerParams(collective_id=collective_id, has_side_effects=True),
        cost_estimate=pl.CostEstimate(flops=0, bytes_accessed=2 * nbytes, transcendentals=0),
    )(x)


def local(tokens, expert_ids, route_weights, w_gate, w_up, w_down):
    tok_rows = expert_ids.shape[0]
    top_count = expert_ids.shape[1]
    local_experts = w_gate.shape[0]
    groups_wide = lax.axis_size("wide")
    experts_all = local_experts * groups_wide
    capacity = 7 * tok_rows * top_count // (6 * experts_all)
    slots_all = experts_all * capacity
    flat_ids = expert_ids.reshape(-1)
    onehot = (flat_ids[:, None] == jnp.arange(experts_all, dtype=jnp.int32)[None, :]).astype(
        jnp.int32
    )
    running = jnp.cumsum(onehot, axis=0)
    slot_index = jnp.sum(running * onehot, axis=1) - 1
    destination = (flat_ids * capacity + slot_index).reshape(tok_rows, top_count)
    hit = destination[:, :, None] == jnp.arange(slots_all, dtype=jnp.int32)[None, None, :]
    dispatch = jnp.any(hit, axis=1).astype(jnp.bfloat16)
    combine = jnp.sum(
        jnp.where(hit, route_weights.astype(jnp.float32)[:, :, None], 0.0), axis=1
    ).astype(jnp.bfloat16)
    dispatch = dispatch.reshape(tok_rows, groups_wide, capacity)
    combine = combine.reshape(tok_rows, groups_wide, capacity)
    outgoing = jnp.einsum(
        "tbc,td->bcd", dispatch, tokens, preferred_element_type=jnp.float32
    ).astype(jnp.bfloat16)
    n_narrow = lax.axis_size("narrow")
    width = tokens.shape[1]
    slot_rows = _dispatch(outgoing, n_narrow, 0)
    wg = w_gate[0].reshape(-1, n_narrow, width)
    wu = w_up[0].reshape(-1, n_narrow, width)
    wd = w_down[0].reshape(-1, n_narrow, width)
    gate_proj = jnp.einsum("nbcd,fnd->bcf", slot_rows, wg, preferred_element_type=jnp.float32)
    up_proj = jnp.einsum("nbcd,fnd->bcf", slot_rows, wu, preferred_element_type=jnp.float32)
    hidden = (jax.nn.silu(gate_proj) * up_proj).astype(jnp.bfloat16)
    partial_value = jnp.einsum(
        "sf,fnd->nsd", hidden.reshape(slots_all, -1), wd, preferred_element_type=jnp.float32
    ).astype(jnp.bfloat16)
    returned = _reduce(partial_value, groups_wide, 1)
    mixed = jnp.einsum("tbc,bcd->td", combine, returned, preferred_element_type=jnp.float32)
    return mixed.astype(jnp.bfloat16)


def solution(mesh):
    in_specs = (
        P("wide", "narrow"),
        P("wide", None),
        P("wide", None),
        P("wide", "narrow", None),
        P("wide", "narrow", None),
        P("wide", "narrow", None),
    )
    out_specs = P("wide", "narrow")
    return jax.shard_map(local, mesh=mesh, in_specs=in_specs, out_specs=out_specs, check_vma=False)
```

```python
import types

import jax
import jax.numpy as jnp
from jax import lax
from jax.experimental import pallas as pl
from jax.experimental.pallas import tpu as pltpu
from jax.sharding import PartitionSpec as P

MESH = pl.DeviceIdType.MESH


def _exchange_kernel(n_peers, pick_src, axis, x_ref, y_ref, send_sem, recv_sem, own_sem):
    me = lax.axis_index(axis)
    other = lax.axis_index("wide" if axis == "narrow" else "narrow")
    if axis == "narrow":
        dev = lambda p: (other, p)
    else:
        dev = lambda p: (p, other)
    barrier = pltpu.get_barrier_semaphore()
    for k in range(1, n_peers):
        peer = lax.rem(me + k, n_peers)
        pl.semaphore_signal(barrier, inc=1, device_id=dev(peer), device_id_type=MESH)
    pl.semaphore_wait(barrier, n_peers - 1)
    own = pltpu.make_async_copy(pick_src(x_ref, me), y_ref.at[me], own_sem)
    own.start()
    copies = []
    for k in range(1, n_peers):
        peer = lax.rem(me + k, n_peers)
        c = pltpu.make_async_remote_copy(
            src_ref=pick_src(x_ref, peer),
            dst_ref=y_ref.at[me],
            send_sem=send_sem.at[k - 1],
            recv_sem=recv_sem.at[k - 1],
            device_id=dev(peer),
            device_id_type=MESH,
        )
        c.start()
        copies.append(c)
    for k in range(1, n_peers):
        src = lax.rem(me + n_peers - k, n_peers)
        pltpu.make_async_remote_copy(
            src_ref=pick_src(x_ref, src),
            dst_ref=y_ref.at[src],
            send_sem=send_sem.at[k - 1],
            recv_sem=recv_sem.at[k - 1],
            device_id=dev(src),
            device_id_type=MESH,
        ).wait_recv()
    for c in copies:
        c.wait_send()
    own.wait()


def _gather_chain(x_ref, slot_of, sem_y, sem_x1, sem_x2, own_sem):
    me = lax.axis_index("narrow")
    w = lax.axis_index("wide")
    yh = me // 4
    xi = me % 4
    partner = (1 - yh) * 4 + xi
    right = yh * 4 + (xi + 1) % 4
    left = yh * 4 + (xi + 3) % 4

    y_ref = types.SimpleNamespace(at=_Slots(slot_of))

    def remote(src, slot, sem, peer):
        return pltpu.make_async_remote_copy(
            src_ref=src,
            dst_ref=y_ref.at[slot],
            send_sem=sem[0],
            recv_sem=sem[1],
            device_id=(w, peer),
            device_id_type=MESH,
        )

    own = pltpu.make_async_copy(x_ref, y_ref.at[me], own_sem)
    own.start()
    cy = remote(x_ref, me, (sem_y.at[0], sem_y.at[1]), partner)
    cy.start()
    c1 = [
        remote(x_ref, me, (sem_x1.at[0, 0], sem_x1.at[0, 1]), right),
        remote(x_ref, me, (sem_x1.at[1, 0], sem_x1.at[1, 1]), left),
    ]
    for c in c1:
        c.start()
    remote(x_ref, partner, (sem_y.at[0], sem_y.at[1]), partner).wait_recv()
    c2 = [
        remote(y_ref.at[partner], partner, (sem_x1.at[2, 0], sem_x1.at[2, 1]), right),
        remote(y_ref.at[partner], partner, (sem_x1.at[3, 0], sem_x1.at[3, 1]), left),
    ]
    for c in c2:
        c.start()
    lp = (1 - yh) * 4 + (xi + 3) % 4
    rp = (1 - yh) * 4 + (xi + 1) % 4
    remote(x_ref, left, (sem_x1.at[0, 0], sem_x1.at[0, 1]), left).wait_recv()
    remote(x_ref, right, (sem_x1.at[1, 0], sem_x1.at[1, 1]), right).wait_recv()
    c3 = [
        remote(y_ref.at[left], left, (sem_x2.at[0, 0], sem_x2.at[0, 1]), right),
    ]
    c3[0].start()
    remote(x_ref, rp, (sem_x1.at[3, 0], sem_x1.at[3, 1]), right).wait_recv()
    c4 = remote(y_ref.at[rp], rp, (sem_x2.at[1, 0], sem_x2.at[1, 1]), left)
    c4.start()
    remote(x_ref, lp, (sem_x1.at[2, 0], sem_x1.at[2, 1]), left).wait_recv()
    far = yh * 4 + (xi + 2) % 4
    far_p = (1 - yh) * 4 + (xi + 2) % 4
    remote(x_ref, far, (sem_x2.at[0, 0], sem_x2.at[0, 1]), left).wait_recv()
    remote(x_ref, far_p, (sem_x2.at[1, 0], sem_x2.at[1, 1]), right).wait_recv()
    return [cy] + c1 + c2 + c3 + [c4], own


class _Slots:
    def __init__(self, fn):
        self.fn = fn

    def __getitem__(self, k):
        return self.fn(k)


def _narrow_peers():
    me = lax.axis_index("narrow")
    yh = me // 4
    xi = me % 4
    return ((1 - yh) * 4 + xi, yh * 4 + (xi + 1) % 4, yh * 4 + (xi + 3) % 4)


def _dispatch_kernel(x_ref, y_ref, r_ref, sem_w, own_w, sem_y, sem_x1, sem_x2, own_g):
    nw, _, cols = x_ref.shape
    halves = 2
    cw = cols // halves
    me_w = lax.axis_index("wide")
    me = lax.axis_index("narrow")
    barrier = pltpu.get_barrier_semaphore()

    def greet(k, carry):
        pl.semaphore_signal(barrier, inc=1, device_id=((me_w + k) % nw, me), device_id_type=MESH)
        return carry

    lax.fori_loop(1, nw, greet, 0)
    for peer in _narrow_peers():
        pl.semaphore_signal(barrier, inc=1, device_id=(me_w, peer), device_id_type=MESH)
    pl.semaphore_wait(barrier, nw - 1 + 3)

    def wide_copy(h, k, peer_of_copy, target):
        cs = pl.ds(h * cw, cw)
        return pltpu.make_async_remote_copy(
            src_ref=x_ref.at[peer_of_copy, :, cs],
            dst_ref=r_ref.at[target, :, cs],
            send_sem=sem_w.at[h, k, 0],
            recv_sem=sem_w.at[h, k, 1],
            device_id=(peer_of_copy, me),
            device_id_type=MESH,
        )

    def wide_start(h):
        cs = pl.ds(h * cw, cw)
        own = pltpu.make_async_copy(x_ref.at[me_w, :, cs], r_ref.at[me_w, :, cs], own_w.at[h])
        own.start()

        def body(k, carry):
            wide_copy(h, k, (me_w + k) % nw, me_w).start()
            return carry

        lax.fori_loop(1, nw, body, 0)
        return own

    def wide_wait(h, own):
        def body(k, carry):
            src = (me_w + nw - k) % nw
            pltpu.make_async_remote_copy(
                src_ref=x_ref.at[src, :, pl.ds(h * cw, cw)],
                dst_ref=r_ref.at[src, :, pl.ds(h * cw, cw)],
                send_sem=sem_w.at[h, k, 0],
                recv_sem=sem_w.at[h, k, 1],
                device_id=(src, me),
                device_id_type=MESH,
            ).wait_recv()
            return carry

        lax.fori_loop(1, nw, body, 0)
        own.wait()

    def wide_sent(h):
        def body(k, carry):
            wide_copy(h, k, (me_w + k) % nw, me_w).wait_send()
            return carry

        lax.fori_loop(1, nw, body, 0)

    pending = []
    own0 = wide_start(0)
    wide_wait(0, own0)
    own1 = wide_start(1)
    for h in range(halves):
        if h == 1:
            wide_wait(1, own1)
        cs = pl.ds(h * cw, cw)
        sends, own = _gather_chain(
            r_ref.at[:, :, cs],
            lambda k, cs=cs: y_ref.at[k, :, :, cs],
            sem_y.at[h],
            sem_x1.at[h],
            sem_x2.at[h],
            own_g.at[h],
        )
        pending.append((sends, own))
    for h in range(halves):
        wide_sent(h)
        sends, own = pending[h]
        for c in sends:
            c.wait_send()
        own.wait()


def _dispatch(x, n_narrow, collective_id):
    nw, rows, cols = x.shape
    return pl.pallas_call(
        _dispatch_kernel,
        out_shape=jax.ShapeDtypeStruct((n_narrow, nw, rows, cols), x.dtype),
        in_specs=[pl.BlockSpec(memory_space=pl.ANY)],
        out_specs=pl.BlockSpec(memory_space=pl.ANY),
        scratch_shapes=[
            pltpu.VMEM((nw, rows, cols), x.dtype),
            pltpu.SemaphoreType.DMA((2, nw, 2)),
            pltpu.SemaphoreType.DMA((2,)),
            pltpu.SemaphoreType.DMA((2, 2)),
            pltpu.SemaphoreType.DMA((2, 4, 2)),
            pltpu.SemaphoreType.DMA((2, 2, 2)),
            pltpu.SemaphoreType.DMA((2,)),
        ],
        compiler_params=pltpu.CompilerParams(collective_id=collective_id, has_side_effects=True),
        cost_estimate=pl.CostEstimate(
            flops=0, bytes_accessed=2 * (n_narrow + 1) * x.size * x.dtype.itemsize, transcendentals=0
        ),
    )(x)


def _add_into(dst, *srcs):
    rows_all = dst.shape[0]
    step = 128 if rows_all % 128 == 0 else rows_all

    def body(i, carry):
        rows = pl.ds(pl.multiple_of(i * step, step), step)
        total = srcs[0][rows].astype(jnp.float32)
        for src in srcs[1:]:
            total = total + src[rows].astype(jnp.float32)
        dst[rows] = total.astype(dst.dtype)
        return carry

    lax.fori_loop(0, rows_all // step, body, 0)


def _reduce_kernel(p_ref, r_ref, rp, rm, sp, sm, qy, ry, o_ref, sem_p, sem_m, sem_y, sem_w, own_w):
    me = lax.axis_index("narrow")
    w = lax.axis_index("wide")
    yh = me // 4
    xi = me % 4
    other = 1 - yh
    partner = other * 4 + xi
    right = yh * 4 + (xi + 1) % 4
    left = yh * 4 + (xi + 3) % 4
    nw = r_ref.shape[0]
    barrier = pltpu.get_barrier_semaphore()
    for peer in (partner, right, left):
        pl.semaphore_signal(barrier, inc=1, device_id=(w, peer), device_id_type=MESH)

    def greet(k, carry):
        pl.semaphore_signal(barrier, inc=1, device_id=((w + k) % nw, me), device_id_type=MESH)
        return carry

    lax.fori_loop(1, nw, greet, 0)
    pl.semaphore_wait(barrier, 3 + nw - 1)

    def remote(src, dst, sem, peer):
        return pltpu.make_async_remote_copy(
            src_ref=src,
            dst_ref=dst,
            send_sem=sem.at[0],
            recv_sem=sem.at[1],
            device_id=(w, peer),
            device_id_type=MESH,
        )

    half = p_ref.shape[2] // 2
    cols = (pl.ds(0, half), pl.ds(half, half))
    peers = (right, left)
    froms = (left, right)
    offsets = ((3, 2, 1), (1, 2, 3))

    def plane(h, rb, sb, sem):
        sends = []
        for d in (0, 1):
            src = p_ref.at[h * 4 + (xi + offsets[d][0]) % 4, :, cols[d]]
            c = remote(src, rb.at[d, 0], sem.at[d, 0], peers[d])
            c.start()
            sends.append(c)
        for step in (1, 2):
            for d in (0, 1):
                remote(sb.at[d, step - 1], rb.at[d, step - 1], sem.at[d, step - 1], froms[d]).wait_recv()
                term = p_ref.at[h * 4 + (xi + offsets[d][step]) % 4, :, cols[d]]
                _add_into(sb.at[d, step - 1], rb.at[d, step - 1], term)
                c = remote(sb.at[d, step - 1], rb.at[d, step], sem.at[d, step], peers[d])
                c.start()
                sends.append(c)
        for d in (0, 1):
            remote(sb.at[d, 1], rb.at[d, 2], sem.at[d, 2], froms[d]).wait_recv()
        return sends

    sends = plane(other, rp, sp, sem_p)
    for d in (0, 1):
        _add_into(qy.at[:, cols[d]], rp.at[d, 2], p_ref.at[other * 4 + xi, :, cols[d]])
    c = remote(qy, ry, sem_y, partner)
    c.start()
    sends.append(c)
    sends += plane(yh, rm, sm, sem_m)
    remote(qy, ry, sem_y, partner).wait_recv()
    own_p = p_ref.at[yh * 4 + xi]
    cap = o_ref.shape[1]
    for b in range(nw):
        rows = pl.ds(b * cap, cap)
        for d in (0, 1):
            total = rm[d, 2, rows, :].astype(jnp.float32) + own_p[rows, cols[d]].astype(jnp.float32)
            o_ref[b, :, cols[d]] = (total + ry[rows, cols[d]].astype(jnp.float32)).astype(o_ref.dtype)
    own = pltpu.make_async_copy(o_ref.at[w], r_ref.at[w], own_w)
    own.start()

    def wide_copy(k, peer, origin):
        return pltpu.make_async_remote_copy(
            src_ref=o_ref.at[peer],
            dst_ref=r_ref.at[origin],
            send_sem=sem_w.at[k, 0],
            recv_sem=sem_w.at[k, 1],
            device_id=(peer, me),
            device_id_type=MESH,
        )

    def send_body(k, carry):
        wide_copy(k, (w + k) % nw, w).start()
        return carry

    lax.fori_loop(1, nw, send_body, 0)

    def recv_body(k, carry):
        src = (w + nw - k) % nw
        wide_copy(k, src, src).wait_recv()
        return carry

    lax.fori_loop(1, nw, recv_body, 0)

    def sent_body(k, carry):
        wide_copy(k, (w + k) % nw, w).wait_send()
        return carry

    lax.fori_loop(1, nw, sent_body, 0)
    own.wait()
    for c in sends:
        c.wait_send()


def _reduce(p, nw, collective_id):
    one = p.shape[1:]
    blocks = (nw, one[0] // nw, one[1])
    block = pltpu.VMEM(one, p.dtype)
    return pl.pallas_call(
        _reduce_kernel,
        out_shape=jax.ShapeDtypeStruct(blocks, p.dtype),
        in_specs=[pl.BlockSpec(memory_space=pltpu.VMEM)],
        out_specs=pl.BlockSpec(memory_space=pl.ANY),
        scratch_shapes=[
            pltpu.VMEM((2, 3, one[0], one[1] // 2), p.dtype),
            pltpu.VMEM((2, 3, one[0], one[1] // 2), p.dtype),
            pltpu.VMEM((2, 2, one[0], one[1] // 2), p.dtype),
            pltpu.VMEM((2, 2, one[0], one[1] // 2), p.dtype),
            block,
            block,
            pltpu.VMEM(blocks, p.dtype),
            pltpu.SemaphoreType.DMA((2, 3, 2)),
            pltpu.SemaphoreType.DMA((2, 3, 2)),
            pltpu.SemaphoreType.DMA((2,)),
            pltpu.SemaphoreType.DMA((nw, 2)),
            pltpu.SemaphoreType.DMA(()),
        ],
        compiler_params=pltpu.CompilerParams(collective_id=collective_id, has_side_effects=True),
        cost_estimate=pl.CostEstimate(
            flops=2 * p.size, bytes_accessed=2 * p.size * p.dtype.itemsize, transcendentals=0
        ),
    )(p)


def _exchange(x, n_peers, gather, collective_id, axis="narrow"):
    if gather:
        out_shape = (n_peers,) + x.shape
        pick_src = lambda ref, i: ref
    else:
        out_shape = x.shape
        pick_src = lambda ref, i: ref.at[i]
    nbytes = x.size * x.dtype.itemsize
    return pl.pallas_call(
        lambda *refs: _exchange_kernel(n_peers, pick_src, axis, *refs),
        out_shape=jax.ShapeDtypeStruct(out_shape, x.dtype),
        in_specs=[pl.BlockSpec(memory_space=pl.ANY)],
        out_specs=pl.BlockSpec(memory_space=pl.ANY),
        scratch_shapes=[
            pltpu.SemaphoreType.DMA((n_peers - 1,)),
            pltpu.SemaphoreType.DMA((n_peers - 1,)),
            pltpu.SemaphoreType.DMA(()),
        ],
        compiler_params=pltpu.CompilerParams(collective_id=collective_id, has_side_effects=True),
        cost_estimate=pl.CostEstimate(flops=0, bytes_accessed=2 * nbytes, transcendentals=0),
    )(x)


def local(tokens, expert_ids, route_weights, w_gate, w_up, w_down):
    tok_rows = expert_ids.shape[0]
    top_count = expert_ids.shape[1]
    local_experts = w_gate.shape[0]
    groups_wide = lax.axis_size("wide")
    experts_all = local_experts * groups_wide
    capacity = 7 * tok_rows * top_count // (6 * experts_all)
    slots_all = experts_all * capacity
    flat_ids = expert_ids.reshape(-1)
    onehot = (flat_ids[:, None] == jnp.arange(experts_all, dtype=jnp.int32)[None, :]).astype(
        jnp.int32
    )
    running = jnp.cumsum(onehot, axis=0)
    slot_index = jnp.sum(running * onehot, axis=1) - 1
    destination = (flat_ids * capacity + slot_index).reshape(tok_rows, top_count)
    hit = destination[:, :, None] == jnp.arange(slots_all, dtype=jnp.int32)[None, None, :]
    dispatch = jnp.any(hit, axis=1).astype(jnp.bfloat16)
    combine = jnp.sum(
        jnp.where(hit, route_weights.astype(jnp.float32)[:, :, None], 0.0), axis=1
    ).astype(jnp.bfloat16)
    dispatch = dispatch.reshape(tok_rows, groups_wide, capacity)
    combine = combine.reshape(tok_rows, groups_wide, capacity)
    outgoing = jnp.einsum(
        "tbc,td->bcd", dispatch, tokens, preferred_element_type=jnp.float32
    ).astype(jnp.bfloat16)
    n_narrow = lax.axis_size("narrow")
    width = tokens.shape[1]
    slot_rows = _dispatch(outgoing, n_narrow, 0)
    wg = w_gate[0].reshape(-1, n_narrow, width)
    wu = w_up[0].reshape(-1, n_narrow, width)
    wd = w_down[0].reshape(-1, n_narrow, width)
    gate_proj = jnp.einsum("nbcd,fnd->bcf", slot_rows, wg, preferred_element_type=jnp.float32)
    up_proj = jnp.einsum("nbcd,fnd->bcf", slot_rows, wu, preferred_element_type=jnp.float32)
    hidden = (jax.nn.silu(gate_proj) * up_proj).astype(jnp.bfloat16)
    partial_value = jnp.einsum(
        "sf,fnd->nsd", hidden.reshape(slots_all, -1), wd, preferred_element_type=jnp.float32
    ).astype(jnp.bfloat16)
    returned = _reduce(partial_value, groups_wide, 1)
    mixed = jnp.einsum("tbc,bcd->td", combine, returned, preferred_element_type=jnp.float32)
    return mixed.astype(jnp.bfloat16)


def solution(mesh):
    in_specs = (
        P("wide", "narrow"),
        P("wide", None),
        P("wide", None),
        P("wide", "narrow", None),
        P("wide", "narrow", None),
        P("wide", "narrow", None),
    )
    out_specs = P("wide", "narrow")
    return jax.shard_map(local, mesh=mesh, in_specs=in_specs, out_specs=out_specs, check_vma=False)
```

```python
import types

import jax
import jax.numpy as jnp
from jax import lax
from jax.experimental import pallas as pl
from jax.experimental.pallas import tpu as pltpu
from jax.sharding import PartitionSpec as P

MESH = pl.DeviceIdType.MESH


def _exchange_kernel(n_peers, pick_src, axis, x_ref, y_ref, send_sem, recv_sem, own_sem):
    me = lax.axis_index(axis)
    other = lax.axis_index("wide" if axis == "narrow" else "narrow")
    if axis == "narrow":
        dev = lambda p: (other, p)
    else:
        dev = lambda p: (p, other)
    barrier = pltpu.get_barrier_semaphore()
    for k in range(1, n_peers):
        peer = lax.rem(me + k, n_peers)
        pl.semaphore_signal(barrier, inc=1, device_id=dev(peer), device_id_type=MESH)
    pl.semaphore_wait(barrier, n_peers - 1)
    own = pltpu.make_async_copy(pick_src(x_ref, me), y_ref.at[me], own_sem)
    own.start()
    copies = []
    for k in range(1, n_peers):
        peer = lax.rem(me + k, n_peers)
        c = pltpu.make_async_remote_copy(
            src_ref=pick_src(x_ref, peer),
            dst_ref=y_ref.at[me],
            send_sem=send_sem.at[k - 1],
            recv_sem=recv_sem.at[k - 1],
            device_id=dev(peer),
            device_id_type=MESH,
        )
        c.start()
        copies.append(c)
    for k in range(1, n_peers):
        src = lax.rem(me + n_peers - k, n_peers)
        pltpu.make_async_remote_copy(
            src_ref=pick_src(x_ref, src),
            dst_ref=y_ref.at[src],
            send_sem=send_sem.at[k - 1],
            recv_sem=recv_sem.at[k - 1],
            device_id=dev(src),
            device_id_type=MESH,
        ).wait_recv()
    for c in copies:
        c.wait_send()
    own.wait()


def _gather_chain(x_ref, slot_of, sem_y, sem_x1, sem_x2, own_sem):
    me = lax.axis_index("narrow")
    w = lax.axis_index("wide")
    yh = me // 4
    xi = me % 4
    partner = (1 - yh) * 4 + xi
    right = yh * 4 + (xi + 1) % 4
    left = yh * 4 + (xi + 3) % 4

    y_ref = types.SimpleNamespace(at=_Slots(slot_of))

    def remote(src, slot, sem, peer):
        return pltpu.make_async_remote_copy(
            src_ref=src,
            dst_ref=y_ref.at[slot],
            send_sem=sem[0],
            recv_sem=sem[1],
            device_id=(w, peer),
            device_id_type=MESH,
        )

    own = pltpu.make_async_copy(x_ref, y_ref.at[me], own_sem)
    own.start()
    cy = remote(x_ref, me, (sem_y.at[0], sem_y.at[1]), partner)
    cy.start()
    c1 = [
        remote(x_ref, me, (sem_x1.at[0, 0], sem_x1.at[0, 1]), right),
        remote(x_ref, me, (sem_x1.at[1, 0], sem_x1.at[1, 1]), left),
    ]
    for c in c1:
        c.start()
    remote(x_ref, partner, (sem_y.at[0], sem_y.at[1]), partner).wait_recv()
    c2 = [
        remote(y_ref.at[partner], partner, (sem_x1.at[2, 0], sem_x1.at[2, 1]), right),
        remote(y_ref.at[partner], partner, (sem_x1.at[3, 0], sem_x1.at[3, 1]), left),
    ]
    for c in c2:
        c.start()
    lp = (1 - yh) * 4 + (xi + 3) % 4
    rp = (1 - yh) * 4 + (xi + 1) % 4
    remote(x_ref, left, (sem_x1.at[0, 0], sem_x1.at[0, 1]), left).wait_recv()
    remote(x_ref, right, (sem_x1.at[1, 0], sem_x1.at[1, 1]), right).wait_recv()
    c3 = [
        remote(y_ref.at[left], left, (sem_x2.at[0, 0], sem_x2.at[0, 1]), right),
    ]
    c3[0].start()
    remote(x_ref, rp, (sem_x1.at[3, 0], sem_x1.at[3, 1]), right).wait_recv()
    c4 = remote(y_ref.at[rp], rp, (sem_x2.at[1, 0], sem_x2.at[1, 1]), left)
    c4.start()
    remote(x_ref, lp, (sem_x1.at[2, 0], sem_x1.at[2, 1]), left).wait_recv()
    far = yh * 4 + (xi + 2) % 4
    far_p = (1 - yh) * 4 + (xi + 2) % 4
    remote(x_ref, far, (sem_x2.at[0, 0], sem_x2.at[0, 1]), left).wait_recv()
    remote(x_ref, far_p, (sem_x2.at[1, 0], sem_x2.at[1, 1]), right).wait_recv()
    return [cy] + c1 + c2 + c3 + [c4], own


class _Slots:
    def __init__(self, fn):
        self.fn = fn

    def __getitem__(self, k):
        return self.fn(k)


def _narrow_peers():
    me = lax.axis_index("narrow")
    yh = me // 4
    xi = me % 4
    return ((1 - yh) * 4 + xi, yh * 4 + (xi + 1) % 4, yh * 4 + (xi + 3) % 4)


def _dispatch_kernel(x_ref, y_ref, r_ref, sem_w, own_w, sem_y, sem_x1, sem_x2, own_g):
    nw, _, cols = x_ref.shape
    halves = 1
    cw = cols // halves
    me_w = lax.axis_index("wide")
    me = lax.axis_index("narrow")
    barrier = pltpu.get_barrier_semaphore()

    def greet(k, carry):
        pl.semaphore_signal(barrier, inc=1, device_id=((me_w + k) % nw, me), device_id_type=MESH)
        return carry

    lax.fori_loop(1, nw, greet, 0)
    for peer in _narrow_peers():
        pl.semaphore_signal(barrier, inc=1, device_id=(me_w, peer), device_id_type=MESH)
    pl.semaphore_wait(barrier, nw - 1 + 3)

    def wide_copy(h, k, peer_of_copy, target):
        cs = pl.ds(h * cw, cw)
        return pltpu.make_async_remote_copy(
            src_ref=x_ref.at[peer_of_copy, :, cs],
            dst_ref=r_ref.at[target, :, cs],
            send_sem=sem_w.at[h, k, 0],
            recv_sem=sem_w.at[h, k, 1],
            device_id=(peer_of_copy, me),
            device_id_type=MESH,
        )

    def wide_start(h):
        cs = pl.ds(h * cw, cw)
        own = pltpu.make_async_copy(x_ref.at[me_w, :, cs], r_ref.at[me_w, :, cs], own_w.at[h])
        own.start()

        def body(k, carry):
            wide_copy(h, k, (me_w + k) % nw, me_w).start()
            return carry

        lax.fori_loop(1, nw, body, 0)
        return own

    def wide_wait(h, own):
        def body(k, carry):
            src = (me_w + nw - k) % nw
            pltpu.make_async_remote_copy(
                src_ref=x_ref.at[src, :, pl.ds(h * cw, cw)],
                dst_ref=r_ref.at[src, :, pl.ds(h * cw, cw)],
                send_sem=sem_w.at[h, k, 0],
                recv_sem=sem_w.at[h, k, 1],
                device_id=(src, me),
                device_id_type=MESH,
            ).wait_recv()
            return carry

        lax.fori_loop(1, nw, body, 0)
        own.wait()

    def wide_sent(h):
        def body(k, carry):
            wide_copy(h, k, (me_w + k) % nw, me_w).wait_send()
            return carry

        lax.fori_loop(1, nw, body, 0)

    pending = []
    own0 = wide_start(0)
    wide_wait(0, own0)
    if halves > 1:
        own1 = wide_start(1)
    for h in range(halves):
        if h == 1:
            wide_wait(1, own1)
        cs = pl.ds(h * cw, cw)
        sends, own = _gather_chain(
            r_ref.at[:, :, cs],
            lambda k, cs=cs: y_ref.at[k, :, :, cs],
            sem_y.at[h],
            sem_x1.at[h],
            sem_x2.at[h],
            own_g.at[h],
        )
        pending.append((sends, own))
    for h in range(halves):
        wide_sent(h)
        sends, own = pending[h]
        for c in sends:
            c.wait_send()
        own.wait()


def _dispatch(x, n_narrow, collective_id):
    nw, rows, cols = x.shape
    return pl.pallas_call(
        _dispatch_kernel,
        out_shape=jax.ShapeDtypeStruct((n_narrow, nw, rows, cols), x.dtype),
        in_specs=[pl.BlockSpec(memory_space=pl.ANY)],
        out_specs=pl.BlockSpec(memory_space=pl.ANY),
        scratch_shapes=[
            pltpu.VMEM((nw, rows, cols), x.dtype),
            pltpu.SemaphoreType.DMA((2, nw, 2)),
            pltpu.SemaphoreType.DMA((2,)),
            pltpu.SemaphoreType.DMA((2, 2)),
            pltpu.SemaphoreType.DMA((2, 4, 2)),
            pltpu.SemaphoreType.DMA((2, 2, 2)),
            pltpu.SemaphoreType.DMA((2,)),
        ],
        compiler_params=pltpu.CompilerParams(collective_id=collective_id, has_side_effects=True),
        cost_estimate=pl.CostEstimate(
            flops=0, bytes_accessed=2 * (n_narrow + 1) * x.size * x.dtype.itemsize, transcendentals=0
        ),
    )(x)


def _add_into(dst, *srcs):
    rows_all = dst.shape[0]
    step = 128 if rows_all % 128 == 0 else rows_all

    def body(i, carry):
        rows = pl.ds(pl.multiple_of(i * step, step), step)
        total = srcs[0][rows].astype(jnp.float32)
        for src in srcs[1:]:
            total = total + src[rows].astype(jnp.float32)
        dst[rows] = total.astype(dst.dtype)
        return carry

    lax.fori_loop(0, rows_all // step, body, 0)


def _reduce_kernel(p_ref, r_ref, rp, rm, sp, sm, qy, ry, o_ref, sem_p, sem_m, sem_y, sem_w, own_w):
    me = lax.axis_index("narrow")
    w = lax.axis_index("wide")
    yh = me // 4
    xi = me % 4
    other = 1 - yh
    partner = other * 4 + xi
    right = yh * 4 + (xi + 1) % 4
    left = yh * 4 + (xi + 3) % 4
    nw = r_ref.shape[0]
    barrier = pltpu.get_barrier_semaphore()
    for peer in (partner, right, left):
        pl.semaphore_signal(barrier, inc=1, device_id=(w, peer), device_id_type=MESH)

    def greet(k, carry):
        pl.semaphore_signal(barrier, inc=1, device_id=((w + k) % nw, me), device_id_type=MESH)
        return carry

    lax.fori_loop(1, nw, greet, 0)
    pl.semaphore_wait(barrier, 3 + nw - 1)

    def remote(src, dst, sem, peer):
        return pltpu.make_async_remote_copy(
            src_ref=src,
            dst_ref=dst,
            send_sem=sem.at[0],
            recv_sem=sem.at[1],
            device_id=(w, peer),
            device_id_type=MESH,
        )

    half = p_ref.shape[2] // 2
    cols = (pl.ds(0, half), pl.ds(half, half))
    peers = (right, left)
    froms = (left, right)
    offsets = ((3, 2, 1), (1, 2, 3))

    def plane(h, rb, sb, sem):
        sends = []
        for d in (0, 1):
            src = p_ref.at[h * 4 + (xi + offsets[d][0]) % 4, :, cols[d]]
            c = remote(src, rb.at[d, 0], sem.at[d, 0], peers[d])
            c.start()
            sends.append(c)
        for step in (1, 2):
            for d in (0, 1):
                remote(sb.at[d, step - 1], rb.at[d, step - 1], sem.at[d, step - 1], froms[d]).wait_recv()
                term = p_ref.at[h * 4 + (xi + offsets[d][step]) % 4, :, cols[d]]
                _add_into(sb.at[d, step - 1], rb.at[d, step - 1], term)
                c = remote(sb.at[d, step - 1], rb.at[d, step], sem.at[d, step], peers[d])
                c.start()
                sends.append(c)
        for d in (0, 1):
            remote(sb.at[d, 1], rb.at[d, 2], sem.at[d, 2], froms[d]).wait_recv()
        return sends

    sends = plane(other, rp, sp, sem_p)
    for d in (0, 1):
        _add_into(qy.at[:, cols[d]], rp.at[d, 2], p_ref.at[other * 4 + xi, :, cols[d]])
    c = remote(qy, ry, sem_y, partner)
    c.start()
    sends.append(c)
    sends += plane(yh, rm, sm, sem_m)
    remote(qy, ry, sem_y, partner).wait_recv()
    own_p = p_ref.at[yh * 4 + xi]
    cap = o_ref.shape[1]
    for b in range(nw):
        rows = pl.ds(b * cap, cap)
        for d in (0, 1):
            total = rm[d, 2, rows, :].astype(jnp.float32) + own_p[rows, cols[d]].astype(jnp.float32)
            o_ref[b, :, cols[d]] = (total + ry[rows, cols[d]].astype(jnp.float32)).astype(o_ref.dtype)
    own = pltpu.make_async_copy(o_ref.at[w], r_ref.at[w], own_w)
    own.start()

    def wide_copy(k, peer, origin):
        return pltpu.make_async_remote_copy(
            src_ref=o_ref.at[peer],
            dst_ref=r_ref.at[origin],
            send_sem=sem_w.at[k, 0],
            recv_sem=sem_w.at[k, 1],
            device_id=(peer, me),
            device_id_type=MESH,
        )

    def send_body(k, carry):
        wide_copy(k, (w + k) % nw, w).start()
        return carry

    lax.fori_loop(1, nw, send_body, 0)

    def recv_body(k, carry):
        src = (w + nw - k) % nw
        wide_copy(k, src, src).wait_recv()
        return carry

    lax.fori_loop(1, nw, recv_body, 0)

    def sent_body(k, carry):
        wide_copy(k, (w + k) % nw, w).wait_send()
        return carry

    lax.fori_loop(1, nw, sent_body, 0)
    own.wait()
    for c in sends:
        c.wait_send()


def _reduce(p, nw, collective_id):
    one = p.shape[1:]
    blocks = (nw, one[0] // nw, one[1])
    block = pltpu.VMEM(one, p.dtype)
    return pl.pallas_call(
        _reduce_kernel,
        out_shape=jax.ShapeDtypeStruct(blocks, p.dtype),
        in_specs=[pl.BlockSpec(memory_space=pltpu.VMEM)],
        out_specs=pl.BlockSpec(memory_space=pl.ANY),
        scratch_shapes=[
            pltpu.VMEM((2, 3, one[0], one[1] // 2), p.dtype),
            pltpu.VMEM((2, 3, one[0], one[1] // 2), p.dtype),
            pltpu.VMEM((2, 2, one[0], one[1] // 2), p.dtype),
            pltpu.VMEM((2, 2, one[0], one[1] // 2), p.dtype),
            block,
            block,
            pltpu.VMEM(blocks, p.dtype),
            pltpu.SemaphoreType.DMA((2, 3, 2)),
            pltpu.SemaphoreType.DMA((2, 3, 2)),
            pltpu.SemaphoreType.DMA((2,)),
            pltpu.SemaphoreType.DMA((nw, 2)),
            pltpu.SemaphoreType.DMA(()),
        ],
        compiler_params=pltpu.CompilerParams(collective_id=collective_id, has_side_effects=True),
        cost_estimate=pl.CostEstimate(
            flops=2 * p.size, bytes_accessed=2 * p.size * p.dtype.itemsize, transcendentals=0
        ),
    )(p)


def _exchange(x, n_peers, gather, collective_id, axis="narrow"):
    if gather:
        out_shape = (n_peers,) + x.shape
        pick_src = lambda ref, i: ref
    else:
        out_shape = x.shape
        pick_src = lambda ref, i: ref.at[i]
    nbytes = x.size * x.dtype.itemsize
    return pl.pallas_call(
        lambda *refs: _exchange_kernel(n_peers, pick_src, axis, *refs),
        out_shape=jax.ShapeDtypeStruct(out_shape, x.dtype),
        in_specs=[pl.BlockSpec(memory_space=pl.ANY)],
        out_specs=pl.BlockSpec(memory_space=pl.ANY),
        scratch_shapes=[
            pltpu.SemaphoreType.DMA((n_peers - 1,)),
            pltpu.SemaphoreType.DMA((n_peers - 1,)),
            pltpu.SemaphoreType.DMA(()),
        ],
        compiler_params=pltpu.CompilerParams(collective_id=collective_id, has_side_effects=True),
        cost_estimate=pl.CostEstimate(flops=0, bytes_accessed=2 * nbytes, transcendentals=0),
    )(x)


def local(tokens, expert_ids, route_weights, w_gate, w_up, w_down):
    tok_rows = expert_ids.shape[0]
    top_count = expert_ids.shape[1]
    local_experts = w_gate.shape[0]
    groups_wide = lax.axis_size("wide")
    experts_all = local_experts * groups_wide
    capacity = 7 * tok_rows * top_count // (6 * experts_all)
    slots_all = experts_all * capacity
    flat_ids = expert_ids.reshape(-1)
    onehot = (flat_ids[:, None] == jnp.arange(experts_all, dtype=jnp.int32)[None, :]).astype(
        jnp.int32
    )
    running = jnp.cumsum(onehot, axis=0)
    slot_index = jnp.sum(running * onehot, axis=1) - 1
    destination = (flat_ids * capacity + slot_index).reshape(tok_rows, top_count)
    hit = destination[:, :, None] == jnp.arange(slots_all, dtype=jnp.int32)[None, None, :]
    dispatch = jnp.any(hit, axis=1).astype(jnp.bfloat16)
    combine = jnp.sum(
        jnp.where(hit, route_weights.astype(jnp.float32)[:, :, None], 0.0), axis=1
    ).astype(jnp.bfloat16)
    dispatch = dispatch.reshape(tok_rows, groups_wide, capacity)
    combine = combine.reshape(tok_rows, groups_wide, capacity)
    outgoing = jnp.einsum(
        "tbc,td->bcd", dispatch, tokens, preferred_element_type=jnp.float32
    ).astype(jnp.bfloat16)
    n_narrow = lax.axis_size("narrow")
    width = tokens.shape[1]
    slot_rows = _dispatch(outgoing, n_narrow, 0)
    wg = w_gate[0].reshape(-1, n_narrow, width)
    wu = w_up[0].reshape(-1, n_narrow, width)
    wd = w_down[0].reshape(-1, n_narrow, width)
    gate_proj = jnp.einsum("nbcd,fnd->bcf", slot_rows, wg, preferred_element_type=jnp.float32)
    up_proj = jnp.einsum("nbcd,fnd->bcf", slot_rows, wu, preferred_element_type=jnp.float32)
    hidden = (jax.nn.silu(gate_proj) * up_proj).astype(jnp.bfloat16)
    partial_value = jnp.einsum(
        "sf,fnd->nsd", hidden.reshape(slots_all, -1), wd, preferred_element_type=jnp.float32
    ).astype(jnp.bfloat16)
    returned = _reduce(partial_value, groups_wide, 1)
    mixed = jnp.einsum("tbc,bcd->td", combine, returned, preferred_element_type=jnp.float32)
    return mixed.astype(jnp.bfloat16)


def solution(mesh):
    in_specs = (
        P("wide", "narrow"),
        P("wide", None),
        P("wide", None),
        P("wide", "narrow", None),
        P("wide", "narrow", None),
        P("wide", "narrow", None),
    )
    out_specs = P("wide", "narrow")
    return jax.shard_map(local, mesh=mesh, in_specs=in_specs, out_specs=out_specs, check_vma=False)
```

```python
import types

import jax
import jax.numpy as jnp
from jax import lax
from jax.experimental import pallas as pl
from jax.experimental.pallas import tpu as pltpu
from jax.sharding import PartitionSpec as P

MESH = pl.DeviceIdType.MESH


def _exchange_kernel(n_peers, pick_src, axis, x_ref, y_ref, send_sem, recv_sem, own_sem):
    me = lax.axis_index(axis)
    other = lax.axis_index("wide" if axis == "narrow" else "narrow")
    if axis == "narrow":
        dev = lambda p: (other, p)
    else:
        dev = lambda p: (p, other)
    barrier = pltpu.get_barrier_semaphore()
    for k in range(1, n_peers):
        peer = lax.rem(me + k, n_peers)
        pl.semaphore_signal(barrier, inc=1, device_id=dev(peer), device_id_type=MESH)
    pl.semaphore_wait(barrier, n_peers - 1)
    own = pltpu.make_async_copy(pick_src(x_ref, me), y_ref.at[me], own_sem)
    own.start()
    copies = []
    for k in range(1, n_peers):
        peer = lax.rem(me + k, n_peers)
        c = pltpu.make_async_remote_copy(
            src_ref=pick_src(x_ref, peer),
            dst_ref=y_ref.at[me],
            send_sem=send_sem.at[k - 1],
            recv_sem=recv_sem.at[k - 1],
            device_id=dev(peer),
            device_id_type=MESH,
        )
        c.start()
        copies.append(c)
    for k in range(1, n_peers):
        src = lax.rem(me + n_peers - k, n_peers)
        pltpu.make_async_remote_copy(
            src_ref=pick_src(x_ref, src),
            dst_ref=y_ref.at[src],
            send_sem=send_sem.at[k - 1],
            recv_sem=recv_sem.at[k - 1],
            device_id=dev(src),
            device_id_type=MESH,
        ).wait_recv()
    for c in copies:
        c.wait_send()
    own.wait()


def _gather_chain(x_ref, slot_of, sem_y, sem_x1, sem_x2, own_sem, after_start=None):
    me = lax.axis_index("narrow")
    w = lax.axis_index("wide")
    yh = me // 4
    xi = me % 4
    partner = (1 - yh) * 4 + xi
    right = yh * 4 + (xi + 1) % 4
    left = yh * 4 + (xi + 3) % 4

    y_ref = types.SimpleNamespace(at=_Slots(slot_of))

    def remote(src, slot, sem, peer):
        return pltpu.make_async_remote_copy(
            src_ref=src,
            dst_ref=y_ref.at[slot],
            send_sem=sem[0],
            recv_sem=sem[1],
            device_id=(w, peer),
            device_id_type=MESH,
        )

    own = pltpu.make_async_copy(x_ref, y_ref.at[me], own_sem)
    own.start()
    cy = remote(x_ref, me, (sem_y.at[0], sem_y.at[1]), partner)
    cy.start()
    c1 = [
        remote(x_ref, me, (sem_x1.at[0, 0], sem_x1.at[0, 1]), right),
        remote(x_ref, me, (sem_x1.at[1, 0], sem_x1.at[1, 1]), left),
    ]
    for c in c1:
        c.start()
    if after_start is not None:
        after_start()
    remote(x_ref, partner, (sem_y.at[0], sem_y.at[1]), partner).wait_recv()
    c2 = [
        remote(y_ref.at[partner], partner, (sem_x1.at[2, 0], sem_x1.at[2, 1]), right),
        remote(y_ref.at[partner], partner, (sem_x1.at[3, 0], sem_x1.at[3, 1]), left),
    ]
    for c in c2:
        c.start()
    lp = (1 - yh) * 4 + (xi + 3) % 4
    rp = (1 - yh) * 4 + (xi + 1) % 4
    remote(x_ref, left, (sem_x1.at[0, 0], sem_x1.at[0, 1]), left).wait_recv()
    remote(x_ref, right, (sem_x1.at[1, 0], sem_x1.at[1, 1]), right).wait_recv()
    c3 = [
        remote(y_ref.at[left], left, (sem_x2.at[0, 0], sem_x2.at[0, 1]), right),
    ]
    c3[0].start()
    remote(x_ref, rp, (sem_x1.at[3, 0], sem_x1.at[3, 1]), right).wait_recv()
    c4 = remote(y_ref.at[rp], rp, (sem_x2.at[1, 0], sem_x2.at[1, 1]), left)
    c4.start()
    remote(x_ref, lp, (sem_x1.at[2, 0], sem_x1.at[2, 1]), left).wait_recv()
    far = yh * 4 + (xi + 2) % 4
    far_p = (1 - yh) * 4 + (xi + 2) % 4
    remote(x_ref, far, (sem_x2.at[0, 0], sem_x2.at[0, 1]), left).wait_recv()
    remote(x_ref, far_p, (sem_x2.at[1, 0], sem_x2.at[1, 1]), right).wait_recv()
    return [cy] + c1 + c2 + c3 + [c4], own


class _Slots:
    def __init__(self, fn):
        self.fn = fn

    def __getitem__(self, k):
        return self.fn(k)


def _narrow_peers():
    me = lax.axis_index("narrow")
    yh = me // 4
    xi = me % 4
    return ((1 - yh) * 4 + xi, yh * 4 + (xi + 1) % 4, yh * 4 + (xi + 3) % 4)


def _dispatch_kernel(x_ref, y_ref, r_ref, sem_w, own_w, sem_y, sem_x1, sem_x2, own_g):
    nw, _, cols = x_ref.shape
    halves = 2
    cw = cols // halves
    me_w = lax.axis_index("wide")
    me = lax.axis_index("narrow")
    barrier = pltpu.get_barrier_semaphore()

    def greet(k, carry):
        pl.semaphore_signal(barrier, inc=1, device_id=((me_w + k) % nw, me), device_id_type=MESH)
        return carry

    lax.fori_loop(1, nw, greet, 0)
    for peer in _narrow_peers():
        pl.semaphore_signal(barrier, inc=1, device_id=(me_w, peer), device_id_type=MESH)
    pl.semaphore_wait(barrier, nw - 1 + 3)

    def wide_copy(h, k, peer_of_copy, target):
        cs = pl.ds(h * cw, cw)
        return pltpu.make_async_remote_copy(
            src_ref=x_ref.at[peer_of_copy, :, cs],
            dst_ref=r_ref.at[target, :, cs],
            send_sem=sem_w.at[h, k, 0],
            recv_sem=sem_w.at[h, k, 1],
            device_id=(peer_of_copy, me),
            device_id_type=MESH,
        )

    def wide_start(h):
        cs = pl.ds(h * cw, cw)
        own = pltpu.make_async_copy(x_ref.at[me_w, :, cs], r_ref.at[me_w, :, cs], own_w.at[h])
        own.start()

        def body(k, carry):
            wide_copy(h, k, (me_w + k) % nw, me_w).start()
            return carry

        lax.fori_loop(1, nw, body, 0)
        return own

    def wide_wait(h, own):
        def body(k, carry):
            src = (me_w + nw - k) % nw
            pltpu.make_async_remote_copy(
                src_ref=x_ref.at[src, :, pl.ds(h * cw, cw)],
                dst_ref=r_ref.at[src, :, pl.ds(h * cw, cw)],
                send_sem=sem_w.at[h, k, 0],
                recv_sem=sem_w.at[h, k, 1],
                device_id=(src, me),
                device_id_type=MESH,
            ).wait_recv()
            return carry

        lax.fori_loop(1, nw, body, 0)
        own.wait()

    def wide_sent(h):
        def body(k, carry):
            wide_copy(h, k, (me_w + k) % nw, me_w).wait_send()
            return carry

        lax.fori_loop(1, nw, body, 0)

    pending = []
    own0 = wide_start(0)
    wide_wait(0, own0)
    owns = []
    for h in range(halves):
        if h == 1:
            wide_wait(1, owns[0])
        cs = pl.ds(h * cw, cw)
        sends, own = _gather_chain(
            r_ref.at[:, :, cs],
            lambda k, cs=cs: y_ref.at[k, :, :, cs],
            sem_y.at[h],
            sem_x1.at[h],
            sem_x2.at[h],
            own_g.at[h],
            (lambda: owns.append(wide_start(1))) if h == 0 else None,
        )
        pending.append((sends, own))
    for h in range(halves):
        wide_sent(h)
        sends, own = pending[h]
        for c in sends:
            c.wait_send()
        own.wait()


def _dispatch(x, n_narrow, collective_id):
    nw, rows, cols = x.shape
    return pl.pallas_call(
        _dispatch_kernel,
        out_shape=jax.ShapeDtypeStruct((n_narrow, nw, rows, cols), x.dtype),
        in_specs=[pl.BlockSpec(memory_space=pl.ANY)],
        out_specs=pl.BlockSpec(memory_space=pl.ANY),
        scratch_shapes=[
            pltpu.VMEM((nw, rows, cols), x.dtype),
            pltpu.SemaphoreType.DMA((2, nw, 2)),
            pltpu.SemaphoreType.DMA((2,)),
            pltpu.SemaphoreType.DMA((2, 2)),
            pltpu.SemaphoreType.DMA((2, 4, 2)),
            pltpu.SemaphoreType.DMA((2, 2, 2)),
            pltpu.SemaphoreType.DMA((2,)),
        ],
        compiler_params=pltpu.CompilerParams(collective_id=collective_id, has_side_effects=True),
        cost_estimate=pl.CostEstimate(
            flops=0, bytes_accessed=2 * (n_narrow + 1) * x.size * x.dtype.itemsize, transcendentals=0
        ),
    )(x)


def _add_into(dst, *srcs):
    rows_all = dst.shape[0]
    step = 128 if rows_all % 128 == 0 else rows_all

    def body(i, carry):
        rows = pl.ds(pl.multiple_of(i * step, step), step)
        total = srcs[0][rows].astype(jnp.float32)
        for src in srcs[1:]:
            total = total + src[rows].astype(jnp.float32)
        dst[rows] = total.astype(dst.dtype)
        return carry

    lax.fori_loop(0, rows_all // step, body, 0)


def _reduce_kernel(p_ref, r_ref, rp, rm, sp, sm, qy, ry, o_ref, sem_p, sem_m, sem_y, sem_w, own_w):
    me = lax.axis_index("narrow")
    w = lax.axis_index("wide")
    yh = me // 4
    xi = me % 4
    other = 1 - yh
    partner = other * 4 + xi
    right = yh * 4 + (xi + 1) % 4
    left = yh * 4 + (xi + 3) % 4
    nw = r_ref.shape[0]
    barrier = pltpu.get_barrier_semaphore()
    for peer in (partner, right, left):
        pl.semaphore_signal(barrier, inc=1, device_id=(w, peer), device_id_type=MESH)

    def greet(k, carry):
        pl.semaphore_signal(barrier, inc=1, device_id=((w + k) % nw, me), device_id_type=MESH)
        return carry

    lax.fori_loop(1, nw, greet, 0)
    pl.semaphore_wait(barrier, 3 + nw - 1)

    def remote(src, dst, sem, peer):
        return pltpu.make_async_remote_copy(
            src_ref=src,
            dst_ref=dst,
            send_sem=sem.at[0],
            recv_sem=sem.at[1],
            device_id=(w, peer),
            device_id_type=MESH,
        )

    half = p_ref.shape[2] // 2
    cols = (pl.ds(0, half), pl.ds(half, half))
    peers = (right, left)
    froms = (left, right)
    offsets = ((3, 2, 1), (1, 2, 3))

    def plane(h, rb, sb, sem):
        sends = []
        for d in (0, 1):
            src = p_ref.at[h * 4 + (xi + offsets[d][0]) % 4, :, cols[d]]
            c = remote(src, rb.at[d, 0], sem.at[d, 0], peers[d])
            c.start()
            sends.append(c)
        for step in (1, 2):
            for d in (0, 1):
                remote(sb.at[d, step - 1], rb.at[d, step - 1], sem.at[d, step - 1], froms[d]).wait_recv()
                term = p_ref.at[h * 4 + (xi + offsets[d][step]) % 4, :, cols[d]]
                _add_into(sb.at[d, step - 1], rb.at[d, step - 1], term)
                c = remote(sb.at[d, step - 1], rb.at[d, step], sem.at[d, step], peers[d])
                c.start()
                sends.append(c)
        for d in (0, 1):
            remote(sb.at[d, 1], rb.at[d, 2], sem.at[d, 2], froms[d]).wait_recv()
        return sends

    sends = plane(other, rp, sp, sem_p)
    for d in (0, 1):
        _add_into(qy.at[:, cols[d]], rp.at[d, 2], p_ref.at[other * 4 + xi, :, cols[d]])
    c = remote(qy, ry, sem_y, partner)
    c.start()
    sends.append(c)
    sends += plane(yh, rm, sm, sem_m)
    remote(qy, ry, sem_y, partner).wait_recv()
    own_p = p_ref.at[yh * 4 + xi]
    cap = o_ref.shape[1]
    for b in range(nw):
        rows = pl.ds(b * cap, cap)
        for d in (0, 1):
            total = rm[d, 2, rows, :].astype(jnp.float32) + own_p[rows, cols[d]].astype(jnp.float32)
            o_ref[b, :, cols[d]] = (total + ry[rows, cols[d]].astype(jnp.float32)).astype(o_ref.dtype)
    own = pltpu.make_async_copy(o_ref.at[w], r_ref.at[w], own_w)
    own.start()

    def wide_copy(k, peer, origin):
        return pltpu.make_async_remote_copy(
            src_ref=o_ref.at[peer],
            dst_ref=r_ref.at[origin],
            send_sem=sem_w.at[k, 0],
            recv_sem=sem_w.at[k, 1],
            device_id=(peer, me),
            device_id_type=MESH,
        )

    def send_body(k, carry):
        wide_copy(k, (w + k) % nw, w).start()
        return carry

    lax.fori_loop(1, nw, send_body, 0)

    def recv_body(k, carry):
        src = (w + nw - k) % nw
        wide_copy(k, src, src).wait_recv()
        return carry

    lax.fori_loop(1, nw, recv_body, 0)

    def sent_body(k, carry):
        wide_copy(k, (w + k) % nw, w).wait_send()
        return carry

    lax.fori_loop(1, nw, sent_body, 0)
    own.wait()
    for c in sends:
        c.wait_send()


def _reduce(p, nw, collective_id):
    one = p.shape[1:]
    blocks = (nw, one[0] // nw, one[1])
    block = pltpu.VMEM(one, p.dtype)
    return pl.pallas_call(
        _reduce_kernel,
        out_shape=jax.ShapeDtypeStruct(blocks, p.dtype),
        in_specs=[pl.BlockSpec(memory_space=pltpu.VMEM)],
        out_specs=pl.BlockSpec(memory_space=pl.ANY),
        scratch_shapes=[
            pltpu.VMEM((2, 3, one[0], one[1] // 2), p.dtype),
            pltpu.VMEM((2, 3, one[0], one[1] // 2), p.dtype),
            pltpu.VMEM((2, 2, one[0], one[1] // 2), p.dtype),
            pltpu.VMEM((2, 2, one[0], one[1] // 2), p.dtype),
            block,
            block,
            pltpu.VMEM(blocks, p.dtype),
            pltpu.SemaphoreType.DMA((2, 3, 2)),
            pltpu.SemaphoreType.DMA((2, 3, 2)),
            pltpu.SemaphoreType.DMA((2,)),
            pltpu.SemaphoreType.DMA((nw, 2)),
            pltpu.SemaphoreType.DMA(()),
        ],
        compiler_params=pltpu.CompilerParams(collective_id=collective_id, has_side_effects=True),
        cost_estimate=pl.CostEstimate(
            flops=2 * p.size, bytes_accessed=2 * p.size * p.dtype.itemsize, transcendentals=0
        ),
    )(p)


def _exchange(x, n_peers, gather, collective_id, axis="narrow"):
    if gather:
        out_shape = (n_peers,) + x.shape
        pick_src = lambda ref, i: ref
    else:
        out_shape = x.shape
        pick_src = lambda ref, i: ref.at[i]
    nbytes = x.size * x.dtype.itemsize
    return pl.pallas_call(
        lambda *refs: _exchange_kernel(n_peers, pick_src, axis, *refs),
        out_shape=jax.ShapeDtypeStruct(out_shape, x.dtype),
        in_specs=[pl.BlockSpec(memory_space=pl.ANY)],
        out_specs=pl.BlockSpec(memory_space=pl.ANY),
        scratch_shapes=[
            pltpu.SemaphoreType.DMA((n_peers - 1,)),
            pltpu.SemaphoreType.DMA((n_peers - 1,)),
            pltpu.SemaphoreType.DMA(()),
        ],
        compiler_params=pltpu.CompilerParams(collective_id=collective_id, has_side_effects=True),
        cost_estimate=pl.CostEstimate(flops=0, bytes_accessed=2 * nbytes, transcendentals=0),
    )(x)


def local(tokens, expert_ids, route_weights, w_gate, w_up, w_down):
    tok_rows = expert_ids.shape[0]
    top_count = expert_ids.shape[1]
    local_experts = w_gate.shape[0]
    groups_wide = lax.axis_size("wide")
    experts_all = local_experts * groups_wide
    capacity = 7 * tok_rows * top_count // (6 * experts_all)
    slots_all = experts_all * capacity
    flat_ids = expert_ids.reshape(-1)
    onehot = (flat_ids[:, None] == jnp.arange(experts_all, dtype=jnp.int32)[None, :]).astype(
        jnp.int32
    )
    running = jnp.cumsum(onehot, axis=0)
    slot_index = jnp.sum(running * onehot, axis=1) - 1
    destination = (flat_ids * capacity + slot_index).reshape(tok_rows, top_count)
    hit = destination[:, :, None] == jnp.arange(slots_all, dtype=jnp.int32)[None, None, :]
    dispatch = jnp.any(hit, axis=1).astype(jnp.bfloat16)
    combine = jnp.sum(
        jnp.where(hit, route_weights.astype(jnp.float32)[:, :, None], 0.0), axis=1
    ).astype(jnp.bfloat16)
    dispatch = dispatch.reshape(tok_rows, groups_wide, capacity)
    combine = combine.reshape(tok_rows, groups_wide, capacity)
    outgoing = jnp.einsum(
        "tbc,td->bcd", dispatch, tokens, preferred_element_type=jnp.float32
    ).astype(jnp.bfloat16)
    n_narrow = lax.axis_size("narrow")
    width = tokens.shape[1]
    slot_rows = _dispatch(outgoing, n_narrow, 0)
    wg = w_gate[0].reshape(-1, n_narrow, width)
    wu = w_up[0].reshape(-1, n_narrow, width)
    wd = w_down[0].reshape(-1, n_narrow, width)
    gate_proj = jnp.einsum("nbcd,fnd->bcf", slot_rows, wg, preferred_element_type=jnp.float32)
    up_proj = jnp.einsum("nbcd,fnd->bcf", slot_rows, wu, preferred_element_type=jnp.float32)
    hidden = (jax.nn.silu(gate_proj) * up_proj).astype(jnp.bfloat16)
    partial_value = jnp.einsum(
        "sf,fnd->nsd", hidden.reshape(slots_all, -1), wd, preferred_element_type=jnp.float32
    ).astype(jnp.bfloat16)
    returned = _reduce(partial_value, groups_wide, 1)
    mixed = jnp.einsum("tbc,bcd->td", combine, returned, preferred_element_type=jnp.float32)
    return mixed.astype(jnp.bfloat16)


def solution(mesh):
    in_specs = (
        P("wide", "narrow"),
        P("wide", None),
        P("wide", None),
        P("wide", "narrow", None),
        P("wide", "narrow", None),
        P("wide", "narrow", None),
    )
    out_specs = P("wide", "narrow")
    return jax.shard_map(local, mesh=mesh, in_specs=in_specs, out_specs=out_specs, check_vma=False)
```

```python
import types

import jax
import jax.numpy as jnp
from jax import lax
from jax.experimental import pallas as pl
from jax.experimental.pallas import tpu as pltpu
from jax.sharding import PartitionSpec as P

MESH = pl.DeviceIdType.MESH


def _exchange_kernel(n_peers, pick_src, axis, x_ref, y_ref, send_sem, recv_sem, own_sem):
    me = lax.axis_index(axis)
    other = lax.axis_index("wide" if axis == "narrow" else "narrow")
    if axis == "narrow":
        dev = lambda p: (other, p)
    else:
        dev = lambda p: (p, other)
    barrier = pltpu.get_barrier_semaphore()
    for k in range(1, n_peers):
        peer = lax.rem(me + k, n_peers)
        pl.semaphore_signal(barrier, inc=1, device_id=dev(peer), device_id_type=MESH)
    pl.semaphore_wait(barrier, n_peers - 1)
    own = pltpu.make_async_copy(pick_src(x_ref, me), y_ref.at[me], own_sem)
    own.start()
    copies = []
    for k in range(1, n_peers):
        peer = lax.rem(me + k, n_peers)
        c = pltpu.make_async_remote_copy(
            src_ref=pick_src(x_ref, peer),
            dst_ref=y_ref.at[me],
            send_sem=send_sem.at[k - 1],
            recv_sem=recv_sem.at[k - 1],
            device_id=dev(peer),
            device_id_type=MESH,
        )
        c.start()
        copies.append(c)
    for k in range(1, n_peers):
        src = lax.rem(me + n_peers - k, n_peers)
        pltpu.make_async_remote_copy(
            src_ref=pick_src(x_ref, src),
            dst_ref=y_ref.at[src],
            send_sem=send_sem.at[k - 1],
            recv_sem=recv_sem.at[k - 1],
            device_id=dev(src),
            device_id_type=MESH,
        ).wait_recv()
    for c in copies:
        c.wait_send()
    own.wait()


def _gather_chain(x_ref, slot_of, sem_y, sem_x1, sem_x2, own_sem, after_start=None):
    me = lax.axis_index("narrow")
    w = lax.axis_index("wide")
    yh = me // 4
    xi = me % 4
    partner = (1 - yh) * 4 + xi
    right = yh * 4 + (xi + 1) % 4
    left = yh * 4 + (xi + 3) % 4

    y_ref = types.SimpleNamespace(at=_Slots(slot_of))

    def remote(src, slot, sem, peer):
        return pltpu.make_async_remote_copy(
            src_ref=src,
            dst_ref=y_ref.at[slot],
            send_sem=sem[0],
            recv_sem=sem[1],
            device_id=(w, peer),
            device_id_type=MESH,
        )

    own = pltpu.make_async_copy(x_ref, y_ref.at[me], own_sem)
    own.start()
    cy = remote(x_ref, me, (sem_y.at[0], sem_y.at[1]), partner)
    cy.start()
    c1 = [
        remote(x_ref, me, (sem_x1.at[0, 0], sem_x1.at[0, 1]), right),
        remote(x_ref, me, (sem_x1.at[1, 0], sem_x1.at[1, 1]), left),
    ]
    for c in c1:
        c.start()
    if after_start is not None:
        after_start()
    remote(x_ref, partner, (sem_y.at[0], sem_y.at[1]), partner).wait_recv()
    c2 = [
        remote(y_ref.at[partner], partner, (sem_x1.at[2, 0], sem_x1.at[2, 1]), right),
        remote(y_ref.at[partner], partner, (sem_x1.at[3, 0], sem_x1.at[3, 1]), left),
    ]
    for c in c2:
        c.start()
    lp = (1 - yh) * 4 + (xi + 3) % 4
    rp = (1 - yh) * 4 + (xi + 1) % 4
    remote(x_ref, left, (sem_x1.at[0, 0], sem_x1.at[0, 1]), left).wait_recv()
    remote(x_ref, right, (sem_x1.at[1, 0], sem_x1.at[1, 1]), right).wait_recv()
    c3 = [
        remote(y_ref.at[left], left, (sem_x2.at[0, 0], sem_x2.at[0, 1]), right),
    ]
    c3[0].start()
    remote(x_ref, rp, (sem_x1.at[3, 0], sem_x1.at[3, 1]), right).wait_recv()
    c4 = remote(y_ref.at[rp], rp, (sem_x2.at[1, 0], sem_x2.at[1, 1]), left)
    c4.start()
    remote(x_ref, lp, (sem_x1.at[2, 0], sem_x1.at[2, 1]), left).wait_recv()
    far = yh * 4 + (xi + 2) % 4
    far_p = (1 - yh) * 4 + (xi + 2) % 4
    remote(x_ref, far, (sem_x2.at[0, 0], sem_x2.at[0, 1]), left).wait_recv()
    remote(x_ref, far_p, (sem_x2.at[1, 0], sem_x2.at[1, 1]), right).wait_recv()
    return [cy] + c1 + c2 + c3 + [c4], own


class _Slots:
    def __init__(self, fn):
        self.fn = fn

    def __getitem__(self, k):
        return self.fn(k)


def _narrow_peers():
    me = lax.axis_index("narrow")
    yh = me // 4
    xi = me % 4
    return ((1 - yh) * 4 + xi, yh * 4 + (xi + 1) % 4, yh * 4 + (xi + 3) % 4)


def _dispatch_kernel(x_ref, y_ref, r_ref, sem_w, own_w, sem_y, sem_x1, sem_x2, own_g):
    nw, _, cols = x_ref.shape
    halves = 2
    cw = cols // halves
    me_w = lax.axis_index("wide")
    me = lax.axis_index("narrow")
    barrier = pltpu.get_barrier_semaphore()

    def greet(k, carry):
        pl.semaphore_signal(barrier, inc=1, device_id=((me_w + k) % nw, me), device_id_type=MESH)
        return carry

    lax.fori_loop(1, nw, greet, 0)
    for peer in _narrow_peers():
        pl.semaphore_signal(barrier, inc=1, device_id=(me_w, peer), device_id_type=MESH)
    pl.semaphore_wait(barrier, nw - 1 + 3)

    def wide_copy(h, k, peer_of_copy, target):
        cs = pl.ds(h * cw, cw)
        return pltpu.make_async_remote_copy(
            src_ref=x_ref.at[peer_of_copy, :, cs],
            dst_ref=r_ref.at[target, :, cs],
            send_sem=sem_w.at[h, k, 0],
            recv_sem=sem_w.at[h, k, 1],
            device_id=(peer_of_copy, me),
            device_id_type=MESH,
        )

    def wide_start(h):
        cs = pl.ds(h * cw, cw)
        own = pltpu.make_async_copy(x_ref.at[me_w, :, cs], r_ref.at[me_w, :, cs], own_w.at[h])
        own.start()

        def body(k, carry):
            wide_copy(h, k, (me_w + k) % nw, me_w).start()
            return carry

        lax.fori_loop(1, nw, body, 0)
        return own

    def wide_wait(h, own):
        def body(k, carry):
            src = (me_w + nw - k) % nw
            pltpu.make_async_remote_copy(
                src_ref=x_ref.at[src, :, pl.ds(h * cw, cw)],
                dst_ref=r_ref.at[src, :, pl.ds(h * cw, cw)],
                send_sem=sem_w.at[h, k, 0],
                recv_sem=sem_w.at[h, k, 1],
                device_id=(src, me),
                device_id_type=MESH,
            ).wait_recv()
            return carry

        lax.fori_loop(1, nw, body, 0)
        own.wait()

    def wide_sent(h):
        def body(k, carry):
            wide_copy(h, k, (me_w + k) % nw, me_w).wait_send()
            return carry

        lax.fori_loop(1, nw, body, 0)

    pending = []
    own0 = wide_start(0)
    wide_wait(0, own0)
    owns = []
    for h in range(halves):
        if h == 1:
            wide_wait(1, owns[0])
        cs = pl.ds(h * cw, cw)
        sends, own = _gather_chain(
            r_ref.at[:, :, cs],
            lambda k, cs=cs: y_ref.at[k, :, :, cs],
            sem_y.at[h],
            sem_x1.at[h],
            sem_x2.at[h],
            own_g.at[h],
            (lambda: owns.append(wide_start(1))) if h == 0 else None,
        )
        pending.append((sends, own))
    for h in range(halves):
        wide_sent(h)
        sends, own = pending[h]
        for c in sends:
            c.wait_send()
        own.wait()


def _dispatch(x, n_narrow, collective_id):
    nw, rows, cols = x.shape
    return pl.pallas_call(
        _dispatch_kernel,
        out_shape=jax.ShapeDtypeStruct((n_narrow, nw, rows, cols), x.dtype),
        in_specs=[pl.BlockSpec(memory_space=pl.ANY)],
        out_specs=pl.BlockSpec(memory_space=pl.ANY),
        scratch_shapes=[
            pltpu.VMEM((nw, rows, cols), x.dtype),
            pltpu.SemaphoreType.DMA((2, nw, 2)),
            pltpu.SemaphoreType.DMA((2,)),
            pltpu.SemaphoreType.DMA((2, 2)),
            pltpu.SemaphoreType.DMA((2, 4, 2)),
            pltpu.SemaphoreType.DMA((2, 2, 2)),
            pltpu.SemaphoreType.DMA((2,)),
        ],
        compiler_params=pltpu.CompilerParams(collective_id=collective_id, has_side_effects=True),
        cost_estimate=pl.CostEstimate(
            flops=0, bytes_accessed=2 * (n_narrow + 1) * x.size * x.dtype.itemsize, transcendentals=0
        ),
    )(x)


def _add_into(dst, *srcs):
    rows_all = dst.shape[0]
    step = 128 if rows_all % 128 == 0 else rows_all

    def body(i, carry):
        rows = pl.ds(pl.multiple_of(i * step, step), step)
        total = srcs[0][rows].astype(jnp.float32)
        for src in srcs[1:]:
            total = total + src[rows].astype(jnp.float32)
        dst[rows] = total.astype(dst.dtype)
        return carry

    lax.fori_loop(0, rows_all // step, body, 0)


def _reduce_kernel(p_ref, r_ref, rp, rm, sp, sm, qy, ry, o_ref, sem_p, sem_m, sem_y, sem_w, own_w):
    me = lax.axis_index("narrow")
    w = lax.axis_index("wide")
    yh = me // 4
    xi = me % 4
    other = 1 - yh
    partner = other * 4 + xi
    right = yh * 4 + (xi + 1) % 4
    left = yh * 4 + (xi + 3) % 4
    nw = r_ref.shape[0]
    barrier = pltpu.get_barrier_semaphore()
    for peer in (partner, right, left):
        pl.semaphore_signal(barrier, inc=1, device_id=(w, peer), device_id_type=MESH)

    def greet(k, carry):
        pl.semaphore_signal(barrier, inc=1, device_id=((w + k) % nw, me), device_id_type=MESH)
        return carry

    lax.fori_loop(1, nw, greet, 0)
    pl.semaphore_wait(barrier, 3 + nw - 1)

    def remote(src, dst, sem, peer):
        return pltpu.make_async_remote_copy(
            src_ref=src,
            dst_ref=dst,
            send_sem=sem.at[0],
            recv_sem=sem.at[1],
            device_id=(w, peer),
            device_id_type=MESH,
        )

    half = p_ref.shape[2] // 2
    cols = (pl.ds(0, half), pl.ds(half, half))
    peers = (right, left)
    froms = (left, right)
    offsets = ((3, 2, 1), (1, 2, 3))
    cap = o_ref.shape[1]
    own_p = p_ref.at[yh * 4 + xi]

    def wide_copy(hf, k, peer, origin):
        return pltpu.make_async_remote_copy(
            src_ref=o_ref.at[peer, :, cols[hf]],
            dst_ref=r_ref.at[origin, :, cols[hf]],
            send_sem=sem_w.at[hf, k, 0],
            recv_sem=sem_w.at[hf, k, 1],
            device_id=(peer, me),
            device_id_type=MESH,
        )

    sends = []
    owns = []
    for hf in (0, 1):
        jobs = ((other, 0), (yh, 1))
        for j, (h, d) in enumerate(jobs):
            src = p_ref.at[h * 4 + (xi + offsets[d][0]) % 4, :, cols[hf]]
            c = remote(src, rp.at[hf, j, 0], sem_p.at[hf, j, 0], peers[d])
            c.start()
            sends.append(c)
        for step in (1, 2):
            for j, (h, d) in enumerate(jobs):
                remote(sp.at[hf, j, step - 1], rp.at[hf, j, step - 1], sem_p.at[hf, j, step - 1], froms[d]).wait_recv()
                term = p_ref.at[h * 4 + (xi + offsets[d][step]) % 4, :, cols[hf]]
                _add_into(sp.at[hf, j, step - 1], rp.at[hf, j, step - 1], term)
                c = remote(sp.at[hf, j, step - 1], rp.at[hf, j, step], sem_p.at[hf, j, step], peers[d])
                c.start()
                sends.append(c)
        remote(sp.at[hf, 0, 1], rp.at[hf, 0, 2], sem_p.at[hf, 0, 2], froms[0]).wait_recv()
        _add_into(qy.at[hf], rp.at[hf, 0, 2], p_ref.at[other * 4 + xi, :, cols[hf]])
        c = remote(qy.at[hf], ry.at[hf], sem_y.at[hf], partner)
        c.start()
        sends.append(c)
        remote(sp.at[hf, 1, 1], rp.at[hf, 1, 2], sem_p.at[hf, 1, 2], froms[1]).wait_recv()
        remote(qy.at[hf], ry.at[hf], sem_y.at[hf], partner).wait_recv()
        for b in range(nw):
            rows = pl.ds(b * cap, cap)
            total = rp[hf, 1, 2, rows, :].astype(jnp.float32) + own_p[rows, cols[hf]].astype(jnp.float32)
            o_ref[b, :, cols[hf]] = (total + ry[hf, rows, :].astype(jnp.float32)).astype(o_ref.dtype)
        own = pltpu.make_async_copy(o_ref.at[w, :, cols[hf]], r_ref.at[w, :, cols[hf]], own_w.at[hf])
        own.start()
        owns.append(own)

        def send_body(k, carry, hf=hf):
            wide_copy(hf, k, (w + k) % nw, w).start()
            return carry

        lax.fori_loop(1, nw, send_body, 0)

    for hf in (0, 1):

        def recv_body(k, carry, hf=hf):
            src = (w + nw - k) % nw
            wide_copy(hf, k, src, src).wait_recv()
            return carry

        lax.fori_loop(1, nw, recv_body, 0)

        def sent_body(k, carry, hf=hf):
            wide_copy(hf, k, (w + k) % nw, w).wait_send()
            return carry

        lax.fori_loop(1, nw, sent_body, 0)
        owns[hf].wait()
    for c in sends:
        c.wait_send()


def _reduce(p, nw, collective_id):
    one = p.shape[1:]
    blocks = (nw, one[0] // nw, one[1])
    block = pltpu.VMEM(one, p.dtype)
    return pl.pallas_call(
        _reduce_kernel,
        out_shape=jax.ShapeDtypeStruct(blocks, p.dtype),
        in_specs=[pl.BlockSpec(memory_space=pltpu.VMEM)],
        out_specs=pl.BlockSpec(memory_space=pl.ANY),
        scratch_shapes=[
            pltpu.VMEM((2, 2, 3, one[0], one[1] // 2), p.dtype),
            pltpu.VMEM((1,), p.dtype),
            pltpu.VMEM((2, 2, 2, one[0], one[1] // 2), p.dtype),
            pltpu.VMEM((1,), p.dtype),
            pltpu.VMEM((2, one[0], one[1] // 2), p.dtype),
            pltpu.VMEM((2, one[0], one[1] // 2), p.dtype),
            pltpu.VMEM(blocks, p.dtype),
            pltpu.SemaphoreType.DMA((2, 2, 3, 2)),
            pltpu.SemaphoreType.DMA((1,)),
            pltpu.SemaphoreType.DMA((2, 2)),
            pltpu.SemaphoreType.DMA((2, nw, 2)),
            pltpu.SemaphoreType.DMA((2,)),
        ],
        compiler_params=pltpu.CompilerParams(collective_id=collective_id, has_side_effects=True),
        cost_estimate=pl.CostEstimate(
            flops=2 * p.size, bytes_accessed=2 * p.size * p.dtype.itemsize, transcendentals=0
        ),
    )(p)


def _exchange(x, n_peers, gather, collective_id, axis="narrow"):
    if gather:
        out_shape = (n_peers,) + x.shape
        pick_src = lambda ref, i: ref
    else:
        out_shape = x.shape
        pick_src = lambda ref, i: ref.at[i]
    nbytes = x.size * x.dtype.itemsize
    return pl.pallas_call(
        lambda *refs: _exchange_kernel(n_peers, pick_src, axis, *refs),
        out_shape=jax.ShapeDtypeStruct(out_shape, x.dtype),
        in_specs=[pl.BlockSpec(memory_space=pl.ANY)],
        out_specs=pl.BlockSpec(memory_space=pl.ANY),
        scratch_shapes=[
            pltpu.SemaphoreType.DMA((n_peers - 1,)),
            pltpu.SemaphoreType.DMA((n_peers - 1,)),
            pltpu.SemaphoreType.DMA(()),
        ],
        compiler_params=pltpu.CompilerParams(collective_id=collective_id, has_side_effects=True),
        cost_estimate=pl.CostEstimate(flops=0, bytes_accessed=2 * nbytes, transcendentals=0),
    )(x)


def local(tokens, expert_ids, route_weights, w_gate, w_up, w_down):
    tok_rows = expert_ids.shape[0]
    top_count = expert_ids.shape[1]
    local_experts = w_gate.shape[0]
    groups_wide = lax.axis_size("wide")
    experts_all = local_experts * groups_wide
    capacity = 7 * tok_rows * top_count // (6 * experts_all)
    slots_all = experts_all * capacity
    flat_ids = expert_ids.reshape(-1)
    onehot = (flat_ids[:, None] == jnp.arange(experts_all, dtype=jnp.int32)[None, :]).astype(
        jnp.int32
    )
    running = jnp.cumsum(onehot, axis=0)
    slot_index = jnp.sum(running * onehot, axis=1) - 1
    destination = (flat_ids * capacity + slot_index).reshape(tok_rows, top_count)
    hit = destination[:, :, None] == jnp.arange(slots_all, dtype=jnp.int32)[None, None, :]
    dispatch = jnp.any(hit, axis=1).astype(jnp.bfloat16)
    combine = jnp.sum(
        jnp.where(hit, route_weights.astype(jnp.float32)[:, :, None], 0.0), axis=1
    ).astype(jnp.bfloat16)
    dispatch = dispatch.reshape(tok_rows, groups_wide, capacity)
    combine = combine.reshape(tok_rows, groups_wide, capacity)
    outgoing = jnp.einsum(
        "tbc,td->bcd", dispatch, tokens, preferred_element_type=jnp.float32
    ).astype(jnp.bfloat16)
    n_narrow = lax.axis_size("narrow")
    width = tokens.shape[1]
    slot_rows = _dispatch(outgoing, n_narrow, 0)
    wg = w_gate[0].reshape(-1, n_narrow, width)
    wu = w_up[0].reshape(-1, n_narrow, width)
    wd = w_down[0].reshape(-1, n_narrow, width)
    gate_proj = jnp.einsum("nbcd,fnd->bcf", slot_rows, wg, preferred_element_type=jnp.float32)
    up_proj = jnp.einsum("nbcd,fnd->bcf", slot_rows, wu, preferred_element_type=jnp.float32)
    hidden = (jax.nn.silu(gate_proj) * up_proj).astype(jnp.bfloat16)
    partial_value = jnp.einsum(
        "sf,fnd->nsd", hidden.reshape(slots_all, -1), wd, preferred_element_type=jnp.float32
    ).astype(jnp.bfloat16)
    returned = _reduce(partial_value, groups_wide, 1)
    mixed = jnp.einsum("tbc,bcd->td", combine, returned, preferred_element_type=jnp.float32)
    return mixed.astype(jnp.bfloat16)


def solution(mesh):
    in_specs = (
        P("wide", "narrow"),
        P("wide", None),
        P("wide", None),
        P("wide", "narrow", None),
        P("wide", "narrow", None),
        P("wide", "narrow", None),
    )
    out_specs = P("wide", "narrow")
    return jax.shard_map(local, mesh=mesh, in_specs=in_specs, out_specs=out_specs, check_vma=False)
```

```python
import types

import jax
import jax.numpy as jnp
from jax import lax
from jax.experimental import pallas as pl
from jax.experimental.pallas import tpu as pltpu
from jax.sharding import PartitionSpec as P

MESH = pl.DeviceIdType.MESH


def _exchange_kernel(n_peers, pick_src, axis, x_ref, y_ref, send_sem, recv_sem, own_sem):
    me = lax.axis_index(axis)
    other = lax.axis_index("wide" if axis == "narrow" else "narrow")
    if axis == "narrow":
        dev = lambda p: (other, p)
    else:
        dev = lambda p: (p, other)
    barrier = pltpu.get_barrier_semaphore()
    for k in range(1, n_peers):
        peer = lax.rem(me + k, n_peers)
        pl.semaphore_signal(barrier, inc=1, device_id=dev(peer), device_id_type=MESH)
    pl.semaphore_wait(barrier, n_peers - 1)
    own = pltpu.make_async_copy(pick_src(x_ref, me), y_ref.at[me], own_sem)
    own.start()
    copies = []
    for k in range(1, n_peers):
        peer = lax.rem(me + k, n_peers)
        c = pltpu.make_async_remote_copy(
            src_ref=pick_src(x_ref, peer),
            dst_ref=y_ref.at[me],
            send_sem=send_sem.at[k - 1],
            recv_sem=recv_sem.at[k - 1],
            device_id=dev(peer),
            device_id_type=MESH,
        )
        c.start()
        copies.append(c)
    for k in range(1, n_peers):
        src = lax.rem(me + n_peers - k, n_peers)
        pltpu.make_async_remote_copy(
            src_ref=pick_src(x_ref, src),
            dst_ref=y_ref.at[src],
            send_sem=send_sem.at[k - 1],
            recv_sem=recv_sem.at[k - 1],
            device_id=dev(src),
            device_id_type=MESH,
        ).wait_recv()
    for c in copies:
        c.wait_send()
    own.wait()


def _gather_chain(x_ref, slot_of, sem_y, sem_x1, sem_x2, own_sem, after_start=None):
    me = lax.axis_index("narrow")
    w = lax.axis_index("wide")
    yh = me // 4
    xi = me % 4
    partner = (1 - yh) * 4 + xi
    right = yh * 4 + (xi + 1) % 4
    left = yh * 4 + (xi + 3) % 4

    y_ref = types.SimpleNamespace(at=_Slots(slot_of))

    def remote(src, slot, sem, peer):
        return pltpu.make_async_remote_copy(
            src_ref=src,
            dst_ref=y_ref.at[slot],
            send_sem=sem[0],
            recv_sem=sem[1],
            device_id=(w, peer),
            device_id_type=MESH,
        )

    own = pltpu.make_async_copy(x_ref, y_ref.at[me], own_sem)
    own.start()
    cy = remote(x_ref, me, (sem_y.at[0], sem_y.at[1]), partner)
    cy.start()
    c1 = [
        remote(x_ref, me, (sem_x1.at[0, 0], sem_x1.at[0, 1]), right),
        remote(x_ref, me, (sem_x1.at[1, 0], sem_x1.at[1, 1]), left),
    ]
    for c in c1:
        c.start()
    remote(x_ref, partner, (sem_y.at[0], sem_y.at[1]), partner).wait_recv()
    c2 = [
        remote(y_ref.at[partner], partner, (sem_x1.at[2, 0], sem_x1.at[2, 1]), right),
        remote(y_ref.at[partner], partner, (sem_x1.at[3, 0], sem_x1.at[3, 1]), left),
    ]
    for c in c2:
        c.start()
    if after_start is not None:
        after_start()
    lp = (1 - yh) * 4 + (xi + 3) % 4
    rp = (1 - yh) * 4 + (xi + 1) % 4
    remote(x_ref, left, (sem_x1.at[0, 0], sem_x1.at[0, 1]), left).wait_recv()
    remote(x_ref, right, (sem_x1.at[1, 0], sem_x1.at[1, 1]), right).wait_recv()
    c3 = [
        remote(y_ref.at[left], left, (sem_x2.at[0, 0], sem_x2.at[0, 1]), right),
    ]
    c3[0].start()
    remote(x_ref, rp, (sem_x1.at[3, 0], sem_x1.at[3, 1]), right).wait_recv()
    c4 = remote(y_ref.at[rp], rp, (sem_x2.at[1, 0], sem_x2.at[1, 1]), left)
    c4.start()
    remote(x_ref, lp, (sem_x1.at[2, 0], sem_x1.at[2, 1]), left).wait_recv()
    far = yh * 4 + (xi + 2) % 4
    far_p = (1 - yh) * 4 + (xi + 2) % 4
    remote(x_ref, far, (sem_x2.at[0, 0], sem_x2.at[0, 1]), left).wait_recv()
    remote(x_ref, far_p, (sem_x2.at[1, 0], sem_x2.at[1, 1]), right).wait_recv()
    return [cy] + c1 + c2 + c3 + [c4], own


class _Slots:
    def __init__(self, fn):
        self.fn = fn

    def __getitem__(self, k):
        return self.fn(k)


def _narrow_peers():
    me = lax.axis_index("narrow")
    yh = me // 4
    xi = me % 4
    return ((1 - yh) * 4 + xi, yh * 4 + (xi + 1) % 4, yh * 4 + (xi + 3) % 4)


def _dispatch_kernel(x_ref, y_ref, r_ref, sem_w, own_w, sem_y, sem_x1, sem_x2, own_g):
    nw, _, cols = x_ref.shape
    halves = 2
    cw = cols // halves
    me_w = lax.axis_index("wide")
    me = lax.axis_index("narrow")
    barrier = pltpu.get_barrier_semaphore()

    def greet(k, carry):
        pl.semaphore_signal(barrier, inc=1, device_id=((me_w + k) % nw, me), device_id_type=MESH)
        return carry

    lax.fori_loop(1, nw, greet, 0)
    for peer in _narrow_peers():
        pl.semaphore_signal(barrier, inc=1, device_id=(me_w, peer), device_id_type=MESH)
    pl.semaphore_wait(barrier, nw - 1 + 3)

    def wide_copy(h, k, peer_of_copy, target):
        cs = pl.ds(h * cw, cw)
        return pltpu.make_async_remote_copy(
            src_ref=x_ref.at[peer_of_copy, :, cs],
            dst_ref=r_ref.at[target, :, cs],
            send_sem=sem_w.at[h, k, 0],
            recv_sem=sem_w.at[h, k, 1],
            device_id=(peer_of_copy, me),
            device_id_type=MESH,
        )

    def wide_start(h):
        cs = pl.ds(h * cw, cw)
        own = pltpu.make_async_copy(x_ref.at[me_w, :, cs], r_ref.at[me_w, :, cs], own_w.at[h])
        own.start()

        def body(k, carry):
            wide_copy(h, k, (me_w + k) % nw, me_w).start()
            return carry

        lax.fori_loop(1, nw, body, 0)
        return own

    def wide_wait(h, own):
        def body(k, carry):
            src = (me_w + nw - k) % nw
            pltpu.make_async_remote_copy(
                src_ref=x_ref.at[src, :, pl.ds(h * cw, cw)],
                dst_ref=r_ref.at[src, :, pl.ds(h * cw, cw)],
                send_sem=sem_w.at[h, k, 0],
                recv_sem=sem_w.at[h, k, 1],
                device_id=(src, me),
                device_id_type=MESH,
            ).wait_recv()
            return carry

        lax.fori_loop(1, nw, body, 0)
        own.wait()

    def wide_sent(h):
        def body(k, carry):
            wide_copy(h, k, (me_w + k) % nw, me_w).wait_send()
            return carry

        lax.fori_loop(1, nw, body, 0)

    pending = []
    own0 = wide_start(0)
    wide_wait(0, own0)
    owns = []
    for h in range(halves):
        if h == 1:
            wide_wait(1, owns[0])
        cs = pl.ds(h * cw, cw)
        sends, own = _gather_chain(
            r_ref.at[:, :, cs],
            lambda k, cs=cs: y_ref.at[k, :, :, cs],
            sem_y.at[h],
            sem_x1.at[h],
            sem_x2.at[h],
            own_g.at[h],
            (lambda: owns.append(wide_start(1))) if h == 0 else None,
        )
        pending.append((sends, own))
    for h in range(halves):
        wide_sent(h)
        sends, own = pending[h]
        for c in sends:
            c.wait_send()
        own.wait()


def _dispatch(x, n_narrow, collective_id):
    nw, rows, cols = x.shape
    return pl.pallas_call(
        _dispatch_kernel,
        out_shape=jax.ShapeDtypeStruct((n_narrow, nw, rows, cols), x.dtype),
        in_specs=[pl.BlockSpec(memory_space=pl.ANY)],
        out_specs=pl.BlockSpec(memory_space=pl.ANY),
        scratch_shapes=[
            pltpu.VMEM((nw, rows, cols), x.dtype),
            pltpu.SemaphoreType.DMA((2, nw, 2)),
            pltpu.SemaphoreType.DMA((2,)),
            pltpu.SemaphoreType.DMA((2, 2)),
            pltpu.SemaphoreType.DMA((2, 4, 2)),
            pltpu.SemaphoreType.DMA((2, 2, 2)),
            pltpu.SemaphoreType.DMA((2,)),
        ],
        compiler_params=pltpu.CompilerParams(collective_id=collective_id, has_side_effects=True),
        cost_estimate=pl.CostEstimate(
            flops=0, bytes_accessed=2 * (n_narrow + 1) * x.size * x.dtype.itemsize, transcendentals=0
        ),
    )(x)


def _add_into(dst, *srcs):
    rows_all = dst.shape[0]
    step = 128 if rows_all % 128 == 0 else rows_all

    def body(i, carry):
        rows = pl.ds(pl.multiple_of(i * step, step), step)
        total = srcs[0][rows].astype(jnp.float32)
        for src in srcs[1:]:
            total = total + src[rows].astype(jnp.float32)
        dst[rows] = total.astype(dst.dtype)
        return carry

    lax.fori_loop(0, rows_all // step, body, 0)


def _reduce_kernel(p_ref, r_ref, rp, rm, sp, sm, qy, ry, o_ref, sem_p, sem_m, sem_y, sem_w, own_w):
    me = lax.axis_index("narrow")
    w = lax.axis_index("wide")
    yh = me // 4
    xi = me % 4
    other = 1 - yh
    partner = other * 4 + xi
    right = yh * 4 + (xi + 1) % 4
    left = yh * 4 + (xi + 3) % 4
    nw = r_ref.shape[0]
    barrier = pltpu.get_barrier_semaphore()
    for peer in (partner, right, left):
        pl.semaphore_signal(barrier, inc=1, device_id=(w, peer), device_id_type=MESH)

    def greet(k, carry):
        pl.semaphore_signal(barrier, inc=1, device_id=((w + k) % nw, me), device_id_type=MESH)
        return carry

    lax.fori_loop(1, nw, greet, 0)
    pl.semaphore_wait(barrier, 3 + nw - 1)

    def remote(src, dst, sem, peer):
        return pltpu.make_async_remote_copy(
            src_ref=src,
            dst_ref=dst,
            send_sem=sem.at[0],
            recv_sem=sem.at[1],
            device_id=(w, peer),
            device_id_type=MESH,
        )

    half = p_ref.shape[2] // 2
    cols = (pl.ds(0, half), pl.ds(half, half))
    peers = (right, left)
    froms = (left, right)
    offsets = ((3, 2, 1), (1, 2, 3))

    def plane(h, rb, sb, sem):
        sends = []
        for d in (0, 1):
            src = p_ref.at[h * 4 + (xi + offsets[d][0]) % 4, :, cols[d]]
            c = remote(src, rb.at[d, 0], sem.at[d, 0], peers[d])
            c.start()
            sends.append(c)
        for step in (1, 2):
            for d in (0, 1):
                remote(sb.at[d, step - 1], rb.at[d, step - 1], sem.at[d, step - 1], froms[d]).wait_recv()
                term = p_ref.at[h * 4 + (xi + offsets[d][step]) % 4, :, cols[d]]
                _add_into(sb.at[d, step - 1], rb.at[d, step - 1], term)
                c = remote(sb.at[d, step - 1], rb.at[d, step], sem.at[d, step], peers[d])
                c.start()
                sends.append(c)
        for d in (0, 1):
            remote(sb.at[d, 1], rb.at[d, 2], sem.at[d, 2], froms[d]).wait_recv()
        return sends

    sends = plane(other, rp, sp, sem_p)
    for d in (0, 1):
        _add_into(qy.at[:, cols[d]], rp.at[d, 2], p_ref.at[other * 4 + xi, :, cols[d]])
    c = remote(qy, ry, sem_y, partner)
    c.start()
    sends.append(c)
    sends += plane(yh, rm, sm, sem_m)
    remote(qy, ry, sem_y, partner).wait_recv()
    own_p = p_ref.at[yh * 4 + xi]
    cap = o_ref.shape[1]
    for b in range(nw):
        rows = pl.ds(b * cap, cap)
        for d in (0, 1):
            total = rm[d, 2, rows, :].astype(jnp.float32) + own_p[rows, cols[d]].astype(jnp.float32)
            o_ref[b, :, cols[d]] = (total + ry[rows, cols[d]].astype(jnp.float32)).astype(o_ref.dtype)
    own = pltpu.make_async_copy(o_ref.at[w], r_ref.at[w], own_w)
    own.start()

    def wide_copy(k, peer, origin):
        return pltpu.make_async_remote_copy(
            src_ref=o_ref.at[peer],
            dst_ref=r_ref.at[origin],
            send_sem=sem_w.at[k, 0],
            recv_sem=sem_w.at[k, 1],
            device_id=(peer, me),
            device_id_type=MESH,
        )

    def send_body(k, carry):
        wide_copy(k, (w + k) % nw, w).start()
        return carry

    lax.fori_loop(1, nw, send_body, 0)

    def recv_body(k, carry):
        src = (w + nw - k) % nw
        wide_copy(k, src, src).wait_recv()
        return carry

    lax.fori_loop(1, nw, recv_body, 0)

    def sent_body(k, carry):
        wide_copy(k, (w + k) % nw, w).wait_send()
        return carry

    lax.fori_loop(1, nw, sent_body, 0)
    own.wait()
    for c in sends:
        c.wait_send()


def _reduce(p, nw, collective_id):
    one = p.shape[1:]
    blocks = (nw, one[0] // nw, one[1])
    block = pltpu.VMEM(one, p.dtype)
    return pl.pallas_call(
        _reduce_kernel,
        out_shape=jax.ShapeDtypeStruct(blocks, p.dtype),
        in_specs=[pl.BlockSpec(memory_space=pltpu.VMEM)],
        out_specs=pl.BlockSpec(memory_space=pl.ANY),
        scratch_shapes=[
            pltpu.VMEM((2, 3, one[0], one[1] // 2), p.dtype),
            pltpu.VMEM((2, 3, one[0], one[1] // 2), p.dtype),
            pltpu.VMEM((2, 2, one[0], one[1] // 2), p.dtype),
            pltpu.VMEM((2, 2, one[0], one[1] // 2), p.dtype),
            block,
            block,
            pltpu.VMEM(blocks, p.dtype),
            pltpu.SemaphoreType.DMA((2, 3, 2)),
            pltpu.SemaphoreType.DMA((2, 3, 2)),
            pltpu.SemaphoreType.DMA((2,)),
            pltpu.SemaphoreType.DMA((nw, 2)),
            pltpu.SemaphoreType.DMA(()),
        ],
        compiler_params=pltpu.CompilerParams(collective_id=collective_id, has_side_effects=True),
        cost_estimate=pl.CostEstimate(
            flops=2 * p.size, bytes_accessed=2 * p.size * p.dtype.itemsize, transcendentals=0
        ),
    )(p)


def _exchange(x, n_peers, gather, collective_id, axis="narrow"):
    if gather:
        out_shape = (n_peers,) + x.shape
        pick_src = lambda ref, i: ref
    else:
        out_shape = x.shape
        pick_src = lambda ref, i: ref.at[i]
    nbytes = x.size * x.dtype.itemsize
    return pl.pallas_call(
        lambda *refs: _exchange_kernel(n_peers, pick_src, axis, *refs),
        out_shape=jax.ShapeDtypeStruct(out_shape, x.dtype),
        in_specs=[pl.BlockSpec(memory_space=pl.ANY)],
        out_specs=pl.BlockSpec(memory_space=pl.ANY),
        scratch_shapes=[
            pltpu.SemaphoreType.DMA((n_peers - 1,)),
            pltpu.SemaphoreType.DMA((n_peers - 1,)),
            pltpu.SemaphoreType.DMA(()),
        ],
        compiler_params=pltpu.CompilerParams(collective_id=collective_id, has_side_effects=True),
        cost_estimate=pl.CostEstimate(flops=0, bytes_accessed=2 * nbytes, transcendentals=0),
    )(x)


def local(tokens, expert_ids, route_weights, w_gate, w_up, w_down):
    tok_rows = expert_ids.shape[0]
    top_count = expert_ids.shape[1]
    local_experts = w_gate.shape[0]
    groups_wide = lax.axis_size("wide")
    experts_all = local_experts * groups_wide
    capacity = 7 * tok_rows * top_count // (6 * experts_all)
    slots_all = experts_all * capacity
    flat_ids = expert_ids.reshape(-1)
    onehot = (flat_ids[:, None] == jnp.arange(experts_all, dtype=jnp.int32)[None, :]).astype(
        jnp.int32
    )
    running = jnp.cumsum(onehot, axis=0)
    slot_index = jnp.sum(running * onehot, axis=1) - 1
    destination = (flat_ids * capacity + slot_index).reshape(tok_rows, top_count)
    hit = destination[:, :, None] == jnp.arange(slots_all, dtype=jnp.int32)[None, None, :]
    dispatch = jnp.any(hit, axis=1).astype(jnp.bfloat16)
    combine = jnp.sum(
        jnp.where(hit, route_weights.astype(jnp.float32)[:, :, None], 0.0), axis=1
    ).astype(jnp.bfloat16)
    dispatch = dispatch.reshape(tok_rows, groups_wide, capacity)
    combine = combine.reshape(tok_rows, groups_wide, capacity)
    outgoing = jnp.einsum(
        "tbc,td->bcd", dispatch, tokens, preferred_element_type=jnp.float32
    ).astype(jnp.bfloat16)
    n_narrow = lax.axis_size("narrow")
    width = tokens.shape[1]
    slot_rows = _dispatch(outgoing, n_narrow, 0)
    wg = w_gate[0].reshape(-1, n_narrow, width)
    wu = w_up[0].reshape(-1, n_narrow, width)
    wd = w_down[0].reshape(-1, n_narrow, width)
    gate_proj = jnp.einsum("nbcd,fnd->bcf", slot_rows, wg, preferred_element_type=jnp.float32)
    up_proj = jnp.einsum("nbcd,fnd->bcf", slot_rows, wu, preferred_element_type=jnp.float32)
    hidden = (jax.nn.silu(gate_proj) * up_proj).astype(jnp.bfloat16)
    partial_value = jnp.einsum(
        "sf,fnd->nsd", hidden.reshape(slots_all, -1), wd, preferred_element_type=jnp.float32
    ).astype(jnp.bfloat16)
    returned = _reduce(partial_value, groups_wide, 1)
    mixed = jnp.einsum("tbc,bcd->td", combine, returned, preferred_element_type=jnp.float32)
    return mixed.astype(jnp.bfloat16)


def solution(mesh):
    in_specs = (
        P("wide", "narrow"),
        P("wide", None),
        P("wide", None),
        P("wide", "narrow", None),
        P("wide", "narrow", None),
        P("wide", "narrow", None),
    )
    out_specs = P("wide", "narrow")
    return jax.shard_map(local, mesh=mesh, in_specs=in_specs, out_specs=out_specs, check_vma=False)
```

```python
import types

import jax
import jax.numpy as jnp
from jax import lax
from jax.experimental import pallas as pl
from jax.experimental.pallas import tpu as pltpu
from jax.sharding import PartitionSpec as P

MESH = pl.DeviceIdType.MESH


def _exchange_kernel(n_peers, pick_src, axis, x_ref, y_ref, send_sem, recv_sem, own_sem):
    me = lax.axis_index(axis)
    other = lax.axis_index("wide" if axis == "narrow" else "narrow")
    if axis == "narrow":
        dev = lambda p: (other, p)
    else:
        dev = lambda p: (p, other)
    barrier = pltpu.get_barrier_semaphore()
    for k in range(1, n_peers):
        peer = lax.rem(me + k, n_peers)
        pl.semaphore_signal(barrier, inc=1, device_id=dev(peer), device_id_type=MESH)
    pl.semaphore_wait(barrier, n_peers - 1)
    own = pltpu.make_async_copy(pick_src(x_ref, me), y_ref.at[me], own_sem)
    own.start()
    copies = []
    for k in range(1, n_peers):
        peer = lax.rem(me + k, n_peers)
        c = pltpu.make_async_remote_copy(
            src_ref=pick_src(x_ref, peer),
            dst_ref=y_ref.at[me],
            send_sem=send_sem.at[k - 1],
            recv_sem=recv_sem.at[k - 1],
            device_id=dev(peer),
            device_id_type=MESH,
        )
        c.start()
        copies.append(c)
    for k in range(1, n_peers):
        src = lax.rem(me + n_peers - k, n_peers)
        pltpu.make_async_remote_copy(
            src_ref=pick_src(x_ref, src),
            dst_ref=y_ref.at[src],
            send_sem=send_sem.at[k - 1],
            recv_sem=recv_sem.at[k - 1],
            device_id=dev(src),
            device_id_type=MESH,
        ).wait_recv()
    for c in copies:
        c.wait_send()
    own.wait()


def _gather_chain(x_ref, slot_of, sem_y, sem_x1, sem_x2, own_sem, after_start=None):
    me = lax.axis_index("narrow")
    w = lax.axis_index("wide")
    yh = me // 4
    xi = me % 4
    partner = (1 - yh) * 4 + xi
    right = yh * 4 + (xi + 1) % 4
    left = yh * 4 + (xi + 3) % 4

    y_ref = types.SimpleNamespace(at=_Slots(slot_of))

    def remote(src, slot, sem, peer):
        return pltpu.make_async_remote_copy(
            src_ref=src,
            dst_ref=y_ref.at[slot],
            send_sem=sem[0],
            recv_sem=sem[1],
            device_id=(w, peer),
            device_id_type=MESH,
        )

    own = pltpu.make_async_copy(x_ref, y_ref.at[me], own_sem)
    own.start()
    cy = remote(x_ref, me, (sem_y.at[0], sem_y.at[1]), partner)
    cy.start()
    c1 = [
        remote(x_ref, me, (sem_x1.at[0, 0], sem_x1.at[0, 1]), right),
        remote(x_ref, me, (sem_x1.at[1, 0], sem_x1.at[1, 1]), left),
    ]
    for c in c1:
        c.start()
    if after_start is not None:
        after_start()
    remote(x_ref, partner, (sem_y.at[0], sem_y.at[1]), partner).wait_recv()
    c2 = [
        remote(y_ref.at[partner], partner, (sem_x1.at[2, 0], sem_x1.at[2, 1]), right),
        remote(y_ref.at[partner], partner, (sem_x1.at[3, 0], sem_x1.at[3, 1]), left),
    ]
    for c in c2:
        c.start()
    lp = (1 - yh) * 4 + (xi + 3) % 4
    rp = (1 - yh) * 4 + (xi + 1) % 4
    remote(x_ref, left, (sem_x1.at[0, 0], sem_x1.at[0, 1]), left).wait_recv()
    remote(x_ref, right, (sem_x1.at[1, 0], sem_x1.at[1, 1]), right).wait_recv()
    c3 = [
        remote(y_ref.at[left], left, (sem_x2.at[0, 0], sem_x2.at[0, 1]), right),
    ]
    c3[0].start()
    remote(x_ref, rp, (sem_x1.at[3, 0], sem_x1.at[3, 1]), right).wait_recv()
    c4 = remote(y_ref.at[rp], rp, (sem_x2.at[1, 0], sem_x2.at[1, 1]), left)
    c4.start()
    remote(x_ref, lp, (sem_x1.at[2, 0], sem_x1.at[2, 1]), left).wait_recv()
    far = yh * 4 + (xi + 2) % 4
    far_p = (1 - yh) * 4 + (xi + 2) % 4
    remote(x_ref, far, (sem_x2.at[0, 0], sem_x2.at[0, 1]), left).wait_recv()
    remote(x_ref, far_p, (sem_x2.at[1, 0], sem_x2.at[1, 1]), right).wait_recv()
    return [cy] + c1 + c2 + c3 + [c4], own


class _Slots:
    def __init__(self, fn):
        self.fn = fn

    def __getitem__(self, k):
        return self.fn(k)


def _narrow_peers():
    me = lax.axis_index("narrow")
    yh = me // 4
    xi = me % 4
    return ((1 - yh) * 4 + xi, yh * 4 + (xi + 1) % 4, yh * 4 + (xi + 3) % 4)


def _dispatch_kernel(x_ref, y_ref, r_ref, sem_w, own_w, sem_y, sem_x1, sem_x2, own_g):
    nw, _, cols = x_ref.shape
    halves = 2
    cw = cols // halves
    me_w = lax.axis_index("wide")
    me = lax.axis_index("narrow")
    barrier = pltpu.get_barrier_semaphore()

    def greet(k, carry):
        pl.semaphore_signal(barrier, inc=1, device_id=((me_w + k) % nw, me), device_id_type=MESH)
        return carry

    lax.fori_loop(1, nw, greet, 0)
    for peer in _narrow_peers():
        pl.semaphore_signal(barrier, inc=1, device_id=(me_w, peer), device_id_type=MESH)
    pl.semaphore_wait(barrier, nw - 1 + 3)

    def wide_copy(h, k, peer_of_copy, target):
        cs = pl.ds(h * cw, cw)
        return pltpu.make_async_remote_copy(
            src_ref=x_ref.at[peer_of_copy, :, cs],
            dst_ref=r_ref.at[target, :, cs],
            send_sem=sem_w.at[h, k, 0],
            recv_sem=sem_w.at[h, k, 1],
            device_id=(peer_of_copy, me),
            device_id_type=MESH,
        )

    def wide_start(h):
        cs = pl.ds(h * cw, cw)
        own = pltpu.make_async_copy(x_ref.at[me_w, :, cs], r_ref.at[me_w, :, cs], own_w.at[h])
        own.start()

        def body(k, carry):
            wide_copy(h, k, (me_w + k) % nw, me_w).start()
            return carry

        lax.fori_loop(1, nw, body, 0)
        return own

    def wide_wait(h, own):
        def body(k, carry):
            src = (me_w + nw - k) % nw
            pltpu.make_async_remote_copy(
                src_ref=x_ref.at[src, :, pl.ds(h * cw, cw)],
                dst_ref=r_ref.at[src, :, pl.ds(h * cw, cw)],
                send_sem=sem_w.at[h, k, 0],
                recv_sem=sem_w.at[h, k, 1],
                device_id=(src, me),
                device_id_type=MESH,
            ).wait_recv()
            return carry

        lax.fori_loop(1, nw, body, 0)
        own.wait()

    def wide_sent(h):
        def body(k, carry):
            wide_copy(h, k, (me_w + k) % nw, me_w).wait_send()
            return carry

        lax.fori_loop(1, nw, body, 0)

    pending = []
    own0 = wide_start(0)
    wide_wait(0, own0)
    owns = []
    for h in range(halves):
        if h == 1:
            wide_wait(1, owns[0])
        cs = pl.ds(h * cw, cw)
        sends, own = _gather_chain(
            r_ref.at[:, :, cs],
            lambda k, cs=cs: y_ref.at[k, :, :, cs],
            sem_y.at[h],
            sem_x1.at[h],
            sem_x2.at[h],
            own_g.at[h],
            (lambda: owns.append(wide_start(1))) if h == 0 else None,
        )
        pending.append((sends, own))
    for h in range(halves):
        wide_sent(h)
        sends, own = pending[h]
        for c in sends:
            c.wait_send()
        own.wait()


def _dispatch(x, n_narrow, collective_id):
    nw, rows, cols = x.shape
    return pl.pallas_call(
        _dispatch_kernel,
        out_shape=jax.ShapeDtypeStruct((n_narrow, nw, rows, cols), x.dtype),
        in_specs=[pl.BlockSpec(memory_space=pl.ANY)],
        out_specs=pl.BlockSpec(memory_space=pl.ANY),
        scratch_shapes=[
            pltpu.VMEM((nw, rows, cols), x.dtype),
            pltpu.SemaphoreType.DMA((2, nw, 2)),
            pltpu.SemaphoreType.DMA((2,)),
            pltpu.SemaphoreType.DMA((2, 2)),
            pltpu.SemaphoreType.DMA((2, 4, 2)),
            pltpu.SemaphoreType.DMA((2, 2, 2)),
            pltpu.SemaphoreType.DMA((2,)),
        ],
        compiler_params=pltpu.CompilerParams(collective_id=collective_id, has_side_effects=True),
        cost_estimate=pl.CostEstimate(
            flops=0, bytes_accessed=2 * (n_narrow + 1) * x.size * x.dtype.itemsize, transcendentals=0
        ),
    )(x)


def _add_into(dst, *srcs):
    rows_all = dst.shape[0]
    step = 128 if rows_all % 128 == 0 else rows_all

    def body(i, carry):
        rows = pl.ds(pl.multiple_of(i * step, step), step)
        total = srcs[0][rows].astype(jnp.float32)
        for src in srcs[1:]:
            total = total + src[rows].astype(jnp.float32)
        dst[rows] = total.astype(dst.dtype)
        return carry

    lax.fori_loop(0, rows_all // step, body, 0)


def _reduce_kernel(p_ref, r_ref, rp, rm, sp, sm, qy, ry, o_ref, sem_p, sem_m, sem_y, sem_w, own_w):
    me = lax.axis_index("narrow")
    w = lax.axis_index("wide")
    yh = me // 4
    xi = me % 4
    other = 1 - yh
    partner = other * 4 + xi
    right = yh * 4 + (xi + 1) % 4
    left = yh * 4 + (xi + 3) % 4
    nw = r_ref.shape[0]
    barrier = pltpu.get_barrier_semaphore()
    for peer in (partner, right, left):
        pl.semaphore_signal(barrier, inc=1, device_id=(w, peer), device_id_type=MESH)

    def greet(k, carry):
        pl.semaphore_signal(barrier, inc=1, device_id=((w + k) % nw, me), device_id_type=MESH)
        return carry

    lax.fori_loop(1, nw, greet, 0)
    pl.semaphore_wait(barrier, 3 + nw - 1)

    def remote(src, dst, sem, peer):
        return pltpu.make_async_remote_copy(
            src_ref=src,
            dst_ref=dst,
            send_sem=sem.at[0],
            recv_sem=sem.at[1],
            device_id=(w, peer),
            device_id_type=MESH,
        )

    half = p_ref.shape[2] // 2
    cols = (pl.ds(0, half), pl.ds(half, half))
    peers = (right, left)
    froms = (left, right)
    offsets = ((3, 2, 1), (1, 2, 3))

    def plane(h, rb, sb, sem):
        sends = []
        for d in (0, 1):
            src = p_ref.at[h * 4 + (xi + offsets[d][0]) % 4, :, cols[d]]
            c = remote(src, rb.at[d, 0], sem.at[d, 0], peers[d])
            c.start()
            sends.append(c)
        for step in (1, 2):
            for d in (0, 1):
                remote(sb.at[d, step - 1], rb.at[d, step - 1], sem.at[d, step - 1], froms[d]).wait_recv()
                term = p_ref.at[h * 4 + (xi + offsets[d][step]) % 4, :, cols[d]]
                _add_into(sb.at[d, step - 1], rb.at[d, step - 1], term)
                c = remote(sb.at[d, step - 1], rb.at[d, step], sem.at[d, step], peers[d])
                c.start()
                sends.append(c)
        for d in (0, 1):
            remote(sb.at[d, 1], rb.at[d, 2], sem.at[d, 2], froms[d]).wait_recv()
        return sends

    sends = plane(other, rp, sp, sem_p)
    for d in (0, 1):
        _add_into(qy.at[:, cols[d]], rp.at[d, 2], p_ref.at[other * 4 + xi, :, cols[d]])
    c = remote(qy, ry, sem_y, partner)
    c.start()
    sends.append(c)
    sends += plane(yh, rm, sm, sem_m)
    remote(qy, ry, sem_y, partner).wait_recv()
    own_p = p_ref.at[yh * 4 + xi]
    cap = o_ref.shape[1]
    for b in range(nw):
        rows = pl.ds(b * cap, cap)
        for d in (0, 1):
            total = rm[d, 2, rows, :].astype(jnp.float32) + own_p[rows, cols[d]].astype(jnp.float32)
            o_ref[b, :, cols[d]] = (total + ry[rows, cols[d]].astype(jnp.float32)).astype(o_ref.dtype)
    own = pltpu.make_async_copy(o_ref.at[w], r_ref.at[w], own_w)
    own.start()

    def wide_copy(k, peer, origin):
        return pltpu.make_async_remote_copy(
            src_ref=o_ref.at[peer],
            dst_ref=r_ref.at[origin],
            send_sem=sem_w.at[k, 0],
            recv_sem=sem_w.at[k, 1],
            device_id=(peer, me),
            device_id_type=MESH,
        )

    def send_body(k, carry):
        wide_copy(k, (w + k) % nw, w).start()
        return carry

    lax.fori_loop(1, nw, send_body, 0)

    def recv_body(k, carry):
        src = (w + nw - k) % nw
        wide_copy(k, src, src).wait_recv()
        return carry

    lax.fori_loop(1, nw, recv_body, 0)

    def sent_body(k, carry):
        wide_copy(k, (w + k) % nw, w).wait_send()
        return carry

    lax.fori_loop(1, nw, sent_body, 0)
    own.wait()
    for c in sends:
        c.wait_send()


def _reduce(p, nw, collective_id):
    one = p.shape[1:]
    blocks = (nw, one[0] // nw, one[1])
    block = pltpu.VMEM(one, p.dtype)
    return pl.pallas_call(
        _reduce_kernel,
        out_shape=jax.ShapeDtypeStruct(blocks, p.dtype),
        in_specs=[pl.BlockSpec(memory_space=pltpu.VMEM)],
        out_specs=pl.BlockSpec(memory_space=pl.ANY),
        scratch_shapes=[
            pltpu.VMEM((2, 3, one[0], one[1] // 2), p.dtype),
            pltpu.VMEM((2, 3, one[0], one[1] // 2), p.dtype),
            pltpu.VMEM((2, 2, one[0], one[1] // 2), p.dtype),
            pltpu.VMEM((2, 2, one[0], one[1] // 2), p.dtype),
            block,
            block,
            pltpu.VMEM(blocks, p.dtype),
            pltpu.SemaphoreType.DMA((2, 3, 2)),
            pltpu.SemaphoreType.DMA((2, 3, 2)),
            pltpu.SemaphoreType.DMA((2,)),
            pltpu.SemaphoreType.DMA((nw, 2)),
            pltpu.SemaphoreType.DMA(()),
        ],
        compiler_params=pltpu.CompilerParams(collective_id=collective_id, has_side_effects=True),
        cost_estimate=pl.CostEstimate(
            flops=2 * p.size, bytes_accessed=2 * p.size * p.dtype.itemsize, transcendentals=0
        ),
    )(p)


def _exchange(x, n_peers, gather, collective_id, axis="narrow"):
    if gather:
        out_shape = (n_peers,) + x.shape
        pick_src = lambda ref, i: ref
    else:
        out_shape = x.shape
        pick_src = lambda ref, i: ref.at[i]
    nbytes = x.size * x.dtype.itemsize
    return pl.pallas_call(
        lambda *refs: _exchange_kernel(n_peers, pick_src, axis, *refs),
        out_shape=jax.ShapeDtypeStruct(out_shape, x.dtype),
        in_specs=[pl.BlockSpec(memory_space=pl.ANY)],
        out_specs=pl.BlockSpec(memory_space=pl.ANY),
        scratch_shapes=[
            pltpu.SemaphoreType.DMA((n_peers - 1,)),
            pltpu.SemaphoreType.DMA((n_peers - 1,)),
            pltpu.SemaphoreType.DMA(()),
        ],
        compiler_params=pltpu.CompilerParams(collective_id=collective_id, has_side_effects=True),
        cost_estimate=pl.CostEstimate(flops=0, bytes_accessed=2 * nbytes, transcendentals=0),
    )(x)


def local(tokens, expert_ids, route_weights, w_gate, w_up, w_down):
    tok_rows = expert_ids.shape[0]
    top_count = expert_ids.shape[1]
    local_experts = w_gate.shape[0]
    groups_wide = lax.axis_size("wide")
    experts_all = local_experts * groups_wide
    capacity = 7 * tok_rows * top_count // (6 * experts_all)
    slots_all = experts_all * capacity
    flat_ids = expert_ids.reshape(-1)
    onehot = (flat_ids[:, None] == jnp.arange(experts_all, dtype=jnp.int32)[None, :]).astype(
        jnp.int32
    )
    pairs = flat_ids.shape[0]
    order = jnp.arange(pairs, dtype=jnp.int32)
    lower = (order[:, None] >= order[None, :]).astype(jnp.bfloat16)
    running = jnp.dot(lower, onehot.astype(jnp.bfloat16), preferred_element_type=jnp.float32)
    slot_index = jnp.sum(running * onehot, axis=1).astype(jnp.int32) - 1
    destination = (flat_ids * capacity + slot_index).reshape(tok_rows, top_count)
    hit = destination[:, :, None] == jnp.arange(slots_all, dtype=jnp.int32)[None, None, :]
    dispatch = jnp.any(hit, axis=1).astype(jnp.bfloat16)
    combine = jnp.sum(
        jnp.where(hit, route_weights.astype(jnp.float32)[:, :, None], 0.0), axis=1
    ).astype(jnp.bfloat16)
    dispatch = dispatch.reshape(tok_rows, groups_wide, capacity)
    combine = combine.reshape(tok_rows, groups_wide, capacity)
    outgoing = jnp.einsum(
        "tbc,td->bcd", dispatch, tokens, preferred_element_type=jnp.float32
    ).astype(jnp.bfloat16)
    n_narrow = lax.axis_size("narrow")
    width = tokens.shape[1]
    slot_rows = _dispatch(outgoing, n_narrow, 0)
    wg = w_gate[0].reshape(-1, n_narrow, width)
    wu = w_up[0].reshape(-1, n_narrow, width)
    wd = w_down[0].reshape(-1, n_narrow, width)
    gate_proj = jnp.einsum("nbcd,fnd->bcf", slot_rows, wg, preferred_element_type=jnp.float32)
    up_proj = jnp.einsum("nbcd,fnd->bcf", slot_rows, wu, preferred_element_type=jnp.float32)
    hidden = (jax.nn.silu(gate_proj) * up_proj).astype(jnp.bfloat16)
    partial_value = jnp.einsum(
        "sf,fnd->nsd", hidden.reshape(slots_all, -1), wd, preferred_element_type=jnp.float32
    ).astype(jnp.bfloat16)
    returned = _reduce(partial_value, groups_wide, 1)
    mixed = jnp.einsum("tbc,bcd->td", combine, returned, preferred_element_type=jnp.float32)
    return mixed.astype(jnp.bfloat16)


def solution(mesh):
    in_specs = (
        P("wide", "narrow"),
        P("wide", None),
        P("wide", None),
        P("wide", "narrow", None),
        P("wide", "narrow", None),
        P("wide", "narrow", None),
    )
    out_specs = P("wide", "narrow")
    return jax.shard_map(local, mesh=mesh, in_specs=in_specs, out_specs=out_specs, check_vma=False)
```

```python
import types

import jax
import jax.numpy as jnp
from jax import lax
from jax.experimental import pallas as pl
from jax.experimental.pallas import tpu as pltpu
from jax.sharding import PartitionSpec as P

MESH = pl.DeviceIdType.MESH


def _exchange_kernel(n_peers, pick_src, axis, x_ref, y_ref, send_sem, recv_sem, own_sem):
    me = lax.axis_index(axis)
    other = lax.axis_index("wide" if axis == "narrow" else "narrow")
    if axis == "narrow":
        dev = lambda p: (other, p)
    else:
        dev = lambda p: (p, other)
    barrier = pltpu.get_barrier_semaphore()
    for k in range(1, n_peers):
        peer = lax.rem(me + k, n_peers)
        pl.semaphore_signal(barrier, inc=1, device_id=dev(peer), device_id_type=MESH)
    pl.semaphore_wait(barrier, n_peers - 1)
    own = pltpu.make_async_copy(pick_src(x_ref, me), y_ref.at[me], own_sem)
    own.start()
    copies = []
    for k in range(1, n_peers):
        peer = lax.rem(me + k, n_peers)
        c = pltpu.make_async_remote_copy(
            src_ref=pick_src(x_ref, peer),
            dst_ref=y_ref.at[me],
            send_sem=send_sem.at[k - 1],
            recv_sem=recv_sem.at[k - 1],
            device_id=dev(peer),
            device_id_type=MESH,
        )
        c.start()
        copies.append(c)
    for k in range(1, n_peers):
        src = lax.rem(me + n_peers - k, n_peers)
        pltpu.make_async_remote_copy(
            src_ref=pick_src(x_ref, src),
            dst_ref=y_ref.at[src],
            send_sem=send_sem.at[k - 1],
            recv_sem=recv_sem.at[k - 1],
            device_id=dev(src),
            device_id_type=MESH,
        ).wait_recv()
    for c in copies:
        c.wait_send()
    own.wait()


def _gather_chain(x_ref, slot_of, sem_y, sem_x1, sem_x2, own_sem, after_start=None):
    me = lax.axis_index("narrow")
    w = lax.axis_index("wide")
    yh = me // 4
    xi = me % 4
    partner = (1 - yh) * 4 + xi
    right = yh * 4 + (xi + 1) % 4
    left = yh * 4 + (xi + 3) % 4

    y_ref = types.SimpleNamespace(at=_Slots(slot_of))

    def remote(src, slot, sem, peer):
        return pltpu.make_async_remote_copy(
            src_ref=src,
            dst_ref=y_ref.at[slot],
            send_sem=sem[0],
            recv_sem=sem[1],
            device_id=(w, peer),
            device_id_type=MESH,
        )

    own = pltpu.make_async_copy(x_ref, y_ref.at[me], own_sem)
    own.start()
    cy = remote(x_ref, me, (sem_y.at[0], sem_y.at[1]), partner)
    cy.start()
    c1 = [
        remote(x_ref, me, (sem_x1.at[0, 0], sem_x1.at[0, 1]), right),
        remote(x_ref, me, (sem_x1.at[1, 0], sem_x1.at[1, 1]), left),
    ]
    for c in c1:
        c.start()
    if after_start is not None:
        after_start()
    remote(x_ref, partner, (sem_y.at[0], sem_y.at[1]), partner).wait_recv()
    c2 = [
        remote(y_ref.at[partner], partner, (sem_x1.at[2, 0], sem_x1.at[2, 1]), right),
        remote(y_ref.at[partner], partner, (sem_x1.at[3, 0], sem_x1.at[3, 1]), left),
    ]
    for c in c2:
        c.start()
    lp = (1 - yh) * 4 + (xi + 3) % 4
    rp = (1 - yh) * 4 + (xi + 1) % 4
    remote(x_ref, left, (sem_x1.at[0, 0], sem_x1.at[0, 1]), left).wait_recv()
    remote(x_ref, right, (sem_x1.at[1, 0], sem_x1.at[1, 1]), right).wait_recv()
    c3 = [
        remote(y_ref.at[left], left, (sem_x2.at[0, 0], sem_x2.at[0, 1]), right),
    ]
    c3[0].start()
    remote(x_ref, rp, (sem_x1.at[3, 0], sem_x1.at[3, 1]), right).wait_recv()
    c4 = remote(y_ref.at[rp], rp, (sem_x2.at[1, 0], sem_x2.at[1, 1]), left)
    c4.start()
    remote(x_ref, lp, (sem_x1.at[2, 0], sem_x1.at[2, 1]), left).wait_recv()
    far = yh * 4 + (xi + 2) % 4
    far_p = (1 - yh) * 4 + (xi + 2) % 4
    remote(x_ref, far, (sem_x2.at[0, 0], sem_x2.at[0, 1]), left).wait_recv()
    remote(x_ref, far_p, (sem_x2.at[1, 0], sem_x2.at[1, 1]), right).wait_recv()
    return [cy] + c1 + c2 + c3 + [c4], own


class _Slots:
    def __init__(self, fn):
        self.fn = fn

    def __getitem__(self, k):
        return self.fn(k)


def _narrow_peers():
    me = lax.axis_index("narrow")
    yh = me // 4
    xi = me % 4
    return ((1 - yh) * 4 + xi, yh * 4 + (xi + 1) % 4, yh * 4 + (xi + 3) % 4)


def _dispatch_kernel(x_ref, y_ref, r_ref, sem_w, own_w, sem_y, sem_x1, sem_x2, own_g):
    nw, _, cols = x_ref.shape
    halves = 2
    cw = cols // halves
    me_w = lax.axis_index("wide")
    me = lax.axis_index("narrow")
    barrier = pltpu.get_barrier_semaphore()

    def greet(k, carry):
        pl.semaphore_signal(barrier, inc=1, device_id=((me_w + k) % nw, me), device_id_type=MESH)
        return carry

    lax.fori_loop(1, nw, greet, 0)
    for peer in _narrow_peers():
        pl.semaphore_signal(barrier, inc=1, device_id=(me_w, peer), device_id_type=MESH)
    pl.semaphore_wait(barrier, nw - 1 + 3)

    def wide_copy(h, k, peer_of_copy, target):
        cs = pl.ds(h * cw, cw)
        return pltpu.make_async_remote_copy(
            src_ref=x_ref.at[peer_of_copy, :, cs],
            dst_ref=r_ref.at[target, :, cs],
            send_sem=sem_w.at[h, k, 0],
            recv_sem=sem_w.at[h, k, 1],
            device_id=(peer_of_copy, me),
            device_id_type=MESH,
        )

    def wide_start(h):
        cs = pl.ds(h * cw, cw)
        own = pltpu.make_async_copy(x_ref.at[me_w, :, cs], r_ref.at[me_w, :, cs], own_w.at[h])
        own.start()

        def body(k, carry):
            wide_copy(h, k, (me_w + k) % nw, me_w).start()
            return carry

        lax.fori_loop(1, nw, body, 0)
        return own

    def wide_wait(h, own):
        def body(k, carry):
            src = (me_w + nw - k) % nw
            pltpu.make_async_remote_copy(
                src_ref=x_ref.at[src, :, pl.ds(h * cw, cw)],
                dst_ref=r_ref.at[src, :, pl.ds(h * cw, cw)],
                send_sem=sem_w.at[h, k, 0],
                recv_sem=sem_w.at[h, k, 1],
                device_id=(src, me),
                device_id_type=MESH,
            ).wait_recv()
            return carry

        lax.fori_loop(1, nw, body, 0)
        own.wait()

    def wide_sent(h):
        def body(k, carry):
            wide_copy(h, k, (me_w + k) % nw, me_w).wait_send()
            return carry

        lax.fori_loop(1, nw, body, 0)

    pending = []
    own0 = wide_start(0)
    wide_wait(0, own0)
    owns = []
    for h in range(halves):
        if h == 1:
            wide_wait(1, owns[0])
        cs = pl.ds(h * cw, cw)
        sends, own = _gather_chain(
            r_ref.at[:, :, cs],
            lambda k, cs=cs: y_ref.at[k, :, :, cs],
            sem_y.at[h],
            sem_x1.at[h],
            sem_x2.at[h],
            own_g.at[h],
            (lambda: owns.append(wide_start(1))) if h == 0 else None,
        )
        pending.append((sends, own))
    for h in range(halves):
        wide_sent(h)
        sends, own = pending[h]
        for c in sends:
            c.wait_send()
        own.wait()


def _dispatch(x, n_narrow, collective_id):
    nw, rows, cols = x.shape
    return pl.pallas_call(
        _dispatch_kernel,
        out_shape=jax.ShapeDtypeStruct((n_narrow, nw, rows, cols), x.dtype),
        in_specs=[pl.BlockSpec(memory_space=pl.ANY)],
        out_specs=pl.BlockSpec(memory_space=pl.ANY),
        scratch_shapes=[
            pltpu.VMEM((nw, rows, cols), x.dtype),
            pltpu.SemaphoreType.DMA((2, nw, 2)),
            pltpu.SemaphoreType.DMA((2,)),
            pltpu.SemaphoreType.DMA((2, 2)),
            pltpu.SemaphoreType.DMA((2, 4, 2)),
            pltpu.SemaphoreType.DMA((2, 2, 2)),
            pltpu.SemaphoreType.DMA((2,)),
        ],
        compiler_params=pltpu.CompilerParams(collective_id=collective_id, has_side_effects=True),
        cost_estimate=pl.CostEstimate(
            flops=0, bytes_accessed=2 * (n_narrow + 1) * x.size * x.dtype.itemsize, transcendentals=0
        ),
    )(x)


def _add_into(dst, *srcs):
    rows_all = dst.shape[0]
    step = 128 if rows_all % 128 == 0 else rows_all

    def body(i, carry):
        rows = pl.ds(pl.multiple_of(i * step, step), step)
        total = srcs[0][rows].astype(jnp.float32)
        for src in srcs[1:]:
            total = total + src[rows].astype(jnp.float32)
        dst[rows] = total.astype(dst.dtype)
        return carry

    lax.fori_loop(0, rows_all // step, body, 0)


def _reduce_kernel(p_ref, r_ref, rp, rm, sp, sm, qy, ry, o_ref, sem_p, sem_m, sem_y, sem_w, own_w):
    me = lax.axis_index("narrow")
    w = lax.axis_index("wide")
    yh = me // 4
    xi = me % 4
    other = 1 - yh
    partner = other * 4 + xi
    right = yh * 4 + (xi + 1) % 4
    left = yh * 4 + (xi + 3) % 4
    nw = r_ref.shape[0]
    barrier = pltpu.get_barrier_semaphore()
    for peer in (partner, right, left):
        pl.semaphore_signal(barrier, inc=1, device_id=(w, peer), device_id_type=MESH)

    def greet(k, carry):
        pl.semaphore_signal(barrier, inc=1, device_id=((w + k) % nw, me), device_id_type=MESH)
        return carry

    lax.fori_loop(1, nw, greet, 0)
    pl.semaphore_wait(barrier, 3 + nw - 1)

    def remote(src, dst, sem, peer):
        return pltpu.make_async_remote_copy(
            src_ref=src,
            dst_ref=dst,
            send_sem=sem.at[0],
            recv_sem=sem.at[1],
            device_id=(w, peer),
            device_id_type=MESH,
        )

    half = p_ref.shape[2] // 2
    cols = (pl.ds(0, half), pl.ds(half, half))
    peers = (right, left)
    froms = (left, right)
    offsets = ((3, 2, 1), (1, 2, 3))

    def first(h, rb, sem):
        sends = []
        for d in (0, 1):
            src = p_ref.at[h * 4 + (xi + offsets[d][0]) % 4, :, cols[d]]
            c = remote(src, rb.at[d, 0], sem.at[d, 0], peers[d])
            c.start()
            sends.append(c)
        return sends

    def plane(h, rb, sb, sem):
        sends = []
        for step in (1, 2):
            for d in (0, 1):
                remote(sb.at[d, step - 1], rb.at[d, step - 1], sem.at[d, step - 1], froms[d]).wait_recv()
                term = p_ref.at[h * 4 + (xi + offsets[d][step]) % 4, :, cols[d]]
                _add_into(sb.at[d, step - 1], rb.at[d, step - 1], term)
                c = remote(sb.at[d, step - 1], rb.at[d, step], sem.at[d, step], peers[d])
                c.start()
                sends.append(c)
        for d in (0, 1):
            remote(sb.at[d, 1], rb.at[d, 2], sem.at[d, 2], froms[d]).wait_recv()
        return sends

    sends = first(other, rp, sem_p) + first(yh, rm, sem_m)
    sends += plane(other, rp, sp, sem_p)
    for d in (0, 1):
        _add_into(qy.at[:, cols[d]], rp.at[d, 2], p_ref.at[other * 4 + xi, :, cols[d]])
    c = remote(qy, ry, sem_y, partner)
    c.start()
    sends.append(c)
    sends += plane(yh, rm, sm, sem_m)
    remote(qy, ry, sem_y, partner).wait_recv()
    own_p = p_ref.at[yh * 4 + xi]
    cap = o_ref.shape[1]
    for b in range(nw):
        rows = pl.ds(b * cap, cap)
        for d in (0, 1):
            total = rm[d, 2, rows, :].astype(jnp.float32) + own_p[rows, cols[d]].astype(jnp.float32)
            o_ref[b, :, cols[d]] = (total + ry[rows, cols[d]].astype(jnp.float32)).astype(o_ref.dtype)
    own = pltpu.make_async_copy(o_ref.at[w], r_ref.at[w], own_w)
    own.start()

    def wide_copy(k, peer, origin):
        return pltpu.make_async_remote_copy(
            src_ref=o_ref.at[peer],
            dst_ref=r_ref.at[origin],
            send_sem=sem_w.at[k, 0],
            recv_sem=sem_w.at[k, 1],
            device_id=(peer, me),
            device_id_type=MESH,
        )

    def send_body(k, carry):
        wide_copy(k, (w + k) % nw, w).start()
        return carry

    lax.fori_loop(1, nw, send_body, 0)

    def recv_body(k, carry):
        src = (w + nw - k) % nw
        wide_copy(k, src, src).wait_recv()
        return carry

    lax.fori_loop(1, nw, recv_body, 0)

    def sent_body(k, carry):
        wide_copy(k, (w + k) % nw, w).wait_send()
        return carry

    lax.fori_loop(1, nw, sent_body, 0)
    own.wait()
    for c in sends:
        c.wait_send()


def _reduce(p, nw, collective_id):
    one = p.shape[1:]
    blocks = (nw, one[0] // nw, one[1])
    block = pltpu.VMEM(one, p.dtype)
    return pl.pallas_call(
        _reduce_kernel,
        out_shape=jax.ShapeDtypeStruct(blocks, p.dtype),
        in_specs=[pl.BlockSpec(memory_space=pltpu.VMEM)],
        out_specs=pl.BlockSpec(memory_space=pl.ANY),
        scratch_shapes=[
            pltpu.VMEM((2, 3, one[0], one[1] // 2), p.dtype),
            pltpu.VMEM((2, 3, one[0], one[1] // 2), p.dtype),
            pltpu.VMEM((2, 2, one[0], one[1] // 2), p.dtype),
            pltpu.VMEM((2, 2, one[0], one[1] // 2), p.dtype),
            block,
            block,
            pltpu.VMEM(blocks, p.dtype),
            pltpu.SemaphoreType.DMA((2, 3, 2)),
            pltpu.SemaphoreType.DMA((2, 3, 2)),
            pltpu.SemaphoreType.DMA((2,)),
            pltpu.SemaphoreType.DMA((nw, 2)),
            pltpu.SemaphoreType.DMA(()),
        ],
        compiler_params=pltpu.CompilerParams(collective_id=collective_id, has_side_effects=True),
        cost_estimate=pl.CostEstimate(
            flops=2 * p.size, bytes_accessed=2 * p.size * p.dtype.itemsize, transcendentals=0
        ),
    )(p)


def _exchange(x, n_peers, gather, collective_id, axis="narrow"):
    if gather:
        out_shape = (n_peers,) + x.shape
        pick_src = lambda ref, i: ref
    else:
        out_shape = x.shape
        pick_src = lambda ref, i: ref.at[i]
    nbytes = x.size * x.dtype.itemsize
    return pl.pallas_call(
        lambda *refs: _exchange_kernel(n_peers, pick_src, axis, *refs),
        out_shape=jax.ShapeDtypeStruct(out_shape, x.dtype),
        in_specs=[pl.BlockSpec(memory_space=pl.ANY)],
        out_specs=pl.BlockSpec(memory_space=pl.ANY),
        scratch_shapes=[
            pltpu.SemaphoreType.DMA((n_peers - 1,)),
            pltpu.SemaphoreType.DMA((n_peers - 1,)),
            pltpu.SemaphoreType.DMA(()),
        ],
        compiler_params=pltpu.CompilerParams(collective_id=collective_id, has_side_effects=True),
        cost_estimate=pl.CostEstimate(flops=0, bytes_accessed=2 * nbytes, transcendentals=0),
    )(x)


def local(tokens, expert_ids, route_weights, w_gate, w_up, w_down):
    tok_rows = expert_ids.shape[0]
    top_count = expert_ids.shape[1]
    local_experts = w_gate.shape[0]
    groups_wide = lax.axis_size("wide")
    experts_all = local_experts * groups_wide
    capacity = 7 * tok_rows * top_count // (6 * experts_all)
    slots_all = experts_all * capacity
    flat_ids = expert_ids.reshape(-1)
    onehot = (flat_ids[:, None] == jnp.arange(experts_all, dtype=jnp.int32)[None, :]).astype(
        jnp.int32
    )
    pairs = flat_ids.shape[0]
    order = jnp.arange(pairs, dtype=jnp.int32)
    lower = (order[:, None] >= order[None, :]).astype(jnp.bfloat16)
    running = jnp.dot(lower, onehot.astype(jnp.bfloat16), preferred_element_type=jnp.float32)
    slot_index = jnp.sum(running * onehot, axis=1).astype(jnp.int32) - 1
    destination = (flat_ids * capacity + slot_index).reshape(tok_rows, top_count)
    hit = destination[:, :, None] == jnp.arange(slots_all, dtype=jnp.int32)[None, None, :]
    dispatch = jnp.any(hit, axis=1).astype(jnp.bfloat16)
    combine = jnp.sum(
        jnp.where(hit, route_weights.astype(jnp.float32)[:, :, None], 0.0), axis=1
    ).astype(jnp.bfloat16)
    dispatch = dispatch.reshape(tok_rows, groups_wide, capacity)
    combine = combine.reshape(tok_rows, groups_wide, capacity)
    outgoing = jnp.einsum(
        "tbc,td->bcd", dispatch, tokens, preferred_element_type=jnp.float32
    ).astype(jnp.bfloat16)
    n_narrow = lax.axis_size("narrow")
    width = tokens.shape[1]
    slot_rows = _dispatch(outgoing, n_narrow, 0)
    wg = w_gate[0].reshape(-1, n_narrow, width)
    wu = w_up[0].reshape(-1, n_narrow, width)
    wd = w_down[0].reshape(-1, n_narrow, width)
    gate_proj = jnp.einsum("nbcd,fnd->bcf", slot_rows, wg, preferred_element_type=jnp.float32)
    up_proj = jnp.einsum("nbcd,fnd->bcf", slot_rows, wu, preferred_element_type=jnp.float32)
    hidden = (jax.nn.silu(gate_proj) * up_proj).astype(jnp.bfloat16)
    partial_value = jnp.einsum(
        "sf,fnd->nsd", hidden.reshape(slots_all, -1), wd, preferred_element_type=jnp.float32
    ).astype(jnp.bfloat16)
    returned = _reduce(partial_value, groups_wide, 1)
    mixed = jnp.einsum("tbc,bcd->td", combine, returned, preferred_element_type=jnp.float32)
    return mixed.astype(jnp.bfloat16)


def solution(mesh):
    in_specs = (
        P("wide", "narrow"),
        P("wide", None),
        P("wide", None),
        P("wide", "narrow", None),
        P("wide", "narrow", None),
        P("wide", "narrow", None),
    )
    out_specs = P("wide", "narrow")
    return jax.shard_map(local, mesh=mesh, in_specs=in_specs, out_specs=out_specs, check_vma=False)
```

```python
import types

import jax
import jax.numpy as jnp
from jax import lax
from jax.experimental import pallas as pl
from jax.experimental.pallas import tpu as pltpu
from jax.sharding import PartitionSpec as P

MESH = pl.DeviceIdType.MESH


def _exchange_kernel(n_peers, pick_src, axis, x_ref, y_ref, send_sem, recv_sem, own_sem):
    me = lax.axis_index(axis)
    other = lax.axis_index("wide" if axis == "narrow" else "narrow")
    if axis == "narrow":
        dev = lambda p: (other, p)
    else:
        dev = lambda p: (p, other)
    barrier = pltpu.get_barrier_semaphore()
    for k in range(1, n_peers):
        peer = lax.rem(me + k, n_peers)
        pl.semaphore_signal(barrier, inc=1, device_id=dev(peer), device_id_type=MESH)
    pl.semaphore_wait(barrier, n_peers - 1)
    own = pltpu.make_async_copy(pick_src(x_ref, me), y_ref.at[me], own_sem)
    own.start()
    copies = []
    for k in range(1, n_peers):
        peer = lax.rem(me + k, n_peers)
        c = pltpu.make_async_remote_copy(
            src_ref=pick_src(x_ref, peer),
            dst_ref=y_ref.at[me],
            send_sem=send_sem.at[k - 1],
            recv_sem=recv_sem.at[k - 1],
            device_id=dev(peer),
            device_id_type=MESH,
        )
        c.start()
        copies.append(c)
    for k in range(1, n_peers):
        src = lax.rem(me + n_peers - k, n_peers)
        pltpu.make_async_remote_copy(
            src_ref=pick_src(x_ref, src),
            dst_ref=y_ref.at[src],
            send_sem=send_sem.at[k - 1],
            recv_sem=recv_sem.at[k - 1],
            device_id=dev(src),
            device_id_type=MESH,
        ).wait_recv()
    for c in copies:
        c.wait_send()
    own.wait()


def _gather_chain(x_ref, slot_of, sem_y, sem_x1, sem_x2, own_sem, after_start=None):
    me = lax.axis_index("narrow")
    w = lax.axis_index("wide")
    yh = me // 4
    xi = me % 4
    partner = (1 - yh) * 4 + xi
    right = yh * 4 + (xi + 1) % 4
    left = yh * 4 + (xi + 3) % 4

    y_ref = types.SimpleNamespace(at=_Slots(slot_of))

    def remote(src, slot, sem, peer):
        return pltpu.make_async_remote_copy(
            src_ref=src,
            dst_ref=y_ref.at[slot],
            send_sem=sem[0],
            recv_sem=sem[1],
            device_id=(w, peer),
            device_id_type=MESH,
        )

    own = pltpu.make_async_copy(x_ref, y_ref.at[me], own_sem)
    own.start()
    cy = remote(x_ref, me, (sem_y.at[0], sem_y.at[1]), partner)
    cy.start()
    c1 = [
        remote(x_ref, me, (sem_x1.at[0, 0], sem_x1.at[0, 1]), right),
        remote(x_ref, me, (sem_x1.at[1, 0], sem_x1.at[1, 1]), left),
    ]
    for c in c1:
        c.start()
    if after_start is not None:
        after_start()
    remote(x_ref, partner, (sem_y.at[0], sem_y.at[1]), partner).wait_recv()
    c2 = [
        remote(y_ref.at[partner], partner, (sem_x1.at[2, 0], sem_x1.at[2, 1]), right),
        remote(y_ref.at[partner], partner, (sem_x1.at[3, 0], sem_x1.at[3, 1]), left),
    ]
    for c in c2:
        c.start()
    lp = (1 - yh) * 4 + (xi + 3) % 4
    rp = (1 - yh) * 4 + (xi + 1) % 4
    remote(x_ref, left, (sem_x1.at[0, 0], sem_x1.at[0, 1]), left).wait_recv()
    remote(x_ref, right, (sem_x1.at[1, 0], sem_x1.at[1, 1]), right).wait_recv()
    c3 = [
        remote(y_ref.at[left], left, (sem_x2.at[0, 0], sem_x2.at[0, 1]), right),
    ]
    c3[0].start()
    remote(x_ref, rp, (sem_x1.at[3, 0], sem_x1.at[3, 1]), right).wait_recv()
    c4 = remote(y_ref.at[rp], rp, (sem_x2.at[1, 0], sem_x2.at[1, 1]), left)
    c4.start()
    remote(x_ref, lp, (sem_x1.at[2, 0], sem_x1.at[2, 1]), left).wait_recv()
    far = yh * 4 + (xi + 2) % 4
    far_p = (1 - yh) * 4 + (xi + 2) % 4
    remote(x_ref, far, (sem_x2.at[0, 0], sem_x2.at[0, 1]), left).wait_recv()
    remote(x_ref, far_p, (sem_x2.at[1, 0], sem_x2.at[1, 1]), right).wait_recv()
    return [cy] + c1 + c2 + c3 + [c4], own


class _Slots:
    def __init__(self, fn):
        self.fn = fn

    def __getitem__(self, k):
        return self.fn(k)


def _narrow_peers():
    me = lax.axis_index("narrow")
    yh = me // 4
    xi = me % 4
    return ((1 - yh) * 4 + xi, yh * 4 + (xi + 1) % 4, yh * 4 + (xi + 3) % 4)


def _dispatch_kernel(x_ref, y_ref, r_ref, sem_w, own_w, sem_y, sem_x1, sem_x2, own_g):
    nw, _, cols = x_ref.shape
    halves = 2
    cw = cols // halves
    me_w = lax.axis_index("wide")
    me = lax.axis_index("narrow")
    barrier = pltpu.get_barrier_semaphore()

    def greet(k, carry):
        pl.semaphore_signal(barrier, inc=1, device_id=((me_w + k) % nw, me), device_id_type=MESH)
        return carry

    lax.fori_loop(1, nw, greet, 0)
    for peer in _narrow_peers():
        pl.semaphore_signal(barrier, inc=1, device_id=(me_w, peer), device_id_type=MESH)
    pl.semaphore_wait(barrier, nw - 1 + 3)

    def wide_copy(h, k, peer_of_copy, target):
        cs = pl.ds(h * cw, cw)
        return pltpu.make_async_remote_copy(
            src_ref=x_ref.at[peer_of_copy, :, cs],
            dst_ref=r_ref.at[target, :, cs],
            send_sem=sem_w.at[h, k, 0],
            recv_sem=sem_w.at[h, k, 1],
            device_id=(peer_of_copy, me),
            device_id_type=MESH,
        )

    def wide_start(h):
        cs = pl.ds(h * cw, cw)
        own = pltpu.make_async_copy(x_ref.at[me_w, :, cs], r_ref.at[me_w, :, cs], own_w.at[h])
        own.start()

        def body(k, carry):
            wide_copy(h, k, (me_w + k) % nw, me_w).start()
            return carry

        lax.fori_loop(1, nw, body, 0)
        return own

    def wide_wait(h, own):
        def body(k, carry):
            src = (me_w + nw - k) % nw
            pltpu.make_async_remote_copy(
                src_ref=x_ref.at[src, :, pl.ds(h * cw, cw)],
                dst_ref=r_ref.at[src, :, pl.ds(h * cw, cw)],
                send_sem=sem_w.at[h, k, 0],
                recv_sem=sem_w.at[h, k, 1],
                device_id=(src, me),
                device_id_type=MESH,
            ).wait_recv()
            return carry

        lax.fori_loop(1, nw, body, 0)
        own.wait()

    def wide_sent(h):
        def body(k, carry):
            wide_copy(h, k, (me_w + k) % nw, me_w).wait_send()
            return carry

        lax.fori_loop(1, nw, body, 0)

    pending = []
    own0 = wide_start(0)
    wide_wait(0, own0)
    owns = []
    for h in range(halves):
        if h == 1:
            wide_wait(1, owns[0])
        cs = pl.ds(h * cw, cw)
        sends, own = _gather_chain(
            r_ref.at[:, :, cs],
            lambda k, cs=cs: y_ref.at[k, :, :, cs],
            sem_y.at[h],
            sem_x1.at[h],
            sem_x2.at[h],
            own_g.at[h],
            (lambda: owns.append(wide_start(1))) if h == 0 else None,
        )
        pending.append((sends, own))
    for h in range(halves):
        wide_sent(h)
        sends, own = pending[h]
        for c in sends:
            c.wait_send()
        own.wait()


def _dispatch(x, n_narrow, collective_id):
    nw, rows, cols = x.shape
    return pl.pallas_call(
        _dispatch_kernel,
        out_shape=jax.ShapeDtypeStruct((n_narrow, nw, rows, cols), x.dtype),
        in_specs=[pl.BlockSpec(memory_space=pl.ANY)],
        out_specs=pl.BlockSpec(memory_space=pl.ANY),
        scratch_shapes=[
            pltpu.VMEM((nw, rows, cols), x.dtype),
            pltpu.SemaphoreType.DMA((2, nw, 2)),
            pltpu.SemaphoreType.DMA((2,)),
            pltpu.SemaphoreType.DMA((2, 2)),
            pltpu.SemaphoreType.DMA((2, 4, 2)),
            pltpu.SemaphoreType.DMA((2, 2, 2)),
            pltpu.SemaphoreType.DMA((2,)),
        ],
        compiler_params=pltpu.CompilerParams(collective_id=collective_id, has_side_effects=True),
        cost_estimate=pl.CostEstimate(
            flops=0, bytes_accessed=2 * (n_narrow + 1) * x.size * x.dtype.itemsize, transcendentals=0
        ),
    )(x)


def _add_into(dst, *srcs):
    rows_all = dst.shape[0]
    step = 128 if rows_all % 128 == 0 else rows_all

    def body(i, carry):
        rows = pl.ds(pl.multiple_of(i * step, step), step)
        total = srcs[0][rows].astype(jnp.float32)
        for src in srcs[1:]:
            total = total + src[rows].astype(jnp.float32)
        dst[rows] = total.astype(dst.dtype)
        return carry

    lax.fori_loop(0, rows_all // step, body, 0)


def _reduce_kernel(p_ref, r_ref, rp, rm, sp, sm, qy, ry, o_ref, sem_p, sem_m, sem_y, sem_w, own_w):
    me = lax.axis_index("narrow")
    w = lax.axis_index("wide")
    yh = me // 4
    xi = me % 4
    other = 1 - yh
    partner = other * 4 + xi
    right = yh * 4 + (xi + 1) % 4
    left = yh * 4 + (xi + 3) % 4
    nw = r_ref.shape[0]
    barrier = pltpu.get_barrier_semaphore()
    for peer in (partner, right, left):
        pl.semaphore_signal(barrier, inc=1, device_id=(w, peer), device_id_type=MESH)

    def greet(k, carry):
        pl.semaphore_signal(barrier, inc=1, device_id=((w + k) % nw, me), device_id_type=MESH)
        return carry

    lax.fori_loop(1, nw, greet, 0)
    pl.semaphore_wait(barrier, 3 + nw - 1)

    def remote(src, dst, sem, peer):
        return pltpu.make_async_remote_copy(
            src_ref=src,
            dst_ref=dst,
            send_sem=sem.at[0],
            recv_sem=sem.at[1],
            device_id=(w, peer),
            device_id_type=MESH,
        )

    half = p_ref.shape[2] // 2
    cols = (pl.ds(0, half), pl.ds(half, half))
    peers = (right, left)
    froms = (left, right)
    offsets = ((3, 2, 1), (1, 2, 3))

    def first(h, rb, sem):
        sends = []
        for d in (0, 1):
            src = p_ref.at[h * 4 + (xi + offsets[d][0]) % 4, :, cols[d]]
            c = remote(src, rb.at[d, 0], sem.at[d, 0], peers[d])
            c.start()
            sends.append(c)
        return sends

    def plane(h, rb, sb, sem):
        sends = []
        for step in (1, 2):
            for d in (0, 1):
                remote(sb.at[d, step - 1], rb.at[d, step - 1], sem.at[d, step - 1], froms[d]).wait_recv()
                term = p_ref.at[h * 4 + (xi + offsets[d][step]) % 4, :, cols[d]]
                _add_into(sb.at[d, step - 1], rb.at[d, step - 1], term)
                c = remote(sb.at[d, step - 1], rb.at[d, step], sem.at[d, step], peers[d])
                c.start()
                sends.append(c)
        for d in (0, 1):
            remote(sb.at[d, 1], rb.at[d, 2], sem.at[d, 2], froms[d]).wait_recv()
        return sends

    sends = first(other, rp, sem_p) + first(yh, rm, sem_m)
    sends += plane(other, rp, sp, sem_p)
    for d in (0, 1):
        _add_into(qy.at[:, cols[d]], rp.at[d, 2], p_ref.at[other * 4 + xi, :, cols[d]])
    c = remote(qy, ry, sem_y, partner)
    c.start()
    sends.append(c)
    sends += plane(yh, rm, sm, sem_m)
    remote(qy, ry, sem_y, partner).wait_recv()
    own_p = p_ref.at[yh * 4 + xi]
    cap = o_ref.shape[1]

    def wide_copy(k, peer, origin):
        return pltpu.make_async_remote_copy(
            src_ref=o_ref.at[peer],
            dst_ref=r_ref.at[origin],
            send_sem=sem_w.at[k, 0],
            recv_sem=sem_w.at[k, 1],
            device_id=(peer, me),
            device_id_type=MESH,
        )

    for b in range(nw):
        rows = pl.ds(b * cap, cap)
        for d in (0, 1):
            total = rm[d, 2, rows, :].astype(jnp.float32) + own_p[rows, cols[d]].astype(jnp.float32)
            o_ref[b, :, cols[d]] = (total + ry[rows, cols[d]].astype(jnp.float32)).astype(o_ref.dtype)

        @pl.when(w != b)
        def _(b=b):
            wide_copy((b + nw - w) % nw, b, w).start()

    own = pltpu.make_async_copy(o_ref.at[w], r_ref.at[w], own_w)
    own.start()

    def recv_body(k, carry):
        src = (w + nw - k) % nw
        wide_copy(k, src, src).wait_recv()
        return carry

    lax.fori_loop(1, nw, recv_body, 0)

    def sent_body(k, carry):
        wide_copy(k, (w + k) % nw, w).wait_send()
        return carry

    lax.fori_loop(1, nw, sent_body, 0)
    own.wait()
    for c in sends:
        c.wait_send()


def _reduce(p, nw, collective_id):
    one = p.shape[1:]
    blocks = (nw, one[0] // nw, one[1])
    block = pltpu.VMEM(one, p.dtype)
    return pl.pallas_call(
        _reduce_kernel,
        out_shape=jax.ShapeDtypeStruct(blocks, p.dtype),
        in_specs=[pl.BlockSpec(memory_space=pltpu.VMEM)],
        out_specs=pl.BlockSpec(memory_space=pl.ANY),
        scratch_shapes=[
            pltpu.VMEM((2, 3, one[0], one[1] // 2), p.dtype),
            pltpu.VMEM((2, 3, one[0], one[1] // 2), p.dtype),
            pltpu.VMEM((2, 2, one[0], one[1] // 2), p.dtype),
            pltpu.VMEM((2, 2, one[0], one[1] // 2), p.dtype),
            block,
            block,
            pltpu.VMEM(blocks, p.dtype),
            pltpu.SemaphoreType.DMA((2, 3, 2)),
            pltpu.SemaphoreType.DMA((2, 3, 2)),
            pltpu.SemaphoreType.DMA((2,)),
            pltpu.SemaphoreType.DMA((nw, 2)),
            pltpu.SemaphoreType.DMA(()),
        ],
        compiler_params=pltpu.CompilerParams(collective_id=collective_id, has_side_effects=True),
        cost_estimate=pl.CostEstimate(
            flops=2 * p.size, bytes_accessed=2 * p.size * p.dtype.itemsize, transcendentals=0
        ),
    )(p)


def _exchange(x, n_peers, gather, collective_id, axis="narrow"):
    if gather:
        out_shape = (n_peers,) + x.shape
        pick_src = lambda ref, i: ref
    else:
        out_shape = x.shape
        pick_src = lambda ref, i: ref.at[i]
    nbytes = x.size * x.dtype.itemsize
    return pl.pallas_call(
        lambda *refs: _exchange_kernel(n_peers, pick_src, axis, *refs),
        out_shape=jax.ShapeDtypeStruct(out_shape, x.dtype),
        in_specs=[pl.BlockSpec(memory_space=pl.ANY)],
        out_specs=pl.BlockSpec(memory_space=pl.ANY),
        scratch_shapes=[
            pltpu.SemaphoreType.DMA((n_peers - 1,)),
            pltpu.SemaphoreType.DMA((n_peers - 1,)),
            pltpu.SemaphoreType.DMA(()),
        ],
        compiler_params=pltpu.CompilerParams(collective_id=collective_id, has_side_effects=True),
        cost_estimate=pl.CostEstimate(flops=0, bytes_accessed=2 * nbytes, transcendentals=0),
    )(x)


def local(tokens, expert_ids, route_weights, w_gate, w_up, w_down):
    tok_rows = expert_ids.shape[0]
    top_count = expert_ids.shape[1]
    local_experts = w_gate.shape[0]
    groups_wide = lax.axis_size("wide")
    experts_all = local_experts * groups_wide
    capacity = 7 * tok_rows * top_count // (6 * experts_all)
    slots_all = experts_all * capacity
    flat_ids = expert_ids.reshape(-1)
    onehot = (flat_ids[:, None] == jnp.arange(experts_all, dtype=jnp.int32)[None, :]).astype(
        jnp.int32
    )
    pairs = flat_ids.shape[0]
    order = jnp.arange(pairs, dtype=jnp.int32)
    lower = (order[:, None] >= order[None, :]).astype(jnp.bfloat16)
    running = jnp.dot(lower, onehot.astype(jnp.bfloat16), preferred_element_type=jnp.float32)
    slot_index = jnp.sum(running * onehot, axis=1).astype(jnp.int32) - 1
    destination = (flat_ids * capacity + slot_index).reshape(tok_rows, top_count)
    hit = destination[:, :, None] == jnp.arange(slots_all, dtype=jnp.int32)[None, None, :]
    dispatch = jnp.any(hit, axis=1).astype(jnp.bfloat16)
    combine = jnp.sum(
        jnp.where(hit, route_weights.astype(jnp.float32)[:, :, None], 0.0), axis=1
    ).astype(jnp.bfloat16)
    dispatch = dispatch.reshape(tok_rows, groups_wide, capacity)
    combine = combine.reshape(tok_rows, groups_wide, capacity)
    outgoing = jnp.einsum(
        "tbc,td->bcd", dispatch, tokens, preferred_element_type=jnp.float32
    ).astype(jnp.bfloat16)
    n_narrow = lax.axis_size("narrow")
    width = tokens.shape[1]
    slot_rows = _dispatch(outgoing, n_narrow, 0)
    wg = w_gate[0].reshape(-1, n_narrow, width)
    wu = w_up[0].reshape(-1, n_narrow, width)
    wd = w_down[0].reshape(-1, n_narrow, width)
    gate_proj = jnp.einsum("nbcd,fnd->bcf", slot_rows, wg, preferred_element_type=jnp.float32)
    up_proj = jnp.einsum("nbcd,fnd->bcf", slot_rows, wu, preferred_element_type=jnp.float32)
    hidden = (jax.nn.silu(gate_proj) * up_proj).astype(jnp.bfloat16)
    partial_value = jnp.einsum(
        "sf,fnd->nsd", hidden.reshape(slots_all, -1), wd, preferred_element_type=jnp.float32
    ).astype(jnp.bfloat16)
    returned = _reduce(partial_value, groups_wide, 1)
    mixed = jnp.einsum("tbc,bcd->td", combine, returned, preferred_element_type=jnp.float32)
    return mixed.astype(jnp.bfloat16)


def solution(mesh):
    in_specs = (
        P("wide", "narrow"),
        P("wide", None),
        P("wide", None),
        P("wide", "narrow", None),
        P("wide", "narrow", None),
        P("wide", "narrow", None),
    )
    out_specs = P("wide", "narrow")
    return jax.shard_map(local, mesh=mesh, in_specs=in_specs, out_specs=out_specs, check_vma=False)
```
